32 devices in a mesh: dp: 4 (over y, x), ctx: 2 (over core), tp: 4 (over z).
Axes of the slice: x: 2, y: 2, z: 4, core: 2. Of those that a mesh axis runs over, the one named last changes fastest.
Arguments:
- block_input_activations: bfloat16 [8192, 1024], P(('dp', 'ctx')), may hold values from -6 to 6
- sequence_first_token: int32 [8192], P(('dp', 'ctx')), may hold values from 0 to 1, as said below
- norm_gain: float32 [1024], replicated, may hold values from 0.5 to 1.5
- gate_proj: bfloat16 [1024, 2048], P(('dp', 'ctx'), 'tp'), may hold values from -0.1875 to 0.1875
- input_proj: bfloat16 [1024, 2048], P(('dp', 'ctx'), 'tp'), may hold values from -0.1875 to 0.1875
- step_proj: bfloat16 [1024, 32], P(('dp', 'ctx'), 'tp'), may hold values from -0.1875 to 0.1875
- state_proj: bfloat16 [1024, 256], P(('dp', 'ctx')), may hold values from -0.1875 to 0.1875
- conv_inner_weight: float32 [4, 2048], P(None, 'tp'), may hold values from -3 to 3
- conv_inner_bias: float32 [2048], P('tp'), may hold values from -0.5 to 0.5
- conv_state_weight: float32 [4, 256], replicated, may hold values from -3 to 3
- conv_state_bias: float32 [256], replicated, may hold values from -0.5 to 0.5
- step_bias: float32 [32], P('tp'), may hold values from -6 to -2
- decay_log: float32 [32], P('tp'), may hold values from 0 to 2.5
- skip_weight: float32 [32], P('tp'), may hold values from 0.5 to 1.5
- gate_gain: float32 [2048], P('tp'), may hold values from 0.5 to 1.5
- out_proj: bfloat16 [2048, 1024], P('tp', ('dp', 'ctx')), may hold values from -0.125 to 0.125
- output_cotangent: bfloat16 [8192, 1024], P(('dp', 'ctx')), may hold values from -6 to 6
Outputs:
- block_output: bfloat16 [8192, 1024], P(('dp', 'ctx'), 'tp')
- input_grad: float32 [8192, 1024], P(('dp', 'ctx'), 'tp')
- norm_gain_grad: float32 [1024], P('tp')
- gate_proj_grad: float32 [1024, 2048], P(('dp', 'ctx'), 'tp')
- input_proj_grad: float32 [1024, 2048], P(('dp', 'ctx'), 'tp')
- step_proj_grad: float32 [1024, 32], P(('dp', 'ctx'), 'tp')
- state_proj_grad: float32 [1024, 256], P(('dp', 'ctx'))
- conv_inner_weight_grad: float32 [4, 2048], P(None, 'tp')
- conv_inner_bias_grad: float32 [2048], P('tp')
- conv_state_weight_grad: float32 [4, 256], replicated
- conv_state_bias_grad: float32 [256], replicated
- step_bias_grad: float32 [32], P('tp')
- decay_log_grad: float32 [32], P('tp')
- skip_weight_grad: float32 [32], P('tp')
- gate_gain_grad: float32 [2048], P('tp')
- out_proj_grad: float32 [2048, 1024], P('tp', ('dp', 'ctx'))
The draws below stay inside these ranges and needn't reach their ends.
Inputs may be any that keep to these rules, and one draw needn't show every extreme that they name: `sequence_first_token`: every packed row of 2048 tokens begins with a 1; every sequence has 1 to 1536 positions, and each row holds one of exactly 1536.
All inputs are finite; a program needn't handle non-finite values.
Results may differ from the reference program's by a relative error of at most 0.012.
Values may be sent and summed in bfloat16 or wider, within the bound.
A program may use at most 128 MiB of HBM per device.

```python
import jax
import jax.numpy as jnp
from jax import lax

MODEL_WIDTH = 1024
HEADS = 32
HEADDIM = 64
STATE = 128
KCONV = 4
SPAN = 256
INNER = 2048
ROW_POSITIONS = 2048
LONGEST_SEQUENCE = 1536
PACKED_ROWS = 4
TOKENS = 8192


def draw_sequence_first_token(key, part):
    offset_random_key = jax.random.fold_in(key, 11)
    random_key_base = jax.random.fold_in(key, 23)
    start_shifts = jax.random.randint(offset_random_key, (PACKED_ROWS,), 1, ROW_POSITIONS - LONGEST_SEQUENCE + 1)
    token_position = jnp.arange(ROW_POSITIONS)
    relative = token_position[None, :] - start_shifts[:, None]
    long_start = relative == 0
    long_end = relative == LONGEST_SEQUENCE
    inside = (relative > 0) & (relative < LONGEST_SEQUENCE)
    sampled_starts = jax.random.randint(random_key_base, (PACKED_ROWS, ROW_POSITIONS), 0, 48) == 0
    sequence_starts = long_start | long_end | sampled_starts & jnp.logical_not(inside) | (token_position[None, :] == 0)
    return sequence_starts.astype(jnp.int32).reshape(PACKED_ROWS * ROW_POSITIONS)


def block_levels(own_key, dims, shards, least, top_value):
    level = 1.0
    for axis_at, blocks in shards:
        steps = jax.random.uniform(jax.random.fold_in(jax.random.fold_in(own_key, 6), axis_at), (blocks,), jnp.float32, least / len(shards), top_value / len(shards))
        level = level * jnp.repeat(jnp.exp(steps), dims[axis_at] // blocks).reshape((-1,) + (1,) * (len(dims) - 1 - axis_at))
    return level


def normal_values(rng, shape, scale, bound, cuts=(), kind=jnp.bfloat16):
    drawn = scale * jax.random.normal(rng, shape, jnp.float32)
    if cuts:
        drawn = drawn * block_levels(rng, shape, cuts, -0.22, 0.18)
    return jnp.clip(drawn, -bound, bound).astype(kind)


def setup_inputs(seed: int = 0) -> dict:
    splits = jax.random.split(jax.random.key(seed), 18)
    return {
        "block_input_activations": normal_values(splits[0], (TOKENS, MODEL_WIDTH), 1.0, 6.0, ((0, 8),)),
        "sequence_first_token": draw_sequence_first_token(jax.random.fold_in(splits[17], 71), 0),
        "norm_gain": jnp.clip(1.0 + 0.1 * jax.random.normal(splits[2], (MODEL_WIDTH,), jnp.float32), 0.5, 1.5),
        "gate_proj": normal_values(splits[3], (MODEL_WIDTH, INNER), MODEL_WIDTH ** -0.5, 0.1875, ((0, 8), (1, 4))),
        "input_proj": normal_values(splits[4], (MODEL_WIDTH, INNER), MODEL_WIDTH ** -0.5, 0.1875, ((0, 8), (1, 4))),
        "step_proj": normal_values(splits[5], (MODEL_WIDTH, HEADS), MODEL_WIDTH ** -0.5, 0.1875, ((0, 8), (1, 4))),
        "state_proj": normal_values(splits[6], (MODEL_WIDTH, 2 * STATE), MODEL_WIDTH ** -0.5, 0.1875, ((0, 8),)),
        "conv_inner_weight": normal_values(splits[7], (KCONV, INNER), KCONV ** -0.5, 3.0, ((1, 4),), jnp.float32),
        "conv_inner_bias": jnp.clip(jax.random.uniform(splits[8], (INNER,), jnp.float32, -0.5, 0.5) * block_levels(splits[8], (INNER,), ((0, 4),), -0.4, 0.0), -0.5, 0.5),
        "conv_state_weight": normal_values(splits[9], (KCONV, 2 * STATE), KCONV ** -0.5, 3.0, (), jnp.float32),
        "conv_state_bias": jnp.clip(jax.random.uniform(splits[10], (2 * STATE,), jnp.float32, -0.5, 0.5), -0.5, 0.5),
        "step_bias": jnp.clip(-6.0 + 4.0 * jax.random.uniform(splits[11], (HEADS,), jnp.float32) ** block_levels(splits[11], (HEADS,), ((0, 4),), -0.2, 0.2), -6.0, -2.0),
        "decay_log": jnp.clip(2.5 * jax.random.uniform(splits[12], (HEADS,), jnp.float32) ** block_levels(splits[12], (HEADS,), ((0, 4),), -0.2, 0.2), 0.0, 2.5),
        "skip_weight": jnp.clip(0.5 + 1.0 * jax.random.uniform(splits[13], (HEADS,), jnp.float32) ** block_levels(splits[13], (HEADS,), ((0, 4),), -0.2, 0.2), 0.5, 1.5),
        "gate_gain": jnp.clip(1.0 + 0.1 * jax.random.normal(splits[14], (INNER,), jnp.float32), 0.5, 1.5),
        "out_proj": normal_values(splits[15], (INNER, MODEL_WIDTH), INNER ** -0.5, 0.125, ((0, 4), (1, 8))),
        "output_cotangent": normal_values(splits[16], (TOKENS, MODEL_WIDTH), 1.0, 6.0, ((0, 8),)),
    }


EPSILON = 1e-05
HIGHEST = lax.Precision.HIGHEST

def conv_apply(padded, flags_padded, conv_weight, conv_bias):
    width = KCONV - 1
    count = padded.shape[0] - width
    segments = jnp.cumsum(flags_padded)
    own = segments[width:]
    result = jnp.zeros((count, padded.shape[1]), jnp.float32) + conv_bias[None, :]
    for lag in range(KCONV):
        valid = (segments[width - lag:width - lag + count] == own).astype(jnp.float32)
        result = result + conv_weight[lag][None, :] * padded[width - lag:width - lag + count] * valid[:, None]
    return result

def span_parts(inner_values, step_size, state_in, state_out, sequence_starts, decay_rate):
    count = inner_values.shape[0]
    heads = step_size.shape[1]
    spans = count // SPAN
    log_decay = (step_size * decay_rate[None, :]).reshape(spans, SPAN, heads)
    cumulative = jnp.cumsum(log_decay, axis=1)
    segments = jnp.cumsum(sequence_starts.reshape(spans, SPAN), axis=1)
    block_values = inner_values.reshape(spans, SPAN, heads, HEADDIM)
    block_step = step_size.reshape(spans, SPAN, heads)
    block_in = state_in.reshape(spans, SPAN, STATE)
    block_out = state_out.reshape(spans, SPAN, STATE)
    order = jnp.arange(SPAN)
    lower = order[:, None] >= order[None, :]
    same = ((segments[:, :, None] == segments[:, None, :]) & lower[None])[..., None]
    spread = cumulative[:, :, None, :] - cumulative[:, None, :, :]
    decay = jnp.where(same, jnp.exp(jnp.where(same, spread, 0.0)), 0.0)
    scores = jnp.einsum('ktn,ksn->kts', block_out, block_in, precision=HIGHEST)
    mixing = decay * scores[..., None] * block_step[:, None, :, :]
    inner_mixed = jnp.einsum('ktsh,kshp->kthp', mixing, block_values, precision=HIGHEST)
    ending = (segments == segments[:, -1:])[..., None]
    to_end = jnp.where(ending, jnp.exp(cumulative[:, -1:, :] - cumulative), 0.0) * block_step
    states = jnp.einsum('kshp,ksn->khpn', block_values * to_end[..., None], block_in, precision=HIGHEST)
    passing = jnp.where((segments == 0)[..., None], jnp.exp(cumulative), 0.0)
    return (inner_mixed, states, passing)

def fold_spans(states, passing):
    ends = passing[:, -1, :]

    def advance(carry, item):
        zero_state, product = carry
        state, end = item
        return ((end[:, None, None] * zero_state + state, end * product), (zero_state, product))
    init = (jnp.zeros(states.shape[1:], jnp.float32), jnp.ones(ends.shape[1:], jnp.float32))
    (final_state, final_product), (span_states, span_decays) = lax.scan(advance, init, (states, ends))
    return (span_states, span_decays, final_state, final_product)

def mixer_front(padded, flags_padded, sequence_starts, step_raw, conv_weight, conv_bias, step_bias, decay_log):
    inner_width = padded.shape[1] - 2 * STATE
    activated = jax.nn.silu(conv_apply(padded, flags_padded, conv_weight, conv_bias))
    inner_values = activated[:, :inner_width]
    state_in = activated[:, inner_width:inner_width + STATE]
    state_out = activated[:, inner_width + STATE:]
    step_size = jax.nn.softplus(step_raw + step_bias[None, :])
    decay_rate = -jnp.exp(decay_log)
    inner_mixed, states, passing = span_parts(inner_values, step_size, state_in, state_out, sequence_starts, decay_rate)
    span_states, span_decays, final_state, final_product = fold_spans(states, passing)
    kept = (inner_values, state_out, inner_mixed, passing, span_states, span_decays)
    return (kept, final_state, final_product)

def finish(kept, carried, skip):
    inner_values, state_out, inner_mixed, passing, span_states, span_decays = kept
    spans = inner_mixed.shape[0]
    heads = inner_mixed.shape[2]
    initial = span_states + span_decays[:, :, None, None] * carried[None]
    block_out = state_out.reshape(spans, SPAN, STATE)
    from_state = jnp.einsum('ktn,khpn->kthp', block_out, initial, precision=HIGHEST)
    block_values = inner_values.reshape(spans, SPAN, heads, HEADDIM)
    total = inner_mixed + passing[..., None] * from_state + skip[None, None, :, None] * block_values
    return total.reshape(inner_values.shape[0], heads * HEADDIM)

def mixer(padded, flags_padded, sequence_starts, step_raw, conv_weight, conv_bias, step_bias, decay_log, skip, carried):
    kept, final_state, final_product = mixer_front(padded, flags_padded, sequence_starts, step_raw, conv_weight, conv_bias, step_bias, decay_log)
    output = finish(kept, carried, skip)
    return (output, final_state + final_product[:, None, None] * carried)

def reference(block_input_activations, sequence_first_token, norm_gain, gate_proj, input_proj, step_proj, state_proj, conv_inner_weight, conv_inner_bias, conv_state_weight, conv_state_bias, step_bias, decay_log, skip_weight, gate_gain, out_proj, output_cotangent):
    main_weight = jnp.concatenate([gate_proj, input_proj, state_proj], axis=1)
    conv_weight = jnp.concatenate([conv_inner_weight, conv_state_weight], axis=1)
    conv_bias = jnp.concatenate([conv_inner_bias, conv_state_bias])
    width = KCONV - 1
    carried_zero = jnp.zeros((HEADS, HEADDIM, STATE), jnp.float32)

    def row_pass(totals, item):
        input_row, start_row, cotangent_row = item
        hidden = input_row.astype(jnp.float32)
        inv_rms = lax.rsqrt(lax.optimization_barrier(jnp.mean(hidden * hidden, axis=1, keepdims=True)) + EPSILON)
        normed = (hidden * inv_rms * norm_gain[None, :]).astype(jnp.bfloat16)
        projected = jnp.dot(normed, main_weight, preferred_element_type=jnp.float32)
        step_raw = jnp.dot(normed, step_proj, preferred_element_type=jnp.float32)
        gate = projected[:, :INNER]
        conv_rows = projected[:, INNER:].astype(jnp.bfloat16)
        sequence_starts = start_row.astype(jnp.float32)
        padded = jnp.concatenate([jnp.zeros((width, INNER + 2 * STATE), jnp.float32), conv_rows.astype(jnp.float32)], axis=0)
        flags_padded = jnp.concatenate([jnp.zeros((width,), jnp.float32), sequence_starts])

        def local_mixer(padded_in, raw_in, weight_in, bias_in, step_in, decay_in, skip_in):
            return mixer(padded_in, flags_padded, sequence_starts, raw_in, weight_in, bias_in, step_in, decay_in, skip_in, carried_zero)[0]
        mixed, pullback = jax.vjp(local_mixer, padded, step_raw, conv_weight, conv_bias, step_bias, decay_log, skip_weight)
        gate_silu = jax.nn.silu(gate)
        gated = mixed * gate_silu
        gate_inv = lax.rsqrt(lax.optimization_barrier(jnp.mean(gated * gated, axis=1, keepdims=True)) + EPSILON)
        gated_normed = (gated * gate_inv * gate_gain[None, :]).astype(jnp.bfloat16)
        branch = jnp.dot(gated_normed, out_proj, preferred_element_type=jnp.float32)
        output_row = (hidden + branch).astype(jnp.bfloat16)
        grad_gated_normed = jnp.dot(cotangent_row, out_proj.T, preferred_element_type=jnp.float32)
        grad_out = jnp.dot(gated_normed.T, cotangent_row, preferred_element_type=jnp.float32)
        scaled = grad_gated_normed * gate_gain[None, :]
        grad_gated = gate_inv * scaled - gated * gate_inv ** 3 * lax.optimization_barrier(jnp.mean(gated * scaled, axis=1, keepdims=True))
        grad_gain_gate = lax.optimization_barrier(jnp.sum(grad_gated_normed * gated * gate_inv, axis=0))
        sigmoid_gate = jax.nn.sigmoid(gate)
        grad_mixed = grad_gated * gate_silu
        grad_gate = grad_gated * mixed * sigmoid_gate * (1.0 + gate * (1.0 - sigmoid_gate))
        grad_padded, grad_step_raw, grad_conv_weight, grad_conv_bias, grad_step_bias, grad_decay_log, grad_skip = pullback(grad_mixed)
        grad_main = jnp.concatenate([grad_gate, grad_padded[width:]], axis=1).astype(jnp.bfloat16)
        grad_step = grad_step_raw.astype(jnp.bfloat16)
        grad_main_weight = jnp.dot(normed.T, grad_main, preferred_element_type=jnp.float32)
        grad_step_weight = jnp.dot(normed.T, grad_step, preferred_element_type=jnp.float32)
        grad_normed = jnp.dot(grad_main, main_weight.T, preferred_element_type=jnp.float32) + jnp.dot(grad_step, step_proj.T, preferred_element_type=jnp.float32)
        scaled_in = grad_normed * norm_gain[None, :]
        grad_row = cotangent_row.astype(jnp.float32) + inv_rms * scaled_in - hidden * inv_rms ** 3 * lax.optimization_barrier(jnp.mean(hidden * scaled_in, axis=1, keepdims=True))
        grad_gain_norm = lax.optimization_barrier(jnp.sum(grad_normed * hidden * inv_rms, axis=0))
        terms = (grad_main_weight, grad_step_weight, grad_out, grad_conv_weight, grad_conv_bias, grad_step_bias, grad_decay_log, grad_skip, grad_gain_gate, grad_gain_norm)
        return (jax.tree.map(lambda first, second: first + second, totals, terms), (output_row, grad_row))
    init = (jnp.zeros((MODEL_WIDTH, 2 * INNER + 2 * STATE), jnp.float32), jnp.zeros((MODEL_WIDTH, HEADS), jnp.float32), jnp.zeros((INNER, MODEL_WIDTH), jnp.float32), jnp.zeros((KCONV, INNER + 2 * STATE), jnp.float32), jnp.zeros((INNER + 2 * STATE,), jnp.float32), jnp.zeros((HEADS,), jnp.float32), jnp.zeros((HEADS,), jnp.float32), jnp.zeros((HEADS,), jnp.float32), jnp.zeros((INNER,), jnp.float32), jnp.zeros((MODEL_WIDTH,), jnp.float32))
    entry_list = (block_input_activations.reshape(PACKED_ROWS, ROW_POSITIONS, MODEL_WIDTH), sequence_first_token.reshape(PACKED_ROWS, ROW_POSITIONS), output_cotangent.reshape(PACKED_ROWS, ROW_POSITIONS, MODEL_WIDTH))
    totals, (output_rows, grad_rows) = lax.scan(row_pass, init, entry_list)
    grad_main_weight, grad_step_weight, grad_out, grad_conv_weight, grad_conv_bias, grad_step_bias, grad_decay_log, grad_skip, grad_gain_gate, grad_gain_norm = totals
    return (output_rows.reshape(TOKENS, MODEL_WIDTH), grad_rows.reshape(TOKENS, MODEL_WIDTH), grad_gain_norm, grad_main_weight[:, :INNER], grad_main_weight[:, INNER:2 * INNER], grad_step_weight, grad_main_weight[:, 2 * INNER:], grad_conv_weight[:, :INNER], grad_conv_bias[:INNER], grad_conv_weight[:, INNER:], grad_conv_bias[INNER:], grad_step_bias, grad_decay_log, grad_skip, grad_gain_gate, grad_out)
```

```python
import jax
import jax.numpy as jnp
from jax import lax
from jax.experimental import pallas as pl
from jax.experimental.pallas import tpu as pltpu
from jax.sharding import PartitionSpec as P

MODEL_WIDTH = 1024
HEADDIM = 64
STATE = 128
KCONV = 4
SPAN = 256
INNER = 2048


EPSILON = 1e-05
HIGHEST = lax.Precision.HIGHEST


def passed_along(block, distance):
    devices = range(lax.axis_size("ctx"))
    route = [(i - distance, i) for i in devices if i - distance in devices]
    return lax.ppermute(block, "ctx", route)


def place_in(axes):
    place = lax.axis_index(axes[0])
    for axis in axes[1:]:
        place = place * lax.axis_size(axis) + lax.axis_index(axis)
    return place


def device_at(axes, place):
    if len(axes) == 1:
        return {axes[0]: place}
    inner = lax.axis_size(axes[1])
    return {axes[0]: place // inner, axes[1]: lax.rem(place, inner)}


def exchange_kernel(plans, *refs):
    count = len(plans)
    inputs, outputs = refs[:count], refs[count : 2 * count]
    scratch = refs[2 * count :]
    greeted = []
    for axes, size, _, _, _ in plans:
        if axes not in greeted:
            greeted.append(axes)
    barrier = pltpu.get_barrier_semaphore()
    expected = 0
    for axes in greeted:
        size = [p[1] for p in plans if p[0] == axes][0]
        me = place_in(axes)
        for off in range(1, size):
            pl.semaphore_signal(
                barrier,
                inc=1,
                device_id=device_at(axes, lax.rem(me + off, size)),
                device_id_type=pl.DeviceIdType.MESH,
            )
        expected += size - 1
    pl.semaphore_wait(barrier, expected)
    copies = []
    for index, (axes, size, dim, block, first) in enumerate(plans):
        received, own, send_sem, recv_sem, own_sem = scratch[5 * index : 5 * index + 5]
        x = inputs[index]
        me = place_in(axes)

        def piece(place, x=x, dim=dim, block=block, first=first):
            if dim is None:
                return x
            start = pl.multiple_of(place * block[dim], block[dim])
            if dim == 0:
                return x.at[pl.ds(start, block[0]), pl.ds(first, block[1])]
            return x.at[:, pl.ds(start, block[1])]

        sends = []
        for off in range(size - 1, 0, -1):
            target = lax.rem(me + off, size)
            copy = pltpu.make_async_remote_copy(
                src_ref=piece(target),
                dst_ref=received.at[off - 1],
                send_sem=send_sem.at[off - 1],
                recv_sem=recv_sem.at[off - 1],
                device_id=device_at(axes, target),
                device_id_type=pl.DeviceIdType.MESH,
            )
            copy.start()
            sends.append(copy)
        local = pltpu.make_async_copy(piece(me), own, own_sem)
        local.start()
        copies.append((sends, local))
    for index in reversed(range(count)):
        _, size, _, block, _ = plans[index]
        received, own = scratch[5 * index : 5 * index + 2]
        sends, local = copies[index]
        local.wait()
        for copy in sends:
            copy.wait_recv()
        rows = min(16, block[0])

        def add(step, carry, received=received, own=own, out=outputs[index], size=size, rows=rows):
            at = pl.ds(pl.multiple_of(step * rows, rows), rows)
            total = own[at, :].astype(jnp.float32)
            for k in range(size - 1):
                total = total + received[k, at, :].astype(jnp.float32)
            out[at, :] = total.astype(out.dtype)
            return carry

        lax.fori_loop(0, block[0] // rows, add, 0)
    for sends, _ in copies:
        for copy in sends:
            copy.wait_send()


def exchange(items, collective_id):
    plans, out_shape, scratch = [], [], []
    for x, axes, dim, *more in items:
        size = 1
        for axis in axes:
            size *= lax.axis_size(axis)
        block = list(x.shape)
        if dim is not None:
            block[dim] //= size
        first = 0
        if more:
            first, block[1] = more[0]
        block = tuple(block)
        plans.append((axes, size, dim, block, first))
        out_shape.append(jax.ShapeDtypeStruct(block, more[1] if more else jnp.float32))
        scratch += [
            pltpu.VMEM((size - 1,) + block, x.dtype),
            pltpu.VMEM(block, x.dtype),
            pltpu.SemaphoreType.DMA((size - 1,)),
            pltpu.SemaphoreType.DMA((size - 1,)),
            pltpu.SemaphoreType.DMA,
        ]
    return pl.pallas_call(
        lambda *refs: exchange_kernel(plans, *refs),
        out_shape=tuple(out_shape),
        in_specs=[pl.BlockSpec(memory_space=pl.ANY)] * len(items),
        out_specs=tuple([pl.BlockSpec(memory_space=pltpu.VMEM)] * len(items)),
        scratch_shapes=scratch,
        compiler_params=pltpu.CompilerParams(collective_id=collective_id, has_side_effects=True),
        name="exchange" + str(collective_id),
    )(*[item[0] for item in items])


def flat_rows(parts, rows):
    flat = jnp.concatenate([p.reshape(-1) for p in parts])
    return jnp.pad(flat, (0, rows * 128 - flat.shape[0])).reshape(rows, 128)


def conv_apply(padded, flags_padded, conv_weight, conv_bias):
    width = KCONV - 1
    count = padded.shape[0] - width
    total = flags_padded.shape[0]
    upper = jnp.triu(jnp.ones((total, total), jnp.float32))
    segments = jnp.dot(flags_padded, upper, precision=HIGHEST)
    own = segments[width:]
    result = jnp.zeros((count, padded.shape[1]), jnp.float32) + conv_bias[None, :]
    for lag in range(KCONV):
        valid = (segments[width - lag : width - lag + count] == own).astype(jnp.float32)
        result = (
            result
            + conv_weight[lag][None, :] * padded[width - lag : width - lag + count] * valid[:, None]
        )
    return result


def span_parts(inner_values, step_size, state_in, state_out, sequence_starts, decay_rate):
    count = inner_values.shape[0]
    heads = step_size.shape[1]
    spans = count // SPAN
    log_decay = (step_size * decay_rate[None, :]).reshape(spans, SPAN, heads)
    ones_below = jnp.tril(jnp.ones((SPAN, SPAN), jnp.float32))
    cumulative = jnp.einsum("ts,ksh->kth", ones_below, log_decay, precision=HIGHEST)
    segments = jnp.dot(sequence_starts.reshape(spans, SPAN), ones_below.T, precision=HIGHEST)
    block_values = inner_values.reshape(spans, SPAN, heads, HEADDIM)
    block_step = step_size.reshape(spans, SPAN, heads)
    block_in = state_in.reshape(spans, SPAN, STATE)
    block_out = state_out.reshape(spans, SPAN, STATE)
    order = jnp.arange(SPAN)
    lower = order[:, None] >= order[None, :]
    same = ((segments[:, :, None] == segments[:, None, :]) & lower[None])[..., None]
    spread = cumulative[:, :, None, :] - cumulative[:, None, :, :]
    decay = jnp.where(same, jnp.exp(jnp.where(same, spread, 0.0)), 0.0)
    scores = jnp.einsum("ktn,ksn->kts", block_out, block_in)
    mixing = decay * scores[..., None] * block_step[:, None, :, :]
    inner_mixed = jnp.einsum("ktsh,kshp->kthp", mixing, block_values)
    ending = (segments == segments[:, -1:])[..., None]
    to_end = jnp.where(ending, jnp.exp(cumulative[:, -1:, :] - cumulative), 0.0) * block_step
    states = jnp.einsum(
        "kshp,ksn->khpn", block_values * to_end[..., None], block_in
    )
    passing = jnp.where((segments == 0)[..., None], jnp.exp(cumulative), 0.0)
    return (inner_mixed, states, passing)


def fold_spans(states, passing):
    ends = passing[:, -1, :]
    state = jnp.zeros(states.shape[1:], jnp.float32)
    product = jnp.ones(ends.shape[1:], jnp.float32)
    span_states, span_decays = [], []
    for k in range(states.shape[0]):
        span_states.append(state)
        span_decays.append(product)
        state = ends[k][:, None, None] * state + states[k]
        product = ends[k] * product
    return (jnp.stack(span_states), jnp.stack(span_decays), state, product)


def mixer_front(
    padded, flags_padded, sequence_starts, step_raw, conv_weight, conv_bias, step_bias, decay_log
):
    inner_width = padded.shape[1] - 2 * STATE
    activated = jax.nn.silu(conv_apply(padded, flags_padded, conv_weight, conv_bias))
    inner_values = activated[:, :inner_width]
    state_in = activated[:, inner_width : inner_width + STATE]
    state_out = activated[:, inner_width + STATE :]
    step_size = jax.nn.softplus(step_raw + step_bias[None, :])
    decay_rate = -jnp.exp(decay_log)
    inner_mixed, states, passing = span_parts(
        inner_values, step_size, state_in, state_out, sequence_starts, decay_rate
    )
    span_states, span_decays, final_state, final_product = fold_spans(states, passing)
    kept = (inner_values, state_out, inner_mixed, passing, span_states, span_decays)
    return (kept, final_state, final_product)


def finish(kept, carried, skip):
    inner_values, state_out, inner_mixed, passing, span_states, span_decays = kept
    spans = inner_mixed.shape[0]
    heads = inner_mixed.shape[2]
    initial = span_states + span_decays[:, :, None, None] * carried[None]
    block_out = state_out.reshape(spans, SPAN, STATE)
    from_state = jnp.einsum("ktn,khpn->kthp", block_out, initial)
    block_values = inner_values.reshape(spans, SPAN, heads, HEADDIM)
    total = inner_mixed + passing[..., None] * from_state + skip[None, None, :, None] * block_values
    return total.reshape(inner_values.shape[0], heads * HEADDIM)


def mixer(
    padded,
    flags_padded,
    sequence_starts,
    step_raw,
    conv_weight,
    conv_bias,
    step_bias,
    decay_log,
    skip,
    carried,
):
    kept, final_state, final_product = mixer_front(
        padded,
        flags_padded,
        sequence_starts,
        step_raw,
        conv_weight,
        conv_bias,
        step_bias,
        decay_log,
    )
    output = finish(kept, carried, skip)
    return (output, final_state + final_product[:, None, None] * carried)


def on_device(
    block_input_activations,
    sequence_first_token,
    norm_gain,
    gate_proj,
    input_proj,
    step_proj,
    state_proj,
    conv_inner_weight,
    conv_inner_bias,
    conv_state_weight,
    conv_state_bias,
    step_bias,
    decay_log,
    skip_weight,
    gate_gain,
    out_proj,
    output_cotangent,
):
    everyone = ("dp", "ctx")
    bf16 = jnp.bfloat16
    local_inner = gate_proj.shape[1]
    heads = step_bias.shape[0]
    width = KCONV - 1
    full_weight = lax.all_gather(
        jnp.concatenate([gate_proj, input_proj, state_proj, step_proj], axis=1),
        everyone,
        axis=0,
        tiled=True,
    )
    full_out_t = lax.all_gather(out_proj.T, everyone, axis=0, tiled=True)
    hidden = block_input_activations.astype(jnp.float32)
    inv_rms = lax.rsqrt(jnp.mean(hidden * hidden, axis=1, keepdims=True) + EPSILON)
    normed = (hidden * inv_rms * norm_gain[None, :]).astype(bf16)
    projected = jnp.dot(normed, full_weight, preferred_element_type=jnp.float32)
    step_raw = projected[:, 2 * local_inner + 2 * STATE :]
    gate = projected[:, :local_inner]
    conv_rows = projected[:, local_inner : 2 * local_inner + 2 * STATE].astype(bf16)
    sequence_starts = sequence_first_token.astype(jnp.float32)
    tail_rows, tail_flags = passed_along(
        (conv_rows[-width:], sequence_starts[-width:].astype(bf16)), 1
    )
    padded = jnp.concatenate([tail_rows, conv_rows], axis=0).astype(jnp.float32)
    flags_padded = jnp.concatenate([tail_flags.astype(jnp.float32), sequence_starts])
    conv_weight = jnp.concatenate([conv_inner_weight, conv_state_weight], axis=1)
    conv_bias = jnp.concatenate([conv_inner_bias, conv_state_bias])
    kept, final_state, final_product = mixer_front(
        padded,
        flags_padded,
        sequence_starts,
        step_raw,
        conv_weight,
        conv_bias,
        step_bias,
        decay_log,
    )
    carried = passed_along(final_state, 1)
    mixed = finish(kept, carried, skip_weight)
    gate_silu = jax.nn.silu(gate)
    gated = mixed * gate_silu
    grad_gated_normed = jnp.dot(output_cotangent, full_out_t, preferred_element_type=jnp.float32)
    scaled = grad_gated_normed * gate_gain[None, :]
    tokens = hidden.shape[0]
    (row_sums,) = exchange(
        [
            (
                flat_rows(
                    [jnp.sum(gated * gated, axis=1), jnp.sum(gated * scaled, axis=1)],
                    2 * tokens // 128,
                ),
                ("tp",),
                None,
            )
        ],
        1,
    )
    row_sums = row_sums.reshape(2, tokens)
    gate_inv = lax.rsqrt(row_sums[0] / INNER + EPSILON)[:, None]
    gated_normed = (gated * gate_inv * gate_gain[None, :]).astype(bf16)
    share = MODEL_WIDTH // lax.axis_size("tp")
    column = lax.axis_index("tp") * share
    branch_part = lax.dot_general(
        gated_normed, full_out_t, (((1,), (1,)), ((), ())), preferred_element_type=jnp.float32
    ).astype(bf16)
    own_hidden = lax.dynamic_slice_in_dim(hidden, column, share, 1)
    grad_gated = gate_inv * scaled - gated * gate_inv**3 * (row_sums[1] / INNER)[:, None]
    grad_gain_gate = jnp.sum(grad_gated_normed * gated * gate_inv, axis=0)
    sigmoid_gate = jax.nn.sigmoid(gate)
    grad_mixed = grad_gated * gate_silu
    grad_gate = (
        grad_gated * mixed * sigmoid_gate * (1.0 + gate * (1.0 - sigmoid_gate))
    ).astype(bf16)
    grad_out = lax.dot_general(
        output_cotangent,
        gated_normed,
        (((0,), (0,)), ((), ())),
        preferred_element_type=jnp.float32,
    ).astype(bf16)
    grad_gate_weight = jnp.dot(
        normed.T, grad_gate, preferred_element_type=jnp.float32
    ).astype(bf16)
    first_part = jnp.concatenate([grad_gate_weight, grad_out], axis=1)
    grad_mixed, branch_part, first_part = lax.optimization_barrier(
        (grad_mixed, branch_part, first_part)
    )
    branch = lax.psum_scatter(branch_part, "tp", scatter_dimension=1, tiled=True)
    block_output = (own_hidden + branch.astype(jnp.float32)).astype(bf16)
    first_grads = lax.psum_scatter(
        first_part, everyone, scatter_dimension=0, tiled=True
    ).astype(jnp.float32)
    gate_grad = first_grads[:, :local_inner]
    out_proj_grad = first_grads[:, local_inner:].T

    def state_effect(carried_in):
        return finish(kept, carried_in, skip_weight)

    ignored, state_pull = jax.vjp(state_effect, carried)
    (through_mixed,) = state_pull(grad_mixed)
    next_grad = passed_along(through_mixed, -1)

    def full_mixer(padded_in, raw_in, weight_in, bias_in, step_in, decay_in, skip_in):
        return mixer(
            padded_in,
            flags_padded,
            sequence_starts,
            raw_in,
            weight_in,
            bias_in,
            step_in,
            decay_in,
            skip_in,
            carried,
        )

    ignored_out, pullback = jax.vjp(
        full_mixer,
        padded,
        step_raw,
        conv_weight,
        conv_bias,
        step_bias,
        decay_log,
        skip_weight,
    )
    (
        grad_padded,
        grad_step_raw,
        grad_conv_weight,
        grad_conv_bias,
        grad_step_bias,
        grad_decay_log,
        grad_skip,
    ) = pullback((grad_mixed, next_grad))
    returned = passed_along(grad_padded[:width], -1)
    grad_rows = grad_padded[width:]
    grad_rows = jnp.concatenate([grad_rows[:-width], grad_rows[-width:] + returned])
    grad_late = jnp.concatenate([grad_rows, grad_step_raw], axis=1).astype(bf16)
    grad_all = jnp.concatenate([grad_gate, grad_late], axis=1)
    tensor_part = lax.dot_general(
        grad_all, full_weight, (((1,), (1,)), ((), ())), preferred_element_type=jnp.float32
    )
    mean_sum = jnp.sum(hidden * norm_gain[None, :] * tensor_part, axis=1)
    late_pad = -grad_late.shape[1] % 128
    late_weight = jnp.dot(
        normed.T,
        jnp.pad(grad_late, ((0, 0), (0, late_pad))),
        preferred_element_type=jnp.float32,
    ).astype(bf16)
    per_head = jnp.concatenate([grad_step_bias, grad_decay_log, grad_skip])
    inner_rows = jnp.concatenate(
        [
            grad_conv_weight[:, :local_inner],
            grad_conv_bias[None, :local_inner],
            grad_gain_gate[None, :],
            jnp.pad(per_head, (0, local_inner - 3 * heads))[None, :],
            jnp.zeros((1, local_inner), jnp.float32),
        ]
    )
    state_rows = jnp.concatenate(
        [
            grad_conv_weight[:, local_inner:],
            grad_conv_bias[None, local_inner:],
            jnp.zeros((3, 2 * STATE), jnp.float32),
        ]
    )
    wide = late_weight.shape[1] - local_inner - 2 * STATE
    own_grad, mean_sum, input_grads, state_part, step_grads, inner_rows, state_rows = exchange(
        [
            (tensor_part.astype(bf16), ("tp",), 1),
            (mean_sum.reshape(tokens // 128, 128), ("tp",), None),
            (late_weight, everyone, 0, (0, local_inner), jnp.float32),
            (late_weight, everyone, 0, (local_inner, 2 * STATE), bf16),
            (late_weight, everyone, 0, (local_inner + 2 * STATE, wide), jnp.float32),
            (inner_rows, everyone, None),
            (state_rows, everyone, None),
        ],
        2,
    )
    mean_term = mean_sum.reshape(tokens, 1) / MODEL_WIDTH
    own_cotangent = lax.dynamic_slice_in_dim(output_cotangent, column, share, 1).astype(jnp.float32)
    own_gain = lax.dynamic_slice_in_dim(norm_gain, column, share, 0)
    input_grad = (
        own_cotangent
        + inv_rms * own_grad * own_gain[None, :]
        - own_hidden * inv_rms**3 * mean_term
    )
    grad_gain_norm = jnp.sum(own_grad * own_hidden * inv_rms, axis=0)
    gain_rows = jnp.pad(grad_gain_norm[None, :], ((0, 7), (0, 0)))
    state_grad, state_rows, gain_rows = exchange(
        [
            (state_part, ("tp",), None),
            (state_rows, ("tp",), None),
            (gain_rows, everyone, None),
        ],
        3,
    )
    return (
        block_output,
        input_grad,
        gain_rows[0],
        gate_grad,
        input_grads,
        step_grads[:, :heads],
        state_grad,
        inner_rows[:KCONV],
        inner_rows[KCONV],
        state_rows[:KCONV],
        state_rows[KCONV],
        inner_rows[KCONV + 2, :heads],
        inner_rows[KCONV + 2, heads : 2 * heads],
        inner_rows[KCONV + 2, 2 * heads : 3 * heads],
        inner_rows[KCONV + 1],
        out_proj_grad,
    )


def solution(mesh):
    return jax.shard_map(
        on_device,
        mesh=mesh,
        in_specs=(
            P(("dp", "ctx"), None),
            P(("dp", "ctx")),
            P(),
            P(("dp", "ctx"), "tp"),
            P(("dp", "ctx"), "tp"),
            P(("dp", "ctx"), "tp"),
            P(("dp", "ctx"), None),
            P(None, "tp"),
            P("tp"),
            P(),
            P(),
            P("tp"),
            P("tp"),
            P("tp"),
            P("tp"),
            P("tp", ("dp", "ctx")),
            P(("dp", "ctx"), None),
        ),
        out_specs=(
            P(("dp", "ctx"), "tp"),
            P(("dp", "ctx"), "tp"),
            P("tp"),
            P(("dp", "ctx"), "tp"),
            P(("dp", "ctx"), "tp"),
            P(("dp", "ctx"), "tp"),
            P(("dp", "ctx"), None),
            P(None, "tp"),
            P("tp"),
            P(),
            P(),
            P("tp"),
            P("tp"),
            P("tp"),
            P("tp"),
            P("tp", ("dp", "ctx")),
        ),
        check_vma=False,
    )
```

```python
import jax
import jax.numpy as jnp
from jax import lax
from jax.experimental import pallas as pl
from jax.experimental.pallas import tpu as pltpu
from jax.sharding import PartitionSpec as P

MODEL_WIDTH = 1024
HEADDIM = 64
STATE = 128
KCONV = 4
SPAN = 256
INNER = 2048


EPSILON = 1e-05
HIGHEST = lax.Precision.HIGHEST


def passed_along(block, distance):
    devices = range(lax.axis_size("ctx"))
    route = [(i - distance, i) for i in devices if i - distance in devices]
    return lax.ppermute(block, "ctx", route)


def place_in(axes):
    place = lax.axis_index(axes[0])
    for axis in axes[1:]:
        place = place * lax.axis_size(axis) + lax.axis_index(axis)
    return place


def device_at(axes, place):
    if len(axes) == 1:
        return {axes[0]: place}
    inner = lax.axis_size(axes[1])
    return {axes[0]: place // inner, axes[1]: lax.rem(place, inner)}


def exchange_kernel(plans, *refs):
    count = len(plans)
    inputs, outputs = refs[:count], refs[count : 2 * count]
    scratch = refs[2 * count :]
    greeted = []
    for axes, size, _, _, _ in plans:
        if axes not in greeted:
            greeted.append(axes)
    barrier = pltpu.get_barrier_semaphore()
    expected = 0
    for axes in greeted:
        size = [p[1] for p in plans if p[0] == axes][0]
        me = place_in(axes)
        for off in range(1, size):
            pl.semaphore_signal(
                barrier,
                inc=1,
                device_id=device_at(axes, lax.rem(me + off, size)),
                device_id_type=pl.DeviceIdType.MESH,
            )
        expected += size - 1
    pl.semaphore_wait(barrier, expected)
    copies = []
    for index, (axes, size, dim, block, first) in enumerate(plans):
        received, own, send_sem, recv_sem, own_sem = scratch[5 * index : 5 * index + 5]
        x = inputs[index]
        me = place_in(axes)

        def piece(place, x=x, dim=dim, block=block, first=first):
            if dim is None:
                return x
            start = pl.multiple_of(place * block[dim], block[dim])
            if dim == 0:
                return x.at[pl.ds(start, block[0]), pl.ds(first, block[1])]
            return x.at[:, pl.ds(start, block[1])]

        sends = []
        for off in range(size - 1, 0, -1):
            target = lax.rem(me + off, size)
            copy = pltpu.make_async_remote_copy(
                src_ref=piece(target),
                dst_ref=received.at[off - 1],
                send_sem=send_sem.at[off - 1],
                recv_sem=recv_sem.at[off - 1],
                device_id=device_at(axes, target),
                device_id_type=pl.DeviceIdType.MESH,
            )
            copy.start()
            sends.append(copy)
        local = pltpu.make_async_copy(piece(me), own, own_sem)
        local.start()
        copies.append((sends, local))
    for index in reversed(range(count)):
        _, size, _, block, _ = plans[index]
        received, own = scratch[5 * index : 5 * index + 2]
        sends, local = copies[index]
        local.wait()
        for copy in sends:
            copy.wait_recv()
        rows = min(16, block[0])

        def add(step, carry, received=received, own=own, out=outputs[index], size=size, rows=rows):
            at = pl.ds(pl.multiple_of(step * rows, rows), rows)
            total = own[at, :].astype(jnp.float32)
            for k in range(size - 1):
                total = total + received[k, at, :].astype(jnp.float32)
            out[at, :] = total.astype(out.dtype)
            return carry

        lax.fori_loop(0, block[0] // rows, add, 0)
    for sends, _ in copies:
        for copy in sends:
            copy.wait_send()


def exchange(items, collective_id):
    plans, out_shape, scratch = [], [], []
    for x, axes, dim, *more in items:
        size = 1
        for axis in axes:
            size *= lax.axis_size(axis)
        block = list(x.shape)
        if dim is not None:
            block[dim] //= size
        first = 0
        if more:
            first, block[1] = more[0]
        block = tuple(block)
        plans.append((axes, size, dim, block, first))
        out_shape.append(jax.ShapeDtypeStruct(block, more[1] if more else jnp.float32))
        scratch += [
            pltpu.VMEM((size - 1,) + block, x.dtype),
            pltpu.VMEM(block, x.dtype),
            pltpu.SemaphoreType.DMA((size - 1,)),
            pltpu.SemaphoreType.DMA((size - 1,)),
            pltpu.SemaphoreType.DMA,
        ]
    return pl.pallas_call(
        lambda *refs: exchange_kernel(plans, *refs),
        out_shape=tuple(out_shape),
        in_specs=[pl.BlockSpec(memory_space=pl.ANY)] * len(items),
        out_specs=tuple([pl.BlockSpec(memory_space=pltpu.VMEM)] * len(items)),
        scratch_shapes=scratch,
        compiler_params=pltpu.CompilerParams(collective_id=collective_id, has_side_effects=True),
        name="exchange" + str(collective_id),
    )(*[item[0] for item in items])


LANES = 128
VMEM_LIMIT = 60 * 1024 * 1024
BF16 = jnp.bfloat16
F32 = jnp.float32
BLOCKED = -1e30


def dot_nn(a, b):
    return jnp.dot(a, b, preferred_element_type=F32)


def dot_nt(a, b):
    return lax.dot_general(a, b, (((1,), (1,)), ((), ())), preferred_element_type=F32)


def dot_tn(a, b):
    return lax.dot_general(a, b, (((0,), (0,)), ((), ())), preferred_element_type=F32)


def iota(shape, dim):
    return lax.broadcasted_iota(jnp.int32, shape, dim)


def high_low(a):
    high = a.astype(BF16)
    return high, (a - high.astype(F32)).astype(BF16)


def widen(a, heads, width):
    lane = iota(a.shape, 1)
    high = a.astype(BF16).astype(F32)
    low = pltpu.roll(a - high, heads, 1)
    packed = jnp.where(lane < heads, high, jnp.where(lane < 2 * heads, low, 0.0)).astype(BF16)
    row, column = iota((LANES, width), 0), iota((LANES, width), 1)
    place = jnp.where(row < heads, row, row - heads)
    return dot_nn(packed, (column // HEADDIM == place).astype(BF16))


def per_head_sum(a, heads):
    high, low = high_low(a)
    row, column = iota((LANES, a.shape[1]), 0), iota((LANES, a.shape[1]), 1)
    pick = (column // HEADDIM == row).astype(BF16)
    return dot_nt(high, pick) + dot_nt(low, pick)


def rows_of_heads(column, heads):
    return jnp.concatenate(
        [jnp.broadcast_to(column[h : h + 1, :], (HEADDIM, LANES)) for h in range(heads)], axis=0
    )


def sigmoid(v):
    return 1.0 / (1.0 + jnp.exp(-v))


def normalise(x, gain):
    hidden = x.astype(F32)
    inv = lax.rsqrt(jnp.mean(hidden * hidden, axis=1, keepdims=True) + EPSILON)
    return (hidden * inv * gain).astype(BF16)


def whole(shape):
    return pl.BlockSpec(shape, lambda i: (0,) * len(shape))


def columns_of(array, width, block):
    return pl.BlockSpec((array.shape[0], width), lambda i: (0, block))


def front_kernel(
    heads,
    x_ref,
    marks_ref,
    halo_x_ref,
    gain_ref,
    weight_ref,
    taps_ref,
    bias_ref,
    step_bias_ref,
    decay_ref,
    skip_ref,
    normed_ref,
    rows_ref,
    conv_ref,
    mixed_ref,
    cum_ref,
    raw_ref,
    passing_ref,
    out_map_ref,
    states_ref,
    products_ref,
    final_ref,
    halo_rows_ref,
    state,
    product,
    before,
):
    step = pl.program_id(0)
    channels = heads * HEADDIM
    main = channels + 2 * STATE
    gain = gain_ref[...]

    @pl.when(step == 0)
    def _():
        state[...] = jnp.zeros_like(state)
        product[...] = jnp.ones_like(product)
        halo = dot_nn(normalise(halo_x_ref[...], gain), weight_ref[:, :main]).astype(BF16)
        halo_rows_ref[...] = halo
        before[...] = halo.astype(F32)[8:16]

    normed = normalise(x_ref[...], gain)
    normed_ref[...] = normed
    projected = dot_nn(normed, weight_ref[...])
    rows = projected[:, :main].astype(BF16)
    rows_ref[...] = rows
    rows = rows.astype(F32)
    raw = projected[:, main:] + step_bias_ref[...]
    raw_ref[...] = raw
    extended = jnp.concatenate([before[...], rows], axis=0)
    before[...] = rows[SPAN - 8 :]
    taps = taps_ref[...]
    conv = bias_ref[...] + taps[0:1] * rows
    for lag in range(1, KCONV):
        valid = marks_ref[:, lag : lag + 1]
        conv = conv + (taps[lag : lag + 1] * extended[8 - lag : 8 - lag + SPAN]) * valid
    conv_ref[...] = conv
    act = conv * sigmoid(conv)
    values = act[:, :channels]
    map_in = act[:, channels : channels + STATE].astype(BF16)
    map_out = act[:, channels + STATE :].astype(BF16)
    out_map_ref[...] = map_out

    step_size = jnp.maximum(raw, 0.0) + jnp.log1p(jnp.exp(-jnp.abs(raw)))
    lane = iota((SPAN, LANES), 1)
    log_decay = jnp.where(lane < heads, step_size * (-jnp.exp(decay_ref[...])), 0.0)
    series = jnp.where(lane == heads, marks_ref[:, 0:1], log_decay)
    t, s = iota((SPAN, SPAN), 0), iota((SPAN, SPAN), 1)
    cum = jnp.dot((t >= s).astype(F32), series, precision=HIGHEST, preferred_element_type=F32)
    cum_ref[...] = cum
    cum_rows = cum.T
    segment, segment_row = cum[:, heads : heads + 1], cum_rows[heads : heads + 1, :]
    blocked = jnp.where((segment == segment_row) & (t >= s), 0.0, BLOCKED)
    passing = jnp.where(segment == 0.0, jnp.exp(cum), 0.0)
    product_now = product[...]
    passing_ref[...] = passing * product_now[0:1]
    products_ref[0] = product_now
    product[...] = product_now * passing[SPAN - 1 : SPAN]
    to_end = jnp.where(
        segment == cum[SPAN - 1 : SPAN, heads : heads + 1], jnp.exp(cum[SPAN - 1 : SPAN] - cum), 0.0
    )
    stepped = values * widen(step_size, heads, channels)
    state_now = state[...]
    states_ref[0] = state_now
    scores = dot_nt(map_out, map_in)
    through = widen(passing, heads, channels) * dot_nt(map_out, state_now.astype(BF16))
    half = iota((SPAN, LANES), 1) < HEADDIM
    for pair in range(heads // 2):
        at = slice(pair * LANES, (pair + 1) * LANES)
        both = stepped[:, at]
        total = through[:, at] + skip_ref[:, at] * values[:, at]
        for side in range(2):
            h = 2 * pair + side
            spread = cum[:, h : h + 1] - cum_rows[h : h + 1, :]
            mixing = (jnp.exp(spread + blocked) * scores).astype(BF16)
            own = jnp.where(half if side == 0 else ~half, both, 0.0).astype(BF16)
            total = total + dot_nn(mixing, own)
        mixed_ref[:, at] = total
    ending = (stepped * widen(to_end, heads, channels)).astype(BF16)
    fresh = dot_tn(ending, map_in)
    kept = jnp.where(segment_row[:, SPAN - 1 :] == 0.0, jnp.exp(cum_rows[:, SPAN - 1 :]), 0.0)
    state_next = rows_of_heads(kept, heads) * state_now + fresh
    state[...] = state_next
    final_ref[...] = state_next


def front(x, marks, halo_x, gain, weight, taps, bias, step_bias, decay, skip, heads):
    tokens = x.shape[0]
    channels = heads * HEADDIM
    main = channels + 2 * STATE
    spans = tokens // SPAN

    def chunk(width):
        return pl.BlockSpec((SPAN, width), lambda i: (i, 0))

    def out(shape, dtype):
        return jax.ShapeDtypeStruct(shape, dtype)

    return pl.pallas_call(
        lambda *refs: front_kernel(heads, *refs),
        grid=(spans,),
        in_specs=[
            chunk(MODEL_WIDTH),
            chunk(8),
            whole(halo_x.shape),
            whole(gain.shape),
            whole(weight.shape),
            whole(taps.shape),
            whole(bias.shape),
            whole(step_bias.shape),
            whole(decay.shape),
            whole(skip.shape),
        ],
        out_specs=[
            chunk(MODEL_WIDTH),
            chunk(main),
            chunk(main),
            chunk(channels),
            chunk(LANES),
            chunk(LANES),
            chunk(LANES),
            chunk(STATE),
            pl.BlockSpec((1, channels, STATE), lambda i: (i, 0, 0)),
            pl.BlockSpec((1, 8, LANES), lambda i: (i, 0, 0)),
            whole((channels, STATE)),
            whole((16, main)),
        ],
        out_shape=[
            out((tokens, MODEL_WIDTH), BF16),
            out((tokens, main), BF16),
            out((tokens, main), F32),
            out((tokens, channels), F32),
            out((tokens, LANES), F32),
            out((tokens, LANES), F32),
            out((tokens, LANES), F32),
            out((tokens, STATE), BF16),
            out((spans, channels, STATE), F32),
            out((spans, 8, LANES), F32),
            out((channels, STATE), F32),
            out((16, main), BF16),
        ],
        scratch_shapes=[
            pltpu.VMEM((channels, STATE), F32),
            pltpu.VMEM((8, LANES), F32),
            pltpu.VMEM((8, main), F32),
        ],
        compiler_params=pltpu.CompilerParams(vmem_limit_bytes=VMEM_LIMIT),
        cost_estimate=pl.CostEstimate(
            flops=2 * tokens * (MODEL_WIDTH * weight.shape[1] + 4 * SPAN * channels),
            bytes_accessed=18 * 2**20,
            transcendentals=tokens * SPAN * heads,
        ),
        name="scan_front",
    )(x, marks, halo_x, gain, weight, taps, bias, step_bias, decay, skip)


def gate_kernel(
    heads,
    normed_ref,
    cot_ref,
    local_ref,
    passing_ref,
    out_map_ref,
    carried_ref,
    weight_ref,
    out_t_ref,
    gain_ref,
    gate_ref,
    mixed_ref,
    back_ref,
    sums_ref,
):
    channels = heads * HEADDIM
    gate = dot_nn(normed_ref[...], weight_ref[...])
    gate_ref[...] = gate
    back = dot_nn(cot_ref[...], out_t_ref[...])
    back_ref[...] = back
    from_carried = dot_nt(out_map_ref[...], carried_ref[...].astype(BF16))
    mixed = local_ref[...] + widen(passing_ref[...], heads, channels) * from_carried
    mixed_ref[...] = mixed
    gated = mixed * (gate * sigmoid(gate))
    ones = jnp.ones((8, channels), BF16)
    sums = []
    for term in (gated * gated, gated * (back * gain_ref[...])):
        high, low = high_low(term)
        sums.append(dot_nt(ones, high) + dot_nt(ones, low))
    sums_ref[...] = jnp.where(iota((8, SPAN), 0) < 4, sums[0], sums[1])


def gate_pass(normed, cot, local, passing, out_map, carried, early_weight, gain, heads):
    tokens = normed.shape[0]
    channels = heads * HEADDIM

    def chunk(width):
        return pl.BlockSpec((SPAN, width), lambda i: (i, 0))

    return pl.pallas_call(
        lambda *refs: gate_kernel(heads, *refs),
        grid=(tokens // SPAN,),
        in_specs=[
            chunk(MODEL_WIDTH),
            chunk(MODEL_WIDTH),
            chunk(channels),
            chunk(LANES),
            chunk(STATE),
            whole(carried.shape),
            columns_of(early_weight, channels, 0),
            columns_of(early_weight, channels, 1),
            whole(gain.shape),
        ],
        out_specs=[
            chunk(channels),
            chunk(channels),
            chunk(channels),
            pl.BlockSpec((8, SPAN), lambda i: (0, i)),
        ],
        out_shape=[jax.ShapeDtypeStruct((tokens, channels), F32)] * 3
        + [jax.ShapeDtypeStruct((8, tokens), F32)],
        compiler_params=pltpu.CompilerParams(vmem_limit_bytes=VMEM_LIMIT),
        cost_estimate=pl.CostEstimate(
            flops=4 * tokens * MODEL_WIDTH * channels,
            bytes_accessed=16 * 2**20,
            transcendentals=tokens * channels,
        ),
        name="gate_pass",
    )(normed, cot, local, passing, out_map, carried, early_weight, early_weight, gain)


def middle_kernel(
    heads,
    gate_ref,
    mixed_ref,
    back_ref,
    sums_ref,
    passing_ref,
    out_map_ref,
    out_t_ref,
    gain_ref,
    gated_ref,
    grad_mixed_ref,
    grad_gate_ref,
    branch_ref,
    through_ref,
    grad_gain_ref,
):
    channels = heads * HEADDIM
    step = pl.program_id(0)
    rows = sums_ref[...]
    square = jnp.broadcast_to(rows[0:1], (LANES, SPAN)).T[:, 0:1]
    cross = jnp.broadcast_to(rows[4:5], (LANES, SPAN)).T[:, 0:1]
    inv = lax.rsqrt(square / INNER + EPSILON)
    gate, mixed, back, gain = gate_ref[...], mixed_ref[...], back_ref[...], gain_ref[...]
    sig = sigmoid(gate)
    gate_silu = gate * sig
    gated = mixed * gate_silu
    scaled = back * gain
    normal = gated * inv
    normal_gain = (normal * gain).astype(BF16)
    gated_ref[...] = normal_gain
    branch_ref[...] = dot_nt(normal_gain, out_t_ref[...]).astype(BF16)
    grad_gated = inv * scaled - normal * (inv * inv * (cross / INNER))
    grad_mixed = grad_gated * gate_silu
    grad_mixed_ref[...] = grad_mixed
    grad_gate = grad_gated * mixed * sig * (1.0 + gate * (1.0 - sig))
    grad_gate_ref[...] = grad_gate.astype(BF16)
    reaching = (grad_mixed * widen(passing_ref[...], heads, channels)).astype(BF16)
    through = dot_tn(reaching, out_map_ref[...])
    gain_part = jnp.broadcast_to(jnp.sum(back * normal, axis=0, keepdims=True), (8, channels))

    @pl.when(step == 0)
    def _():
        through_ref[...] = through
        grad_gain_ref[...] = gain_part

    @pl.when(step > 0)
    def _():
        through_ref[...] += through
        grad_gain_ref[...] += gain_part


def middle_pass(gate, mixed, back, sums, passing, out_map, early_weight, gain, heads):
    tokens = gate.shape[0]
    channels = heads * HEADDIM

    def chunk(width):
        return pl.BlockSpec((SPAN, width), lambda i: (i, 0))

    return pl.pallas_call(
        lambda *refs: middle_kernel(heads, *refs),
        grid=(tokens // SPAN,),
        in_specs=[
            chunk(channels),
            chunk(channels),
            chunk(channels),
            pl.BlockSpec((8, SPAN), lambda i: (0, i)),
            chunk(LANES),
            chunk(STATE),
            columns_of(early_weight, channels, 1),
            whole(gain.shape),
        ],
        out_specs=[
            chunk(channels),
            chunk(channels),
            chunk(channels),
            chunk(MODEL_WIDTH),
            whole((channels, STATE)),
            whole((8, channels)),
        ],
        out_shape=[
            jax.ShapeDtypeStruct((tokens, channels), BF16),
            jax.ShapeDtypeStruct((tokens, channels), F32),
            jax.ShapeDtypeStruct((tokens, channels), BF16),
            jax.ShapeDtypeStruct((tokens, MODEL_WIDTH), BF16),
            jax.ShapeDtypeStruct((channels, STATE), F32),
            jax.ShapeDtypeStruct((8, channels), F32),
        ],
        compiler_params=pltpu.CompilerParams(vmem_limit_bytes=VMEM_LIMIT),
        cost_estimate=pl.CostEstimate(
            flops=2 * tokens * MODEL_WIDTH * channels,
            bytes_accessed=14 * 2**20,
            transcendentals=tokens * channels,
        ),
        name="middle_pass",
    )(gate, mixed, back, sums, passing, out_map, early_weight, gain)


def back_kernel(
    heads,
    grad_ref,
    conv_ref,
    rows_ref,
    earlier_ref,
    halo_ref,
    marks_ref,
    raw_ref,
    cum_ref,
    states_ref,
    products_ref,
    carried_ref,
    next_ref,
    taps_ref,
    decay_ref,
    skip_ref,
    late_ref,
    tail_ref,
    halo_grad_ref,
    sums_ref,
    head_sums_ref,
    flowing,
    after,
):
    step = pl.program_id(0)
    spans = pl.num_programs(0)
    channels = heads * HEADDIM
    main = channels + 2 * STATE

    @pl.when(step == 0)
    def _():
        flowing[...] = next_ref[...]
        after[...] = jnp.zeros_like(after)
        sums_ref[...] = jnp.zeros_like(sums_ref)
        head_sums_ref[...] = jnp.zeros_like(head_sums_ref)

    conv = conv_ref[...]
    sig = sigmoid(conv)
    act = conv * sig
    slope = sig * (1.0 + conv * (1.0 - sig))
    values = act[:, :channels]
    map_in = act[:, channels : channels + STATE].astype(BF16)
    map_out = act[:, channels + STATE :].astype(BF16)
    raw = raw_ref[...]
    step_size = jnp.maximum(raw, 0.0) + jnp.log1p(jnp.exp(-jnp.abs(raw)))
    cum = cum_ref[...]
    cum_rows = cum.T
    segment, segment_row = cum[:, heads : heads + 1], cum_rows[heads : heads + 1, :]
    s, t = iota((SPAN, SPAN), 0), iota((SPAN, SPAN), 1)
    blocked = jnp.where((segment == segment_row) & (t >= s), 0.0, BLOCKED)
    passing = jnp.where(segment == 0.0, jnp.exp(cum), 0.0)
    to_end = jnp.where(
        segment == cum[SPAN - 1 : SPAN, heads : heads + 1], jnp.exp(cum[SPAN - 1 : SPAN] - cum), 0.0
    )
    kept = jnp.where(segment_row[:, SPAN - 1 :] == 0.0, jnp.exp(cum_rows[:, SPAN - 1 :]), 0.0)
    product_column = jnp.broadcast_to(products_ref[0][0:1], (LANES, LANES)).T
    state = states_ref[0] + rows_of_heads(product_column[:, 0:1], heads) * carried_ref[...]
    state_bf = state.astype(BF16)
    flow = flowing[...]
    flow_bf = flow.astype(BF16)
    grad = grad_ref[...]
    step_wide = widen(step_size, heads, channels)
    end_wide = widen(to_end, heads, channels)
    stepped = values * step_wide
    stepped_bf = stepped.astype(BF16)
    grad_bf = grad.astype(BF16)
    reaching = grad * widen(passing, heads, channels)
    reaching_bf = reaching.astype(BF16)
    ending = stepped * end_wide
    ending_bf = ending.astype(BF16)
    from_state = dot_nt(map_out, state_bf)
    from_flow = dot_nt(map_in, flow_bf)
    scores = dot_nt(map_in, map_out)
    half = iota((SPAN, LANES), 1) < HEADDIM
    zero = jnp.zeros((SPAN, LANES), BF16)
    lane = iota((SPAN, LANES), 1)
    grad_scores = jnp.zeros((SPAN, SPAN), F32)
    out_sums = jnp.zeros((SPAN, LANES), F32)
    in_sums = []
    grad_stepped = []
    for pair in range(heads // 2):
        at = slice(pair * LANES, (pair + 1) * LANES)
        total = end_wide[:, at] * from_flow[:, at]
        for side in range(2):
            h = 2 * pair + side
            own = half if side == 0 else ~half
            decay = jnp.exp((cum_rows[h : h + 1, :] - cum[:, h : h + 1]) + blocked)
            own_grad = jnp.where(own, grad_bf[:, at], zero)
            total = total + dot_nn((decay * scores).astype(BF16), own_grad)
            flowed = decay * dot_nt(stepped_bf[:, at], own_grad)
            grad_scores = grad_scores + flowed
            weighed = flowed * scores
            in_sums.append(jnp.sum(weighed, axis=0, keepdims=True))
            out_sums = jnp.where(lane == h, jnp.sum(weighed, axis=1, keepdims=True), out_sums)
        grad_stepped.append(total)
    grad_stepped = jnp.concatenate(grad_stepped, axis=1)
    grad_scores = grad_scores.astype(BF16)
    grad_out_map = dot_tn(grad_scores, map_in) + dot_nn(reaching_bf, state_bf)
    grad_in_map = dot_nn(grad_scores, map_out) + dot_nn(ending_bf, flow_bf)
    ended = per_head_sum(ending * from_flow, heads)
    row, column = iota((LANES, channels), 0), iota((LANES, channels), 1)
    pick = (column // HEADDIM == row).astype(BF16)
    high, low = high_low(flow * state)
    at_last = kept * jnp.sum(dot_nn(pick, high) + dot_nn(pick, low), axis=1, keepdims=True)
    in_rows = jnp.concatenate(
        in_sums + [jnp.zeros((LANES - heads, SPAN), F32)], axis=0
    ) + jnp.where(iota((LANES, SPAN), 1) == SPAN - 1, at_last, 0.0)
    last = iota((SPAN, LANES), 0) == SPAN - 1
    grad_cum = (
        in_rows.T
        - out_sums
        + per_head_sum(reaching * from_state, heads)
        - ended
        + jnp.where(last, jnp.sum(ended, axis=0, keepdims=True), 0.0)
    )
    grad_log = jnp.dot((t >= s).astype(F32), grad_cum, precision=HIGHEST, preferred_element_type=F32)
    rate = -jnp.exp(decay_ref[...])
    grad_step = per_head_sum(grad_stepped * values, heads) + grad_log * rate
    grad_raw = jnp.where(lane < heads, grad_step * sigmoid(raw), 0.0)
    late_ref[:, main:] = grad_raw.astype(BF16)
    head_sums_ref[0:1] += jnp.sum(grad_raw, axis=0, keepdims=True)
    head_sums_ref[1:2] += jnp.sum(grad_log * step_size, axis=0, keepdims=True) * rate
    flowing[...] = rows_of_heads(kept, heads) * flow + dot_tn(reaching_bf, map_out)
    grad_values = grad_stepped * step_wide + skip_ref[...] * grad
    grad_act = jnp.concatenate([grad_values, grad_in_map, grad_out_map], axis=1)
    grad_conv = grad_act * slope
    sums_ref[5:6, :channels] += jnp.sum(grad * values, axis=0, keepdims=True)
    sums_ref[4:5] += jnp.sum(grad_conv, axis=0, keepdims=True)
    rows = rows_ref[...].astype(F32)
    first = step == spans - 1
    previous = jnp.where(first, halo_ref[...].astype(F32), earlier_ref[...].astype(F32))[8:16]
    extended = jnp.concatenate([previous, rows], axis=0)
    sums_ref[0:1] += jnp.sum(grad_conv * rows, axis=0, keepdims=True)
    taps = taps_ref[...]
    grad_rows = taps[0:1] * grad_conv
    halo_grad = jnp.zeros((8, main), F32)
    for lag in range(1, KCONV):
        valid = grad_conv * marks_ref[:, lag : lag + 1]
        sums_ref[lag : lag + 1] += jnp.sum(
            valid * extended[8 - lag : 8 - lag + SPAN], axis=0, keepdims=True
        )
        tapped = taps[lag : lag + 1] * valid
        joined = jnp.concatenate([tapped, after[lag - 1]], axis=0)
        grad_rows = grad_rows + joined[lag : lag + SPAN]
        head = tapped[0:8]
        after[lag - 1] = head
        halo_grad = halo_grad + jnp.concatenate([jnp.zeros((8, main), F32), head], axis=0)[lag : lag + 8]
    late_ref[:, :main] = grad_rows.astype(BF16)
    halo_grad_ref[...] = halo_grad

    @pl.when(step == 0)
    def _():
        tail_ref[...] = grad_rows[SPAN - 16 :]


def back_pass(
    grad, conv, rows, halo, marks, raw, cum, states, products, carried, following, taps, decay, skip, heads
):
    tokens = grad.shape[0]
    channels = heads * HEADDIM
    main = channels + 2 * STATE
    spans = tokens // SPAN

    def chunk(width):
        return pl.BlockSpec((SPAN, width), lambda i: (spans - 1 - i, 0))

    return pl.pallas_call(
        lambda *refs: back_kernel(heads, *refs),
        grid=(spans,),
        in_specs=[
            chunk(channels),
            chunk(main),
            chunk(main),
            pl.BlockSpec((16, main), lambda i: (jnp.maximum((spans - 1 - i) * (SPAN // 16) - 1, 0), 0)),
            whole(halo.shape),
            chunk(8),
            chunk(LANES),
            chunk(LANES),
            pl.BlockSpec((1, channels, STATE), lambda i: (spans - 1 - i, 0, 0)),
            pl.BlockSpec((1, 8, LANES), lambda i: (spans - 1 - i, 0, 0)),
            whole(carried.shape),
            whole(following.shape),
            whole(taps.shape),
            whole(decay.shape),
            whole(skip.shape),
        ],
        out_specs=[
            chunk(main + LANES),
            whole((16, main)),
            whole((8, main)),
            whole((8, main)),
            whole((8, LANES)),
        ],
        out_shape=[
            jax.ShapeDtypeStruct((tokens, main + LANES), BF16),
            jax.ShapeDtypeStruct((16, main), F32),
            jax.ShapeDtypeStruct((8, main), F32),
            jax.ShapeDtypeStruct((8, main), F32),
            jax.ShapeDtypeStruct((8, LANES), F32),
        ],
        scratch_shapes=[
            pltpu.VMEM((channels, STATE), F32),
            pltpu.VMEM((KCONV - 1, 8, main), F32),
        ],
        compiler_params=pltpu.CompilerParams(vmem_limit_bytes=VMEM_LIMIT),
        cost_estimate=pl.CostEstimate(
            flops=2 * tokens * 12 * SPAN * channels,
            bytes_accessed=12 * 2**20,
            transcendentals=tokens * SPAN * heads,
        ),
        name="scan_back",
    )(
        grad, conv, rows, rows, halo, marks, raw, cum, states, products, carried, following, taps, decay, skip
    )


def input_kernel(
    x_ref, grad_gate_ref, late_ref, gate_weight_ref, late_weight_ref, gain_ref, part_ref, sums_ref, grad_gain_ref
):
    step = pl.program_id(0)
    part = dot_nt(grad_gate_ref[...], gate_weight_ref[...]) + dot_nt(late_ref[...], late_weight_ref[...])
    part_ref[...] = part.astype(BF16)
    hidden = x_ref[...].astype(F32)
    inv = lax.rsqrt(jnp.mean(hidden * hidden, axis=1, keepdims=True) + EPSILON)
    term = part * hidden
    high, low = high_low(term * gain_ref[...])
    ones = jnp.ones((8, MODEL_WIDTH), BF16)
    sums_ref[...] = dot_nt(ones, high) + dot_nt(ones, low)
    gain_part = jnp.sum(term * inv, axis=0, keepdims=True)

    @pl.when(step == 0)
    def _():
        grad_gain_ref[...] = jnp.zeros_like(grad_gain_ref)

    grad_gain_ref[0:1] += gain_part


def input_pass(x, grad_gate, late, early_weight, late_weight, gain):
    tokens = x.shape[0]
    channels = grad_gate.shape[1]

    def chunk(width):
        return pl.BlockSpec((SPAN, width), lambda i: (i, 0))

    return pl.pallas_call(
        input_kernel,
        grid=(tokens // SPAN,),
        in_specs=[
            chunk(MODEL_WIDTH),
            chunk(channels),
            chunk(late.shape[1]),
            columns_of(early_weight, channels, 0),
            whole(late_weight.shape),
            whole(gain.shape),
        ],
        out_specs=[
            chunk(MODEL_WIDTH),
            pl.BlockSpec((8, SPAN), lambda i: (0, i)),
            whole((8, MODEL_WIDTH)),
        ],
        out_shape=[
            jax.ShapeDtypeStruct((tokens, MODEL_WIDTH), BF16),
            jax.ShapeDtypeStruct((8, tokens), F32),
            jax.ShapeDtypeStruct((8, MODEL_WIDTH), F32),
        ],
        compiler_params=pltpu.CompilerParams(vmem_limit_bytes=VMEM_LIMIT),
        cost_estimate=pl.CostEstimate(
            flops=2 * tokens * MODEL_WIDTH * (channels + late.shape[1]),
            bytes_accessed=10 * 2**20,
            transcendentals=0,
        ),
        name="input_pass",
    )(x, grad_gate, late, early_weight, late_weight, gain)


MESH = pl.DeviceIdType.MESH


def remote(source, target, sends, receives, place):
    return pltpu.make_async_remote_copy(
        src_ref=source,
        dst_ref=target,
        send_sem=sends,
        recv_sem=receives,
        device_id=place,
        device_id_type=MESH,
    )


def greet(places):
    barrier = pltpu.get_barrier_semaphore()
    for place in places:
        pl.semaphore_signal(barrier, inc=1, device_id=place, device_id_type=MESH)
    pl.semaphore_wait(barrier, len(places))


def peers_of(axis):
    size, me = lax.axis_size(axis), lax.axis_index(axis)
    return [lax.rem(me + off, size) for off in range(1, size)]


def gather_kernel(count, *refs):
    shards, (x_ref, flags_ref) = refs[:count], refs[count : count + 2]
    outs, (halo_ref, other_flags_ref) = refs[count + 2 : 2 * count + 2], refs[2 * count + 2 : 2 * count + 4]
    send, receive, pass_send, pass_receive, own_sem, side_send, side_receive = refs[2 * count + 4 :]
    size, me = lax.axis_size("dp"), lax.axis_index("dp")
    core = lax.axis_index("ctx")
    partner = {"ctx": 1 - core}
    peers = peers_of("dp")
    greet([partner] + [{"dp": p} for p in peers])

    def rows(out, owner):
        depth = out.shape[0] // (2 * size)
        return out.at[pl.ds(pl.multiple_of((owner * 2 + core) * depth, depth), depth)]

    last = x_ref.shape[0] - 16
    waits = [
        remote(x_ref.at[pl.ds(last, 16)], halo_ref, side_send.at[0], side_receive.at[0], partner),
        remote(flags_ref, other_flags_ref, side_send.at[1], side_receive.at[1], partner),
    ]
    for copy in waits:
        copy.start()
    arriving, local = [], []
    for k in range(count):
        for off in range(size - 1, 0, -1):
            copy = remote(
                shards[k],
                rows(outs[k], me),
                send.at[k, off - 1],
                receive.at[k, off - 1],
                {"dp": peers[off - 1]},
            )
            copy.start()
            arriving.append((k, off, copy))
        copy = remote(shards[k], rows(outs[k], me), pass_send.at[k, 0], pass_receive.at[k, 0], partner)
        copy.start()
        waits.append(copy)
        copy = pltpu.make_async_copy(shards[k], rows(outs[k], me), own_sem.at[k])
        copy.start()
        local.append(copy)
    for k, off, copy in arriving:
        copy.wait_recv()
        block = rows(outs[k], lax.rem(me + size - off, size))
        onward = remote(block, block, pass_send.at[k, off], pass_receive.at[k, off], partner)
        onward.start()
        waits.append(onward)
    for copy in local + waits:
        copy.wait()
    for _, _, copy in arriving:
        copy.wait_send()


def gather(shards, x, flags, collective_id):
    size, count = lax.axis_size("dp"), len(shards)
    anywhere = pl.BlockSpec(memory_space=pl.ANY)
    dma = pltpu.SemaphoreType.DMA
    return pl.pallas_call(
        lambda *refs: gather_kernel(count, *refs),
        in_specs=[anywhere] * (count + 2),
        out_specs=[anywhere] * (count + 2),
        out_shape=[jax.ShapeDtypeStruct((s.shape[0] * 2 * size, s.shape[1]), s.dtype) for s in shards]
        + [jax.ShapeDtypeStruct((16, x.shape[1]), x.dtype), jax.ShapeDtypeStruct(flags.shape, flags.dtype)],
        scratch_shapes=[
            dma((count, size - 1)),
            dma((count, size - 1)),
            dma((count, size)),
            dma((count, size)),
            dma((count,)),
            dma((2,)),
            dma((2,)),
        ],
        compiler_params=pltpu.CompilerParams(collective_id=collective_id, has_side_effects=True),
        name="gather",
    )(*shards, x, flags)


def add_rows(out, terms, step_rows, first=0, width=None):
    rows = out.shape[0]
    columns = slice(None) if width is None else pl.ds(first, width)

    def add(step, carry):
        at = pl.ds(pl.multiple_of(step * step_rows, step_rows), step_rows)
        total = terms[0][at, columns].astype(F32)
        for term in terms[1:]:
            total = total + term[at, columns].astype(F32)
        out[at, :] = total.astype(out.dtype)
        return carry

    lax.fori_loop(0, rows // step_rows, add, 0)


def final_kernel(
    local_inner,
    shared,
    part_ref,
    mean_ref,
    early_ref,
    late_ref,
    small_ref,
    own_ref,
    mean_out_ref,
    gate_ref,
    out_ref,
    inner_ref,
    state_ref,
    step_ref,
    small_out_ref,
    part_in,
    part_own,
    mean_in,
    early_own,
    early_in,
    early_far,
    late_own,
    late_in,
    late_far,
    small_in,
    small_sum,
    small_far,
    shared_own,
    shared_in,
    state_own,
    state_in,
    z_send,
    z_receive,
    near_send,
    near_receive,
    far_send,
    far_receive,
    own_sem,
    small_send,
    small_receive,
):
    size, me = lax.axis_size("dp"), lax.axis_index("dp")
    line = lax.axis_size("tp")
    core = lax.axis_index("ctx")
    partner = {"ctx": 1 - core}
    dp_peers, tp_peers = peers_of("dp"), peers_of("tp")
    greet([partner] + [{"dp": p} for p in dp_peers] + [{"tp": p} for p in tp_peers])
    share = part_ref.shape[1] // line

    def columns(owner):
        return part_ref.at[:, pl.ds(pl.multiple_of(owner * share, share), share)]

    z_copies = []
    for off in range(line - 1, 0, -1):
        place = {"tp": tp_peers[off - 1]}
        z_copies.append(
            remote(columns(tp_peers[off - 1]), part_in.at[off - 1], z_send.at[0, off - 1], z_receive.at[0, off - 1], place)
        )
        z_copies.append(remote(mean_ref, mean_in.at[off - 1], z_send.at[1, off - 1], z_receive.at[1, off - 1], place))
    for copy in z_copies:
        copy.start()
    own_part = pltpu.make_async_copy(columns(lax.axis_index("tp")), part_own, own_sem.at[2, 0])
    own_part.start()
    small_near = remote(small_ref, small_in, small_send.at[0], small_receive.at[0], partner)
    small_near.start()
    wide = [(early_ref, early_own, early_in, early_far), (late_ref, late_own, late_in, late_far)]
    near, local = {}, {}
    order = list(range(1, size)) + [0]
    for off in order:
        owner = lax.rem(me + off, size)
        for k, (grads, own, arriving, _) in enumerate(wide):
            depth = grads.shape[0] // (2 * size)

            def block(c, grads=grads, depth=depth, owner=owner):
                return grads.at[pl.ds(pl.multiple_of((owner * 2 + c) * depth, depth), depth)]

            near[off, k] = remote(
                block(1 - core), arriving.at[off], near_send.at[k, off], near_receive.at[k, off], partner
            )
            near[off, k].start()
            local[off, k] = pltpu.make_async_copy(block(core), own.at[off], own_sem.at[k, off])
            local[off, k].start()
    far = []
    for off in order:
        for k, (_, own, arriving, remote_in) in enumerate(wide):
            local[off, k].wait()
            near[off, k].wait_recv()
            add_rows(own.at[off], [own.at[off], arriving.at[off]], 16)
            if off > 0:
                copy = remote(
                    own.at[off],
                    remote_in.at[off - 1],
                    far_send.at[k, off - 1],
                    far_receive.at[k, off - 1],
                    {"dp": dp_peers[off - 1]},
                )
                copy.start()
                far.append(copy)
    small_near.wait_recv()
    small_sum[...] = small_ref[...] + small_in[...]
    small_copies = []
    for off in range(1, size):
        copy = remote(
            small_sum, small_far.at[off - 1], small_send.at[off], small_receive.at[off], {"dp": dp_peers[off - 1]}
        )
        copy.start()
        small_copies.append(copy)
    for copy in small_copies:
        copy.wait_recv()
    total = small_sum[...]
    for off in range(1, size):
        total = total + small_far[off - 1]
    small_out_ref[...] = total
    shared_own[...] = total[:, -shared:]
    for copy in far:
        copy.wait_recv()
    others = range(size - 1)
    early_terms = [early_own.at[0]] + [early_far.at[i] for i in others]
    late_terms = [late_own.at[0]] + [late_far.at[i] for i in others]
    add_rows(state_own, late_terms, 16, local_inner, 2 * STATE)
    last = []
    for off in range(1, line):
        place = {"tp": tp_peers[off - 1]}
        last.append(
            remote(state_own, state_in.at[off - 1], z_send.at[2, off - 1], z_receive.at[2, off - 1], place)
        )
        last.append(
            remote(shared_own, shared_in.at[off - 1], z_send.at[3, off - 1], z_receive.at[3, off - 1], place)
        )
    for copy in last:
        copy.start()
    add_rows(gate_ref, early_terms, 16, 0, local_inner)
    add_rows(out_ref, early_terms, 16, local_inner, local_inner)
    add_rows(inner_ref, late_terms, 16, 0, local_inner)
    add_rows(step_ref, late_terms, 16, local_inner + 2 * STATE, LANES)
    for copy in z_copies:
        copy.wait_recv()
    own_part.wait()
    add_rows(own_ref, [part_own] + [part_in.at[i] for i in range(line - 1)], 16)
    add_rows(mean_out_ref, [mean_ref] + [mean_in.at[i] for i in range(line - 1)], 8)
    for copy in last:
        copy.wait_recv()
    add_rows(state_ref, [state_own] + [state_in.at[i] for i in range(line - 1)], 16)
    total = shared_own[...]
    for i in range(line - 1):
        total = total + shared_in[i]
    small_out_ref[:, -shared:] = total
    for copy in z_copies + last + far + small_copies + [small_near] + list(near.values()):
        copy.wait_send()


def final_exchange(part, mean, early, late, small, local_inner, shared, collective_id):
    size, line = lax.axis_size("dp"), lax.axis_size("tp")
    tokens, model = part.shape
    share = model // line
    depth = early.shape[0] // (2 * size)
    anywhere = pl.BlockSpec(memory_space=pl.ANY)
    vmem = pl.BlockSpec(memory_space=pltpu.VMEM)
    dma = pltpu.SemaphoreType.DMA

    def out(*shape):
        return jax.ShapeDtypeStruct(shape, F32)

    def slots(count, like, dtype):
        return pltpu.VMEM((count, depth, like.shape[1]), dtype)

    return pl.pallas_call(
        lambda *refs: final_kernel(local_inner, shared, *refs),
        in_specs=[anywhere, vmem, anywhere, anywhere, vmem],
        out_specs=[vmem] * 8,
        out_shape=[
            out(tokens, share),
            out(*mean.shape),
            out(depth, local_inner),
            out(depth, local_inner),
            out(depth, local_inner),
            out(depth, 2 * STATE),
            out(depth, LANES),
            out(*small.shape),
        ],
        scratch_shapes=[
            pltpu.VMEM((line - 1, tokens, share), BF16),
            pltpu.VMEM((tokens, share), BF16),
            pltpu.VMEM((line - 1,) + mean.shape, F32),
            slots(size, early, BF16),
            slots(size, early, BF16),
            slots(size - 1, early, BF16),
            slots(size, late, BF16),
            slots(size, late, BF16),
            slots(size - 1, late, BF16),
            pltpu.VMEM(small.shape, F32),
            pltpu.VMEM(small.shape, F32),
            pltpu.VMEM((size - 1,) + small.shape, F32),
            pltpu.VMEM((8, shared), F32),
            pltpu.VMEM((line - 1, 8, shared), F32),
            pltpu.VMEM((depth, 2 * STATE), BF16),
            pltpu.VMEM((line - 1, depth, 2 * STATE), BF16),
            dma((4, line - 1)),
            dma((4, line - 1)),
            dma((2, size)),
            dma((2, size)),
            dma((2, size - 1)),
            dma((2, size - 1)),
            dma((3, size)),
            dma((size,)),
            dma((size,)),
        ],
        compiler_params=pltpu.CompilerParams(
            collective_id=collective_id, has_side_effects=True, vmem_limit_bytes=VMEM_LIMIT
        ),
        name="final_exchange",
    )(part, mean, early, late, small)


def row(v, width):
    return jnp.pad(v, (0, width - v.shape[0]))[None, :]


def on_device(
    block_input_activations,
    sequence_first_token,
    norm_gain,
    gate_proj,
    input_proj,
    step_proj,
    state_proj,
    conv_inner_weight,
    conv_inner_bias,
    conv_state_weight,
    conv_state_bias,
    step_bias,
    decay_log,
    skip_weight,
    gate_gain,
    out_proj,
    output_cotangent,
):
    everyone = ("dp", "ctx")
    x = block_input_activations
    local_inner = gate_proj.shape[1]
    heads = step_bias.shape[0]
    tokens = x.shape[0]
    main = local_inner + 2 * STATE
    width = KCONV - 1
    step_pad = jnp.pad(step_proj, ((0, 0), (0, LANES - heads)))
    flags = sequence_first_token.astype(F32)
    late_full, early_full, halo_x, other_flags = gather(
        [
            jnp.concatenate([input_proj, state_proj, step_pad], axis=1),
            jnp.concatenate([gate_proj, out_proj.T], axis=1),
        ],
        x,
        flags.reshape(-1, LANES),
        4,
    )
    going_on = 1.0 - jnp.concatenate([other_flags.reshape(-1)[-width:], flags])
    lag1 = going_on[width:]
    lag2 = lag1 * going_on[width - 1 : width - 1 + tokens]
    lag3 = lag2 * going_on[width - 2 : width - 2 + tokens]
    none = jnp.zeros_like(flags)
    marks = jnp.stack([flags, lag1, lag2, lag3, none, none, none, none], axis=1)
    gain = norm_gain[None, :]
    taps = jnp.concatenate([conv_inner_weight, conv_state_weight], axis=1)
    bias = jnp.concatenate([conv_inner_bias, conv_state_bias])[None, :]
    decay_row = row(decay_log, LANES)
    skip_row = jnp.repeat(skip_weight, HEADDIM)[None, :]
    gated_gain = gate_gain[None, :]
    (
        normed,
        rows,
        conv,
        mixed_local,
        cum,
        raw,
        passing,
        out_map,
        states,
        products,
        final_state,
        halo_rows,
    ) = front(
        x, marks, halo_x, gain, late_full, taps, bias, row(step_bias, LANES), decay_row, skip_row, heads
    )
    carried = passed_along(final_state, 1)
    gate, mixed, back, sums = gate_pass(
        normed, output_cotangent, mixed_local, passing, out_map, carried, early_full, gated_gain, heads
    )
    (sums,) = exchange([(sums.reshape(-1, LANES), ("tp",), None)], 1)
    sums = sums.reshape(8, tokens)
    gated_normed, grad_mixed, grad_gate, branch_part, through, grad_gain_gate = middle_pass(
        gate, mixed, back, sums, passing, out_map, early_full, gated_gain, heads
    )
    following = passed_along(through, -1)
    share = MODEL_WIDTH // lax.axis_size("tp")
    column = lax.axis_index("tp") * share
    own_hidden = lax.dynamic_slice_in_dim(x, column, share, 1).astype(F32)
    branch = lax.psum_scatter(branch_part, "tp", scatter_dimension=1, tiled=True)
    block_output = (own_hidden + branch.astype(F32)).astype(BF16)
    grad_out = dot_tn(output_cotangent, gated_normed).astype(BF16)
    grad_gate_weight = dot_tn(normed, grad_gate).astype(BF16)
    early_weight = jnp.concatenate([grad_gate_weight, grad_out], axis=1)
    late, tail, halo_grad, conv_sums, head_sums = back_pass(
        grad_mixed,
        conv,
        rows,
        halo_rows,
        marks,
        raw,
        cum,
        states,
        products,
        carried,
        following,
        taps,
        decay_row,
        skip_row,
        heads,
    )
    returned = passed_along(halo_grad, -1)
    tail = (tail + jnp.pad(returned, ((8, 0), (0, 0)))).astype(BF16)
    late = lax.dynamic_update_slice(late, tail, (tokens - 16, 0))
    tensor_part, mean_sum, gain_sums = input_pass(x, grad_gate, late, early_full, late_full, gain)
    late_weight = dot_tn(normed, late).astype(BF16)
    shared = 2 * STATE + MODEL_WIDTH
    small = jnp.concatenate(
        [conv_sums[:, :local_inner], grad_gain_gate, head_sums, conv_sums[:, local_inner:], gain_sums], axis=1
    )
    own_grad, mean_sum, gate_grad, out_grad, inner_grad, state_grad, step_grad, small = final_exchange(
        tensor_part, mean_sum, early_weight, late_weight, small, local_inner, shared, 2
    )
    mean_term = mean_sum[0][:, None] / MODEL_WIDTH
    hidden = x.astype(F32)
    inv_rms = lax.rsqrt(jnp.mean(hidden * hidden, axis=1, keepdims=True) + EPSILON)
    own_cotangent = lax.dynamic_slice_in_dim(output_cotangent, column, share, 1).astype(F32)
    own_gain = lax.dynamic_slice_in_dim(norm_gain, column, share, 0)
    input_grad = (
        own_cotangent + inv_rms * own_grad * own_gain[None, :] - own_hidden * inv_rms**3 * mean_term
    )
    inner_sums = small[:, :local_inner]
    head_sums = small[:, 2 * local_inner : 2 * local_inner + heads]
    state_sums = small[:, 2 * local_inner + LANES : 2 * local_inner + LANES + 2 * STATE]
    gain_grad = lax.dynamic_slice_in_dim(small[0], small.shape[1] - MODEL_WIDTH + column, share, 0)
    return (
        block_output,
        input_grad,
        gain_grad,
        gate_grad,
        inner_grad,
        step_grad[:, :heads],
        state_grad,
        inner_sums[:KCONV],
        inner_sums[KCONV],
        state_sums[:KCONV],
        state_sums[KCONV],
        head_sums[0],
        head_sums[1],
        inner_sums[5].reshape(heads, HEADDIM).sum(axis=1),
        small[0, local_inner : 2 * local_inner],
        out_grad.T,
    )


def solution(mesh):
    return jax.shard_map(
        on_device,
        mesh=mesh,
        in_specs=(
            P(("dp", "ctx"), None),
            P(("dp", "ctx")),
            P(),
            P(("dp", "ctx"), "tp"),
            P(("dp", "ctx"), "tp"),
            P(("dp", "ctx"), "tp"),
            P(("dp", "ctx"), None),
            P(None, "tp"),
            P("tp"),
            P(),
            P(),
            P("tp"),
            P("tp"),
            P("tp"),
            P("tp"),
            P("tp", ("dp", "ctx")),
            P(("dp", "ctx"), None),
        ),
        out_specs=(
            P(("dp", "ctx"), "tp"),
            P(("dp", "ctx"), "tp"),
            P("tp"),
            P(("dp", "ctx"), "tp"),
            P(("dp", "ctx"), "tp"),
            P(("dp", "ctx"), "tp"),
            P(("dp", "ctx"), None),
            P(None, "tp"),
            P("tp"),
            P(),
            P(),
            P("tp"),
            P("tp"),
            P("tp"),
            P("tp"),
            P("tp", ("dp", "ctx")),
        ),
        check_vma=False,
    )
```

```python
import jax
import jax.numpy as jnp
from jax import lax
from jax.experimental import pallas as pl
from jax.experimental.pallas import tpu as pltpu
from jax.sharding import PartitionSpec as P

MODEL_WIDTH = 1024
HEADDIM = 64
STATE = 128
KCONV = 4
SPAN = 256
INNER = 2048


EPSILON = 1e-05
HIGHEST = lax.Precision.HIGHEST


def passed_along(block, distance):
    devices = range(lax.axis_size("ctx"))
    route = [(i - distance, i) for i in devices if i - distance in devices]
    return lax.ppermute(block, "ctx", route)


LANES = 128
VMEM_LIMIT = 60 * 1024 * 1024
BF16 = jnp.bfloat16
F32 = jnp.float32
BLOCKED = -1e30


def dot_nn(a, b):
    return jnp.dot(a, b, preferred_element_type=F32)


def dot_nt(a, b):
    return lax.dot_general(a, b, (((1,), (1,)), ((), ())), preferred_element_type=F32)


def dot_tn(a, b):
    return lax.dot_general(a, b, (((0,), (0,)), ((), ())), preferred_element_type=F32)


def iota(shape, dim):
    return lax.broadcasted_iota(jnp.int32, shape, dim)


def high_low(a):
    high = a.astype(BF16)
    return high, (a - high.astype(F32)).astype(BF16)


def widen(a, heads, width):
    lane = iota(a.shape, 1)
    high = a.astype(BF16).astype(F32)
    low = pltpu.roll(a - high, heads, 1)
    packed = jnp.where(lane < heads, high, jnp.where(lane < 2 * heads, low, 0.0)).astype(BF16)
    row, column = iota((LANES, width), 0), iota((LANES, width), 1)
    place = jnp.where(row < heads, row, row - heads)
    return dot_nn(packed, (column // HEADDIM == place).astype(BF16))


def per_head_sum(a, heads):
    high, low = high_low(a)
    row, column = iota((LANES, a.shape[1]), 0), iota((LANES, a.shape[1]), 1)
    pick = (column // HEADDIM == row).astype(BF16)
    return dot_nt(high, pick) + dot_nt(low, pick)


def row_sum(a):
    folded = a[:, :LANES]
    for i in range(1, a.shape[1] // LANES):
        folded = folded + a[:, i * LANES : (i + 1) * LANES]
    return jnp.sum(folded.T, axis=0, keepdims=True)


def rows_of_heads(column, heads):
    return jnp.concatenate(
        [jnp.broadcast_to(column[h : h + 1, :], (HEADDIM, LANES)) for h in range(heads)], axis=0
    )


def sigmoid(v):
    return 0.5 * jnp.tanh(0.5 * v) + 0.5


def normalise(x, gain):
    hidden = x.astype(F32)
    inv = lax.rsqrt(jnp.mean(hidden * hidden, axis=1, keepdims=True) + EPSILON)
    return (hidden * inv * gain).astype(BF16)


def whole(shape):
    return pl.BlockSpec(shape, lambda i: (0,) * len(shape))


def columns_of(array, width, block):
    return pl.BlockSpec((array.shape[0], width), lambda i: (0, block))


def front_kernel(
    heads,
    x_ref,
    marks_ref,
    halo_x_ref,
    flags_ref,
    gain_ref,
    weight_ref,
    taps_ref,
    bias_ref,
    step_bias_ref,
    decay_ref,
    skip_ref,
    normed_ref,
    rows_ref,
    conv_ref,
    mixed_ref,
    cum_ref,
    raw_ref,
    passing_ref,
    out_map_ref,
    states_ref,
    products_ref,
    final_ref,
    halo_rows_ref,
    state,
    product,
    before,
):
    step = pl.program_id(0)
    channels = heads * HEADDIM
    main = channels + 2 * STATE
    gain = gain_ref[...]

    @pl.when(step == 0)
    def _():
        state[...] = jnp.zeros_like(state)
        product[...] = jnp.ones_like(product)
        halo = dot_nn(normalise(halo_x_ref[...], gain), weight_ref[:, :main]).astype(BF16)
        halo_rows_ref[...] = halo
        before[...] = halo.astype(F32)[8:16]

    normed = normalise(x_ref[...], gain)
    normed_ref[...] = normed
    projected = dot_nn(normed, weight_ref[...])
    rows = projected[:, :main].astype(BF16)
    rows_ref[...] = rows
    rows = rows.astype(F32)
    raw = projected[:, main:] + step_bias_ref[...]
    extended = jnp.concatenate([before[...], rows], axis=0)
    before[...] = rows[SPAN - 8 :]
    taps = taps_ref[...]
    conv = bias_ref[...] + taps[0:1] * rows
    lane = iota((SPAN, LANES), 1)
    boundary = jnp.where(step == 0, flags_ref[flags_ref.shape[0] - 1 :, LANES - KCONV :], 0.0)
    reach = 1.0 - boundary
    at_first, at_second = iota((SPAN, 1), 0) == 0, iota((SPAN, 1), 0) == 1
    nearest, second = reach[:, KCONV - 1 :], reach[:, KCONV - 2 : KCONV - 1]
    edges = [
        None,
        None,
        jnp.where(at_first, nearest, 1.0),
        jnp.where(at_first, nearest * second, jnp.where(at_second, nearest, 1.0)),
    ]
    for lag in range(1, KCONV):
        valid = marks_ref[:, lag : lag + 1]
        if edges[lag] is not None:
            valid = valid * edges[lag]
        raw = jnp.where(lane == heads + lag, valid, raw)
        conv = conv + (taps[lag : lag + 1] * extended[8 - lag : 8 - lag + SPAN]) * valid
    raw_ref[...] = raw
    conv_ref[...] = conv
    act = conv * sigmoid(conv)
    values = act[:, :channels]
    map_in = act[:, channels : channels + STATE].astype(BF16)
    map_out = act[:, channels + STATE :].astype(BF16)
    out_map_ref[...] = map_out

    step_size = jnp.maximum(raw, 0.0) + jnp.log1p(jnp.exp(-jnp.abs(raw)))
    log_decay = jnp.where(lane < heads, step_size * (-jnp.exp(decay_ref[...])), 0.0)
    series = jnp.where(lane == heads, marks_ref[:, 0:1], log_decay)
    t, s = iota((SPAN, SPAN), 0), iota((SPAN, SPAN), 1)
    cum = jnp.dot((t >= s).astype(F32), series, precision=HIGHEST, preferred_element_type=F32)
    cum_ref[...] = cum
    cum_rows = cum.T
    segment, segment_row = cum[:, heads : heads + 1], cum_rows[heads : heads + 1, :]
    blocked = jnp.where((segment == segment_row) & (t >= s), 0.0, BLOCKED)
    passing = jnp.where(segment == 0.0, jnp.exp(cum), 0.0)
    product_now = product[...]
    passing_ref[...] = passing * product_now[0:1]
    products_ref[0] = product_now
    product[...] = product_now * passing[SPAN - 1 : SPAN]
    to_end = jnp.where(
        segment == cum[SPAN - 1 : SPAN, heads : heads + 1], jnp.exp(cum[SPAN - 1 : SPAN] - cum), 0.0
    )
    stepped = values * widen(step_size, heads, channels)
    state_now = state[...]
    states_ref[0] = state_now
    scores = dot_nt(map_out, map_in)
    through = widen(passing, heads, channels) * dot_nt(map_out, state_now.astype(BF16))
    half = iota((SPAN, LANES), 1) < HEADDIM
    for pair in range(heads // 2):
        at = slice(pair * LANES, (pair + 1) * LANES)
        both = stepped[:, at]
        total = through[:, at] + skip_ref[:, at] * values[:, at]
        for side in range(2):
            h = 2 * pair + side
            spread = cum[:, h : h + 1] - cum_rows[h : h + 1, :]
            mixing = (jnp.exp(spread + blocked) * scores).astype(BF16)
            own = jnp.where(half if side == 0 else ~half, both, 0.0).astype(BF16)
            total = total + dot_nn(mixing, own)
        mixed_ref[:, at] = total
    ending = (stepped * widen(to_end, heads, channels)).astype(BF16)
    fresh = dot_tn(ending, map_in)
    kept = jnp.where(segment_row[:, SPAN - 1 :] == 0.0, jnp.exp(cum_rows[:, SPAN - 1 :]), 0.0)
    state_next = rows_of_heads(kept, heads) * state_now + fresh
    state[...] = state_next
    final_ref[...] = state_next


def front(x, marks, halo_x, flags, gain, weight, taps, bias, step_bias, decay, skip, heads):
    tokens = x.shape[0]
    channels = heads * HEADDIM
    main = channels + 2 * STATE
    spans = tokens // SPAN

    def chunk(width):
        return pl.BlockSpec((SPAN, width), lambda i: (i, 0))

    def out(shape, dtype):
        return jax.ShapeDtypeStruct(shape, dtype)

    return pl.pallas_call(
        lambda *refs: front_kernel(heads, *refs),
        grid=(spans,),
        in_specs=[
            chunk(MODEL_WIDTH),
            chunk(8),
            whole(halo_x.shape),
            whole(flags.shape),
            whole(gain.shape),
            whole(weight.shape),
            whole(taps.shape),
            whole(bias.shape),
            whole(step_bias.shape),
            whole(decay.shape),
            whole(skip.shape),
        ],
        out_specs=[
            chunk(MODEL_WIDTH),
            chunk(main),
            chunk(main),
            chunk(channels),
            chunk(LANES),
            chunk(LANES),
            chunk(LANES),
            chunk(STATE),
            pl.BlockSpec((1, channels, STATE), lambda i: (i, 0, 0)),
            pl.BlockSpec((1, 8, LANES), lambda i: (i, 0, 0)),
            whole((channels, STATE)),
            whole((16, main)),
        ],
        out_shape=[
            out((tokens, MODEL_WIDTH), BF16),
            out((tokens, main), BF16),
            out((tokens, main), F32),
            out((tokens, channels), F32),
            out((tokens, LANES), F32),
            out((tokens, LANES), F32),
            out((tokens, LANES), F32),
            out((tokens, STATE), BF16),
            out((spans, channels, STATE), F32),
            out((spans, 8, LANES), F32),
            out((channels, STATE), F32),
            out((16, main), BF16),
        ],
        scratch_shapes=[
            pltpu.VMEM((channels, STATE), F32),
            pltpu.VMEM((8, LANES), F32),
            pltpu.VMEM((8, main), F32),
        ],
        compiler_params=pltpu.CompilerParams(vmem_limit_bytes=VMEM_LIMIT),
        cost_estimate=pl.CostEstimate(
            flops=2 * tokens * (MODEL_WIDTH * weight.shape[1] + 4 * SPAN * channels),
            bytes_accessed=18 * 2**20,
            transcendentals=tokens * SPAN * heads,
        ),
        name="scan_front",
    )(x, marks, halo_x, flags, gain, weight, taps, bias, step_bias, decay, skip)


def gate_kernel(
    heads,
    normed_ref,
    cot_ref,
    local_ref,
    passing_ref,
    out_map_ref,
    carried_ref,
    weight_ref,
    out_t_ref,
    gain_ref,
    gate_ref,
    mixed_ref,
    back_ref,
    sums_ref,
    branch_ref,
):
    channels = heads * HEADDIM
    gate = dot_nn(normed_ref[...], weight_ref[...])
    gate_ref[...] = gate
    back = dot_nn(cot_ref[...], out_t_ref[...])
    back_ref[...] = back
    from_carried = dot_nt(out_map_ref[...], carried_ref[...].astype(BF16))
    mixed = local_ref[...] + widen(passing_ref[...], heads, channels) * from_carried
    mixed_ref[...] = mixed
    gated = mixed * (gate * sigmoid(gate))
    branch_ref[...] = dot_nt((gated * gain_ref[...]).astype(BF16), out_t_ref[...]).astype(BF16)
    square, cross = row_sum(gated * gated), row_sum(gated * (back * gain_ref[...]))
    sums_ref[...] = jnp.where(iota((8, SPAN), 0) < 4, square, cross)


def gate_pass(normed, cot, local, passing, out_map, carried, early_weight, gain, heads):
    tokens = normed.shape[0]
    channels = heads * HEADDIM

    def chunk(width):
        return pl.BlockSpec((SPAN, width), lambda i: (i, 0))

    return pl.pallas_call(
        lambda *refs: gate_kernel(heads, *refs),
        grid=(tokens // SPAN,),
        in_specs=[
            chunk(MODEL_WIDTH),
            chunk(MODEL_WIDTH),
            chunk(channels),
            chunk(LANES),
            chunk(STATE),
            whole(carried.shape),
            columns_of(early_weight, channels, 0),
            columns_of(early_weight, channels, 1),
            whole(gain.shape),
        ],
        out_specs=[
            chunk(channels),
            chunk(channels),
            chunk(channels),
            pl.BlockSpec((8, SPAN), lambda i: (0, i)),
            chunk(MODEL_WIDTH),
        ],
        out_shape=[jax.ShapeDtypeStruct((tokens, channels), F32)] * 3
        + [jax.ShapeDtypeStruct((8, tokens), F32), jax.ShapeDtypeStruct((tokens, MODEL_WIDTH), BF16)],
        compiler_params=pltpu.CompilerParams(vmem_limit_bytes=VMEM_LIMIT),
        cost_estimate=pl.CostEstimate(
            flops=6 * tokens * MODEL_WIDTH * channels,
            bytes_accessed=16 * 2**20,
            transcendentals=tokens * channels,
        ),
        name="gate_pass",
    )(normed, cot, local, passing, out_map, carried, early_weight, early_weight, gain)


def middle_kernel(
    heads,
    gate_ref,
    mixed_ref,
    back_ref,
    sums_ref,
    passing_ref,
    out_map_ref,
    gain_ref,
    gated_ref,
    grad_mixed_ref,
    grad_gate_ref,
    through_ref,
    grad_gain_ref,
):
    channels = heads * HEADDIM
    step = pl.program_id(0)
    rows = sums_ref[...]
    square = jnp.broadcast_to(rows[0:1], (LANES, SPAN)).T[:, 0:1]
    cross = jnp.broadcast_to(rows[4:5], (LANES, SPAN)).T[:, 0:1]
    inv = lax.rsqrt(square / INNER + EPSILON)
    gate, mixed, back, gain = gate_ref[...], mixed_ref[...], back_ref[...], gain_ref[...]
    sig = sigmoid(gate)
    gate_silu = gate * sig
    gated = mixed * gate_silu
    scaled = back * gain
    normal = gated * inv
    gated_ref[...] = (normal * gain).astype(BF16)
    grad_gated = inv * scaled - normal * (inv * inv * (cross / INNER))
    grad_mixed = grad_gated * gate_silu
    grad_mixed_ref[...] = grad_mixed
    grad_gate = grad_gated * mixed * sig * (1.0 + gate * (1.0 - sig))
    grad_gate_ref[...] = grad_gate.astype(BF16)
    reaching = (grad_mixed * widen(passing_ref[...], heads, channels)).astype(BF16)
    through = dot_tn(reaching, out_map_ref[...])
    gain_part = jnp.broadcast_to(jnp.sum(back * normal, axis=0, keepdims=True), (8, channels))

    @pl.when(step == 0)
    def _():
        through_ref[...] = through
        grad_gain_ref[...] = gain_part

    @pl.when(step > 0)
    def _():
        through_ref[...] += through
        grad_gain_ref[...] += gain_part


def middle_pass(gate, mixed, back, sums, passing, out_map, gain, heads):
    tokens = gate.shape[0]
    channels = heads * HEADDIM

    def chunk(width):
        return pl.BlockSpec((SPAN, width), lambda i: (i, 0))

    return pl.pallas_call(
        lambda *refs: middle_kernel(heads, *refs),
        grid=(tokens // SPAN,),
        in_specs=[
            chunk(channels),
            chunk(channels),
            chunk(channels),
            pl.BlockSpec((8, SPAN), lambda i: (0, i)),
            chunk(LANES),
            chunk(STATE),
            whole(gain.shape),
        ],
        out_specs=[
            chunk(channels),
            chunk(channels),
            chunk(channels),
            whole((channels, STATE)),
            whole((8, channels)),
        ],
        out_shape=[
            jax.ShapeDtypeStruct((tokens, channels), BF16),
            jax.ShapeDtypeStruct((tokens, channels), F32),
            jax.ShapeDtypeStruct((tokens, channels), BF16),
            jax.ShapeDtypeStruct((channels, STATE), F32),
            jax.ShapeDtypeStruct((8, channels), F32),
        ],
        compiler_params=pltpu.CompilerParams(vmem_limit_bytes=VMEM_LIMIT),
        cost_estimate=pl.CostEstimate(
            flops=2 * tokens * STATE * channels,
            bytes_accessed=12 * 2**20,
            transcendentals=tokens * channels,
        ),
        name="middle_pass",
    )(gate, mixed, back, sums, passing, out_map, gain)


def back_kernel(
    heads,
    grad_ref,
    conv_ref,
    rows_ref,
    earlier_ref,
    halo_ref,
    raw_ref,
    cum_ref,
    states_ref,
    products_ref,
    carried_ref,
    next_ref,
    taps_ref,
    decay_ref,
    skip_ref,
    late_ref,
    tail_ref,
    halo_grad_ref,
    sums_ref,
    head_sums_ref,
    flowing,
    after,
):
    step = pl.program_id(0)
    spans = pl.num_programs(0)
    channels = heads * HEADDIM
    main = channels + 2 * STATE

    @pl.when(step == 0)
    def _():
        flowing[...] = next_ref[...]
        after[...] = jnp.zeros_like(after)
        sums_ref[...] = jnp.zeros_like(sums_ref)
        head_sums_ref[...] = jnp.zeros_like(head_sums_ref)

    conv = conv_ref[...]
    sig = sigmoid(conv)
    act = conv * sig
    slope = sig * (1.0 + conv * (1.0 - sig))
    values = act[:, :channels]
    map_in = act[:, channels : channels + STATE].astype(BF16)
    map_out = act[:, channels + STATE :].astype(BF16)
    raw = raw_ref[...]
    step_size = jnp.maximum(raw, 0.0) + jnp.log1p(jnp.exp(-jnp.abs(raw)))
    cum = cum_ref[...]
    cum_rows = cum.T
    segment, segment_row = cum[:, heads : heads + 1], cum_rows[heads : heads + 1, :]
    s, t = iota((SPAN, SPAN), 0), iota((SPAN, SPAN), 1)
    blocked = jnp.where((segment == segment_row) & (t >= s), 0.0, BLOCKED)
    passing = jnp.where(segment == 0.0, jnp.exp(cum), 0.0)
    to_end = jnp.where(
        segment == cum[SPAN - 1 : SPAN, heads : heads + 1], jnp.exp(cum[SPAN - 1 : SPAN] - cum), 0.0
    )
    kept = jnp.where(segment_row[:, SPAN - 1 :] == 0.0, jnp.exp(cum_rows[:, SPAN - 1 :]), 0.0)
    product_column = jnp.broadcast_to(products_ref[0][0:1], (LANES, LANES)).T
    state = states_ref[0] + rows_of_heads(product_column[:, 0:1], heads) * carried_ref[...]
    state_bf = state.astype(BF16)
    flow = flowing[...]
    flow_bf = flow.astype(BF16)
    grad = grad_ref[...]
    step_wide = widen(step_size, heads, channels)
    end_wide = widen(to_end, heads, channels)
    stepped = values * step_wide
    stepped_bf = stepped.astype(BF16)
    grad_bf = grad.astype(BF16)
    reaching = grad * widen(passing, heads, channels)
    reaching_bf = reaching.astype(BF16)
    ending = stepped * end_wide
    ending_bf = ending.astype(BF16)
    from_state = dot_nt(map_out, state_bf)
    from_flow = dot_nt(map_in, flow_bf)
    scores = dot_nt(map_in, map_out)
    half = iota((SPAN, LANES), 1) < HEADDIM
    zero = jnp.zeros((SPAN, LANES), BF16)
    lane = iota((SPAN, LANES), 1)
    grad_scores = jnp.zeros((SPAN, SPAN), F32)
    out_sums = jnp.zeros((SPAN, LANES), F32)
    in_sums = []
    grad_stepped = []
    for pair in range(heads // 2):
        at = slice(pair * LANES, (pair + 1) * LANES)
        total = end_wide[:, at] * from_flow[:, at]
        for side in range(2):
            h = 2 * pair + side
            own = half if side == 0 else ~half
            decay = jnp.exp((cum_rows[h : h + 1, :] - cum[:, h : h + 1]) + blocked)
            own_grad = jnp.where(own, grad_bf[:, at], zero)
            total = total + dot_nn((decay * scores).astype(BF16), own_grad)
            flowed = decay * dot_nt(stepped_bf[:, at], own_grad)
            grad_scores = grad_scores + flowed
            weighed = flowed * scores
            in_sums.append(jnp.sum(weighed, axis=0, keepdims=True))
            out_sums = jnp.where(lane == h, jnp.sum(weighed, axis=1, keepdims=True), out_sums)
        grad_stepped.append(total)
    grad_stepped = jnp.concatenate(grad_stepped, axis=1)
    grad_scores = grad_scores.astype(BF16)
    grad_out_map = dot_tn(grad_scores, map_in) + dot_nn(reaching_bf, state_bf)
    grad_in_map = dot_nn(grad_scores, map_out) + dot_nn(ending_bf, flow_bf)
    ended = per_head_sum(ending * from_flow, heads)
    row, column = iota((LANES, channels), 0), iota((LANES, channels), 1)
    pick = (column // HEADDIM == row).astype(BF16)
    high, low = high_low(flow * state)
    at_last = kept * jnp.sum(dot_nn(pick, high) + dot_nn(pick, low), axis=1, keepdims=True)
    in_rows = jnp.concatenate(
        in_sums + [jnp.zeros((LANES - heads, SPAN), F32)], axis=0
    ) + jnp.where(iota((LANES, SPAN), 1) == SPAN - 1, at_last, 0.0)
    last = iota((SPAN, LANES), 0) == SPAN - 1
    grad_cum = (
        in_rows.T
        - out_sums
        + per_head_sum(reaching * from_state, heads)
        - ended
        + jnp.where(last, jnp.sum(ended, axis=0, keepdims=True), 0.0)
    )
    grad_log = jnp.dot((t >= s).astype(F32), grad_cum, precision=HIGHEST, preferred_element_type=F32)
    rate = -jnp.exp(decay_ref[...])
    grad_step = per_head_sum(grad_stepped * values, heads) + grad_log * rate
    grad_raw = jnp.where(lane < heads, grad_step * sigmoid(raw), 0.0)
    late_ref[:, main:] = grad_raw.astype(BF16)
    head_sums_ref[0:1] += jnp.sum(grad_raw, axis=0, keepdims=True)
    head_sums_ref[1:2] += jnp.sum(grad_log * step_size, axis=0, keepdims=True) * rate
    flowing[...] = rows_of_heads(kept, heads) * flow + dot_tn(reaching_bf, map_out)
    grad_values = grad_stepped * step_wide + skip_ref[...] * grad
    grad_act = jnp.concatenate([grad_values, grad_in_map, grad_out_map], axis=1)
    grad_conv = grad_act * slope
    sums_ref[5:6, :channels] += jnp.sum(grad * values, axis=0, keepdims=True)
    sums_ref[4:5] += jnp.sum(grad_conv, axis=0, keepdims=True)
    rows = rows_ref[...].astype(F32)
    first = step == spans - 1
    previous = jnp.where(first, halo_ref[...].astype(F32), earlier_ref[...].astype(F32))[8:16]
    extended = jnp.concatenate([previous, rows], axis=0)
    sums_ref[0:1] += jnp.sum(grad_conv * rows, axis=0, keepdims=True)
    taps = taps_ref[...]
    grad_rows = taps[0:1] * grad_conv
    halo_grad = jnp.zeros((8, main), F32)
    for lag in range(1, KCONV):
        valid = grad_conv * raw[:, heads + lag : heads + lag + 1]
        sums_ref[lag : lag + 1] += jnp.sum(
            valid * extended[8 - lag : 8 - lag + SPAN], axis=0, keepdims=True
        )
        tapped = taps[lag : lag + 1] * valid
        joined = jnp.concatenate([tapped, after[lag - 1]], axis=0)
        grad_rows = grad_rows + joined[lag : lag + SPAN]
        head = tapped[0:8]
        after[lag - 1] = head
        halo_grad = halo_grad + jnp.concatenate([jnp.zeros((8, main), F32), head], axis=0)[lag : lag + 8]
    late_ref[:, :main] = grad_rows.astype(BF16)
    halo_grad_ref[...] = halo_grad

    @pl.when(step == 0)
    def _():
        tail_ref[...] = grad_rows[SPAN - 16 :]


def back_pass(
    grad, conv, rows, halo, raw, cum, states, products, carried, following, taps, decay, skip, heads
):
    tokens = grad.shape[0]
    channels = heads * HEADDIM
    main = channels + 2 * STATE
    spans = tokens // SPAN

    def chunk(width):
        return pl.BlockSpec((SPAN, width), lambda i: (spans - 1 - i, 0))

    return pl.pallas_call(
        lambda *refs: back_kernel(heads, *refs),
        grid=(spans,),
        in_specs=[
            chunk(channels),
            chunk(main),
            chunk(main),
            pl.BlockSpec((16, main), lambda i: (jnp.maximum((spans - 1 - i) * (SPAN // 16) - 1, 0), 0)),
            whole(halo.shape),
            chunk(LANES),
            chunk(LANES),
            pl.BlockSpec((1, channels, STATE), lambda i: (spans - 1 - i, 0, 0)),
            pl.BlockSpec((1, 8, LANES), lambda i: (spans - 1 - i, 0, 0)),
            whole(carried.shape),
            whole(following.shape),
            whole(taps.shape),
            whole(decay.shape),
            whole(skip.shape),
        ],
        out_specs=[
            chunk(main + LANES),
            whole((16, main)),
            whole((8, main)),
            whole((8, main)),
            whole((8, LANES)),
        ],
        out_shape=[
            jax.ShapeDtypeStruct((tokens, main + LANES), BF16),
            jax.ShapeDtypeStruct((16, main), F32),
            jax.ShapeDtypeStruct((8, main), F32),
            jax.ShapeDtypeStruct((8, main), F32),
            jax.ShapeDtypeStruct((8, LANES), F32),
        ],
        scratch_shapes=[
            pltpu.VMEM((channels, STATE), F32),
            pltpu.VMEM((KCONV - 1, 8, main), F32),
        ],
        compiler_params=pltpu.CompilerParams(vmem_limit_bytes=VMEM_LIMIT),
        cost_estimate=pl.CostEstimate(
            flops=2 * tokens * 12 * SPAN * channels,
            bytes_accessed=12 * 2**20,
            transcendentals=tokens * SPAN * heads,
        ),
        name="scan_back",
    )(
        grad, conv, rows, rows, halo, raw, cum, states, products, carried, following, taps, decay, skip
    )


def input_kernel(
    x_ref,
    grad_gate_ref,
    late_ref,
    tail_ref,
    returned_ref,
    gate_weight_ref,
    late_weight_ref,
    gain_ref,
    part_ref,
    sums_ref,
    grad_gain_ref,
    whole_late_ref,
):
    step = pl.program_id(0)
    whole_late_ref[...] = late_ref[...]

    @pl.when(step == pl.num_programs(0) - 1)
    def _():
        main = tail_ref.shape[1]
        tail = tail_ref[...] + jnp.concatenate([jnp.zeros((8, main), F32), returned_ref[...]], axis=0)
        whole_late_ref[SPAN - 16 :, :main] = tail.astype(BF16)

    part = dot_nt(grad_gate_ref[...], gate_weight_ref[...])
    part = part + dot_nt(whole_late_ref[...], late_weight_ref[...])
    part_ref[...] = part.astype(BF16)
    hidden = x_ref[...].astype(F32)
    inv = lax.rsqrt(jnp.mean(hidden * hidden, axis=1, keepdims=True) + EPSILON)
    term = part * hidden
    sums_ref[...] = jnp.broadcast_to(row_sum(term * gain_ref[...]), (8, SPAN))
    gain_part = jnp.sum(term * inv, axis=0, keepdims=True)

    @pl.when(step == 0)
    def _():
        grad_gain_ref[...] = jnp.zeros_like(grad_gain_ref)

    grad_gain_ref[0:1] += gain_part


def input_pass(x, grad_gate, late, tail, returned, early_weight, late_weight, gain):
    tokens = x.shape[0]
    channels = grad_gate.shape[1]

    def chunk(width):
        return pl.BlockSpec((SPAN, width), lambda i: (i, 0))

    return pl.pallas_call(
        input_kernel,
        grid=(tokens // SPAN,),
        in_specs=[
            chunk(MODEL_WIDTH),
            chunk(channels),
            chunk(late.shape[1]),
            whole(tail.shape),
            whole(returned.shape),
            columns_of(early_weight, channels, 0),
            whole(late_weight.shape),
            whole(gain.shape),
        ],
        out_specs=[
            chunk(MODEL_WIDTH),
            pl.BlockSpec((8, SPAN), lambda i: (0, i)),
            whole((8, MODEL_WIDTH)),
            chunk(late.shape[1]),
        ],
        out_shape=[
            jax.ShapeDtypeStruct((tokens, MODEL_WIDTH), BF16),
            jax.ShapeDtypeStruct((8, tokens), F32),
            jax.ShapeDtypeStruct((8, MODEL_WIDTH), F32),
            jax.ShapeDtypeStruct(late.shape, BF16),
        ],
        compiler_params=pltpu.CompilerParams(vmem_limit_bytes=VMEM_LIMIT),
        cost_estimate=pl.CostEstimate(
            flops=2 * tokens * MODEL_WIDTH * (channels + late.shape[1]),
            bytes_accessed=12 * 2**20,
            transcendentals=0,
        ),
        name="input_pass",
    )(x, grad_gate, late, tail, returned, early_weight, late_weight, gain)


def spread_kernel(heads, out_ref, step_ref, gate_ref, inner_ref, state_ref, small_ref, *outs):
    channels = heads * HEADDIM
    out_out, step_out, gate_out, inner_out, state_out = outs[:5]
    taps_out, bias_out, state_taps_out, state_bias_out, step_bias_out, decay_out, skip_out, gain_out = outs[5:]
    out_out[...] = out_ref[...].T
    step_out[...] = step_ref[:, :heads]
    gate_out[...] = gate_ref[...]
    inner_out[...] = inner_ref[...]
    state_out[...] = state_ref[...]
    heads_at = 2 * channels
    state_at = heads_at + LANES
    taps_out[...] = small_ref[:KCONV, :channels]
    bias_out[...] = small_ref[KCONV : KCONV + 1, :channels]
    state_taps_out[...] = small_ref[:KCONV, state_at : state_at + 2 * STATE]
    state_bias_out[...] = small_ref[KCONV : KCONV + 1, state_at : state_at + 2 * STATE]
    step_bias_out[...] = small_ref[0:1, heads_at : heads_at + LANES][:, :heads]
    decay_out[...] = small_ref[1:2, heads_at : heads_at + LANES][:, :heads]
    skip_out[...] = per_head_sum(small_ref[:, :channels], heads)[5:6, :heads]
    gain_out[...] = small_ref[0:1, channels:heads_at]


def spread(out_grad, step_grad, gate_grad, inner_grad, state_grad, small, heads):
    depth = out_grad.shape[0]
    channels = heads * HEADDIM
    vmem = pl.BlockSpec(memory_space=pltpu.VMEM)
    shapes = [
        (channels, depth),
        (depth, heads),
        (depth, channels),
        (depth, channels),
        (depth, 2 * STATE),
        (KCONV, channels),
        (1, channels),
        (KCONV, 2 * STATE),
        (1, 2 * STATE),
        (1, heads),
        (1, heads),
        (1, heads),
        (1, channels),
    ]
    return pl.pallas_call(
        lambda *refs: spread_kernel(heads, *refs),
        in_specs=[vmem] * 6,
        out_specs=[vmem] * len(shapes),
        out_shape=[jax.ShapeDtypeStruct(shape, F32) for shape in shapes],
        name="spread",
    )(out_grad, step_grad, gate_grad, inner_grad, state_grad, small)


def column_of(row):
    return jnp.broadcast_to(row, (LANES, SPAN)).T[:, 0:1]


def finish_kernel(
    place_ref,
    x_ref,
    own_x_ref,
    own_cot_ref,
    part_ref,
    branch_ref,
    sums_ref,
    mean_ref,
    gain_ref,
    output_ref,
    grad_ref,
):
    hidden = x_ref[...].astype(F32)
    inv = lax.rsqrt(jnp.mean(hidden * hidden, axis=1, keepdims=True) + EPSILON)
    own = own_x_ref[...].astype(F32)
    gate_inv = lax.rsqrt(column_of(sums_ref[0:1]) / INNER + EPSILON)
    output_ref[...] = (own + gate_inv * branch_ref[...].astype(F32)).astype(BF16)
    mean = column_of(mean_ref[0:1]) / MODEL_WIDTH
    scaled = part_ref[...].astype(F32) * gain_ref[...]
    grad_ref[...] = own_cot_ref[...].astype(F32) + inv * scaled - own * (inv * inv * inv * mean)


def finish_pass(place, x, cot, part, branch, sums, mean, gain):
    tokens, share = part.shape

    def chunk(width):
        return pl.BlockSpec((SPAN, width), lambda i, place: (i, 0))

    own = pl.BlockSpec((SPAN, share), lambda i, place: (i, place[0]))
    rows = pl.BlockSpec((8, SPAN), lambda i, place: (0, i))
    return pl.pallas_call(
        finish_kernel,
        grid_spec=pltpu.PrefetchScalarGridSpec(
            num_scalar_prefetch=1,
            grid=(tokens // SPAN,),
            in_specs=[
                chunk(MODEL_WIDTH),
                own,
                own,
                chunk(share),
                chunk(share),
                rows,
                rows,
                pl.BlockSpec((1, share), lambda i, place: (0, place[0])),
            ],
            out_specs=[chunk(share), chunk(share)],
        ),
        out_shape=[
            jax.ShapeDtypeStruct((tokens, share), BF16),
            jax.ShapeDtypeStruct((tokens, share), F32),
        ],
        compiler_params=pltpu.CompilerParams(vmem_limit_bytes=VMEM_LIMIT),
        name="finish",
    )(place, x, x, cot, part, branch, sums, mean, gain)


MESH = pl.DeviceIdType.MESH


def remote(source, target, sends, receives, place):
    return pltpu.make_async_remote_copy(
        src_ref=source,
        dst_ref=target,
        send_sem=sends,
        recv_sem=receives,
        device_id=place,
        device_id_type=MESH,
    )


def greet(places):
    barrier = pltpu.get_barrier_semaphore()
    for place in places:
        pl.semaphore_signal(barrier, inc=1, device_id=place, device_id_type=MESH)
    pl.semaphore_wait(barrier, len(places))


def peers_of(axis):
    size, me = lax.axis_size(axis), lax.axis_index(axis)
    return [lax.rem(me + off, size) for off in range(1, size)]


def gather_kernel(count, *refs):
    shards, (x_ref, flags_ref) = refs[:count], refs[count : count + 2]
    outs, (halo_ref, other_flags_ref) = refs[count + 2 : 2 * count + 2], refs[2 * count + 2 : 2 * count + 4]
    send, receive, pass_send, pass_receive, own_sem, side_send, side_receive = refs[2 * count + 4 :]
    size, me = lax.axis_size("dp"), lax.axis_index("dp")
    core = lax.axis_index("ctx")
    partner = {"ctx": 1 - core}
    peers = peers_of("dp")
    greet([partner] + [{"dp": p} for p in peers])

    def rows(out, owner):
        depth = out.shape[0] // (2 * size)
        return out.at[pl.ds(pl.multiple_of((owner * 2 + core) * depth, depth), depth)]

    last = x_ref.shape[0] - 16
    waits = [
        remote(x_ref.at[pl.ds(last, 16)], halo_ref, side_send.at[0], side_receive.at[0], partner),
        remote(flags_ref, other_flags_ref, side_send.at[1], side_receive.at[1], partner),
    ]
    for copy in waits:
        copy.start()
    arriving, local = [], []
    for k in range(count):
        for off in range(size - 1, 0, -1):
            copy = remote(
                shards[k],
                rows(outs[k], me),
                send.at[k, off - 1],
                receive.at[k, off - 1],
                {"dp": peers[off - 1]},
            )
            copy.start()
            arriving.append((k, off, copy))
        copy = remote(shards[k], rows(outs[k], me), pass_send.at[k, 0], pass_receive.at[k, 0], partner)
        copy.start()
        waits.append(copy)
        copy = pltpu.make_async_copy(shards[k], rows(outs[k], me), own_sem.at[k])
        copy.start()
        local.append(copy)
    for k, off, copy in arriving:
        copy.wait_recv()
        block = rows(outs[k], lax.rem(me + size - off, size))
        onward = remote(block, block, pass_send.at[k, off], pass_receive.at[k, off], partner)
        onward.start()
        waits.append(onward)
    for copy in local + waits:
        copy.wait()
    for _, _, copy in arriving:
        copy.wait_send()


def gather(shards, x, flags, collective_id):
    size, count = lax.axis_size("dp"), len(shards)
    anywhere = pl.BlockSpec(memory_space=pl.ANY)
    dma = pltpu.SemaphoreType.DMA
    return pl.pallas_call(
        lambda *refs: gather_kernel(count, *refs),
        in_specs=[anywhere] * (count + 2),
        out_specs=[anywhere] * (count + 2),
        out_shape=[jax.ShapeDtypeStruct((s.shape[0] * 2 * size, s.shape[1]), s.dtype) for s in shards]
        + [jax.ShapeDtypeStruct((16, x.shape[1]), x.dtype), jax.ShapeDtypeStruct(flags.shape, flags.dtype)],
        scratch_shapes=[
            dma((count, size - 1)),
            dma((count, size - 1)),
            dma((count, size)),
            dma((count, size)),
            dma((count,)),
            dma((2,)),
            dma((2,)),
        ],
        compiler_params=pltpu.CompilerParams(collective_id=collective_id, has_side_effects=True),
        name="gather",
    )(*shards, x, flags)


def add_rows(out, terms, step_rows, first=0, width=None):
    rows = out.shape[0]
    columns = slice(None) if width is None else pl.ds(first, width)

    def add(step, carry):
        at = pl.ds(pl.multiple_of(step * step_rows, step_rows), step_rows)
        total = terms[0][at, columns].astype(F32)
        for term in terms[1:]:
            total = total + term[at, columns].astype(F32)
        out[at, :] = total.astype(out.dtype)
        return carry

    lax.fori_loop(0, rows // step_rows, add, 0)


def sums_kernel(sums_ref, out_ref, arriving, send, receive):
    peers = peers_of("tp")
    greet([{"tp": p} for p in peers])
    copies = []
    for i, p in enumerate(peers):
        copies.append(remote(sums_ref, arriving.at[i], send.at[i], receive.at[i], {"tp": p}))
        copies[-1].start()
    for copy in copies:
        copy.wait_recv()
    total = sums_ref[...]
    for i in range(len(peers)):
        total = total + arriving[i]
    out_ref[...] = total
    for copy in copies:
        copy.wait_send()


def sum_over_tp(sums, collective_id):
    others = lax.axis_size("tp") - 1
    vmem = pl.BlockSpec(memory_space=pltpu.VMEM)
    dma = pltpu.SemaphoreType.DMA
    return pl.pallas_call(
        sums_kernel,
        in_specs=[vmem],
        out_specs=vmem,
        out_shape=jax.ShapeDtypeStruct(sums.shape, F32),
        scratch_shapes=[pltpu.VMEM((others,) + sums.shape, F32), dma((others,)), dma((others,))],
        compiler_params=pltpu.CompilerParams(collective_id=collective_id, has_side_effects=True),
        name="sum_over_tp",
    )(sums)


def final_kernel(count, local_inner, shared, *refs):
    mean_ref, small_ref = refs[:2]
    wide_refs = refs[2 : 2 + count]
    mean_out_ref, gate_ref, out_ref, inner_ref, state_ref, step_ref, small_out_ref = refs[2 + count : 9 + count]
    scratch = refs[9 + count :]
    wide = [(wide_refs[k],) + tuple(scratch[3 * k : 3 * k + 3]) for k in range(count)]
    (
        mean_in,
        small_in,
        small_sum,
        small_far,
        shared_own,
        shared_in,
        state_own,
        state_in,
        z_send,
        z_receive,
        near_send,
        near_receive,
        far_send,
        far_receive,
        own_sem,
        small_send,
        small_receive,
    ) = scratch[3 * count :]
    size, me = lax.axis_size("dp"), lax.axis_index("dp")
    line = lax.axis_size("tp")
    core = lax.axis_index("ctx")
    partner = {"ctx": 1 - core}
    dp_peers, tp_peers = peers_of("dp"), peers_of("tp")
    greet([partner] + [{"dp": p} for p in dp_peers] + [{"tp": p} for p in tp_peers])
    near, local = {}, {}
    order = list(range(1, size)) + [0]
    for off in order:
        owner = lax.rem(me + off, size)
        for k, (grads, own, arriving, _) in enumerate(wide):
            depth = grads.shape[0] // (2 * size)

            def block(c, grads=grads, depth=depth, owner=owner):
                return grads.at[pl.ds(pl.multiple_of((owner * 2 + c) * depth, depth), depth)]

            near[off, k] = remote(
                block(1 - core), arriving.at[off], near_send.at[k, off], near_receive.at[k, off], partner
            )
            near[off, k].start()
            local[off, k] = pltpu.make_async_copy(block(core), own.at[off], own_sem.at[k, off])
            local[off, k].start()
    small_near = remote(small_ref, small_in, small_send.at[0], small_receive.at[0], partner)
    small_near.start()
    z_copies = []
    for i in range(line - 1):
        z_copies.append(
            remote(mean_ref, mean_in.at[i], z_send.at[0, i], z_receive.at[0, i], {"tp": tp_peers[i]})
        )
        z_copies[-1].start()
    far = []
    for off in order:
        for k, (_, own, arriving, remote_in) in enumerate(wide):
            local[off, k].wait()
            near[off, k].wait_recv()
            add_rows(own.at[off], [own.at[off], arriving.at[off]], 16)
            if off > 0:
                copy = remote(
                    own.at[off],
                    remote_in.at[off - 1],
                    far_send.at[k, off - 1],
                    far_receive.at[k, off - 1],
                    {"dp": dp_peers[off - 1]},
                )
                copy.start()
                far.append(copy)
    small_near.wait_recv()
    small_sum[...] = small_ref[...] + small_in[...]
    small_copies = []
    for off in range(1, size):
        copy = remote(
            small_sum, small_far.at[off - 1], small_send.at[off], small_receive.at[off], {"dp": dp_peers[off - 1]}
        )
        copy.start()
        small_copies.append(copy)
    for copy in z_copies:
        copy.wait_recv()
    add_rows(mean_out_ref, [mean_ref] + [mean_in.at[i] for i in range(line - 1)], 8)
    for copy in small_copies:
        copy.wait_recv()
    total = small_sum[...]
    for off in range(1, size):
        total = total + small_far[off - 1]
    small_out_ref[...] = total
    shared_own[...] = total[:, -shared:]
    terms = [[own.at[0]] + [remote_in.at[i] for i in range(size - 1)] for _, own, _, remote_in in wide]
    for copy in far:
        copy.wait_recv()
    add_rows(state_own, terms[2], 16, local_inner, 2 * STATE)
    last = []
    for i in range(line - 1):
        place = {"tp": tp_peers[i]}
        last.append(remote(state_own, state_in.at[i], z_send.at[1, i], z_receive.at[1, i], place))
        last.append(remote(shared_own, shared_in.at[i], z_send.at[2, i], z_receive.at[2, i], place))
    for copy in last:
        copy.start()
    add_rows(gate_ref, terms[0], 16)
    add_rows(out_ref, terms[1], 16)
    add_rows(inner_ref, terms[2], 16, 0, local_inner)
    add_rows(step_ref, terms[2], 16, local_inner + 2 * STATE, LANES)
    for copy in last:
        copy.wait_recv()
    add_rows(state_ref, [state_own] + [state_in.at[i] for i in range(line - 1)], 16)
    total = shared_own[...]
    for i in range(line - 1):
        total = total + shared_in[i]
    small_out_ref[:, -shared:] = total
    for copy in z_copies + last + far + small_copies + [small_near] + list(near.values()):
        copy.wait_send()


def final_exchange(mean, small, wide, local_inner, shared, collective_id):
    size, line = lax.axis_size("dp"), lax.axis_size("tp")
    count = len(wide)
    depth = wide[0].shape[0] // (2 * size)
    anywhere = pl.BlockSpec(memory_space=pl.ANY)
    vmem = pl.BlockSpec(memory_space=pltpu.VMEM)
    dma = pltpu.SemaphoreType.DMA

    def out(*shape):
        return jax.ShapeDtypeStruct(shape, F32)

    slots = []
    for like in wide:
        for copies in (size, size, size - 1):
            slots.append(pltpu.VMEM((copies, depth, like.shape[1]), BF16))
    return pl.pallas_call(
        lambda *refs: final_kernel(count, local_inner, shared, *refs),
        in_specs=[vmem, vmem] + [anywhere] * count,
        out_specs=[vmem] * 7,
        out_shape=[
            out(*mean.shape),
            out(depth, local_inner),
            out(depth, local_inner),
            out(depth, local_inner),
            out(depth, 2 * STATE),
            out(depth, LANES),
            out(*small.shape),
        ],
        scratch_shapes=slots
        + [
            pltpu.VMEM((line - 1,) + mean.shape, F32),
            pltpu.VMEM(small.shape, F32),
            pltpu.VMEM(small.shape, F32),
            pltpu.VMEM((size - 1,) + small.shape, F32),
            pltpu.VMEM((8, shared), F32),
            pltpu.VMEM((line - 1, 8, shared), F32),
            pltpu.VMEM((depth, 2 * STATE), BF16),
            pltpu.VMEM((line - 1, depth, 2 * STATE), BF16),
            dma((3, line - 1)),
            dma((3, line - 1)),
            dma((count, size)),
            dma((count, size)),
            dma((count, size - 1)),
            dma((count, size - 1)),
            dma((count, size)),
            dma((size,)),
            dma((size,)),
        ],
        compiler_params=pltpu.CompilerParams(
            collective_id=collective_id, has_side_effects=True, vmem_limit_bytes=VMEM_LIMIT
        ),
        name="final_exchange",
    )(mean, small, *wide)


def row(v, width):
    return jnp.pad(v, (0, width - v.shape[0]))[None, :]


def on_device(
    block_input_activations,
    sequence_first_token,
    norm_gain,
    gate_proj,
    input_proj,
    step_proj,
    state_proj,
    conv_inner_weight,
    conv_inner_bias,
    conv_state_weight,
    conv_state_bias,
    step_bias,
    decay_log,
    skip_weight,
    gate_gain,
    out_proj,
    output_cotangent,
):
    everyone = ("dp", "ctx")
    x = block_input_activations
    local_inner = gate_proj.shape[1]
    heads = step_bias.shape[0]
    tokens = x.shape[0]
    main = local_inner + 2 * STATE
    width = KCONV - 1
    step_pad = jnp.pad(step_proj, ((0, 0), (0, LANES - heads)))
    flags = sequence_first_token.astype(F32)
    early_full = lax.all_gather(
        jnp.concatenate([gate_proj, out_proj.T], axis=1), everyone, axis=0, tiled=True
    )
    late_full, halo_x, other_flags = gather(
        [jnp.concatenate([input_proj, state_proj, step_pad], axis=1)],
        x,
        flags.reshape(-1, LANES),
        4,
    )
    going_on = 1.0 - flags
    before = jnp.concatenate([jnp.ones((width,), F32), going_on])
    lag1 = going_on
    lag2 = lag1 * before[width - 1 : width - 1 + tokens]
    lag3 = lag2 * before[width - 2 : width - 2 + tokens]
    none = jnp.zeros_like(flags)
    marks = jnp.stack([flags, lag1, lag2, lag3, none, none, none, none], axis=1)
    gain = norm_gain[None, :]
    taps = jnp.concatenate([conv_inner_weight, conv_state_weight], axis=1)
    bias = jnp.concatenate([conv_inner_bias, conv_state_bias])[None, :]
    decay_row = row(decay_log, LANES)
    skip_row = jnp.repeat(skip_weight, HEADDIM)[None, :]
    gated_gain = gate_gain[None, :]
    (
        normed,
        rows,
        conv,
        mixed_local,
        cum,
        raw,
        passing,
        out_map,
        states,
        products,
        final_state,
        halo_rows,
    ) = front(
        x, marks, halo_x, other_flags, gain, late_full, taps, bias, row(step_bias, LANES), decay_row, skip_row, heads
    )
    carried = passed_along(final_state, 1)
    gate, mixed, back, sums, branch_part = gate_pass(
        normed, output_cotangent, mixed_local, passing, out_map, carried, early_full, gated_gain, heads
    )
    sums = sum_over_tp(sums, 1)
    sums, branch_part = lax.optimization_barrier((sums, branch_part))
    branch = lax.psum_scatter(branch_part, "tp", scatter_dimension=1, tiled=True)
    gated_normed, grad_mixed, grad_gate, through, grad_gain_gate = middle_pass(
        gate, mixed, back, sums, passing, out_map, gated_gain, heads
    )
    following = passed_along(through, -1)
    grad_out = dot_tn(output_cotangent, gated_normed).astype(BF16)
    grad_gate_weight = dot_tn(normed, grad_gate).astype(BF16)
    grad_mixed, grad_gate_weight, grad_out = lax.optimization_barrier((grad_mixed, grad_gate_weight, grad_out))
    late, tail, halo_grad, conv_sums, head_sums = back_pass(
        grad_mixed,
        conv,
        rows,
        halo_rows,
        raw,
        cum,
        states,
        products,
        carried,
        following,
        taps,
        decay_row,
        skip_row,
        heads,
    )
    returned = passed_along(halo_grad, -1)
    tensor_part, mean_sum, gain_sums, late = input_pass(
        x, grad_gate, late, tail, returned, early_full, late_full, gain
    )
    own_grad = lax.psum_scatter(tensor_part, "tp", scatter_dimension=1, tiled=True)
    late_weight = dot_tn(normed, late).astype(BF16)
    shared = 2 * STATE + MODEL_WIDTH
    small = jnp.concatenate(
        [conv_sums[:, :local_inner], grad_gain_gate, head_sums, conv_sums[:, local_inner:], gain_sums], axis=1
    )
    mean_sum, gate_grad, out_grad, inner_grad, state_grad, step_grad, small = final_exchange(
        mean_sum, small, [grad_gate_weight, grad_out, late_weight], local_inner, shared, 2
    )
    place = lax.axis_index("tp")
    share = MODEL_WIDTH // lax.axis_size("tp")
    gain_grad = lax.dynamic_slice_in_dim(small[0], small.shape[1] - MODEL_WIDTH + place * share, share, 0)
    (
        out_grad,
        step_grad,
        gate_grad,
        inner_grad,
        state_grad,
        inner_taps,
        inner_bias,
        state_taps,
        state_bias,
        step_bias_grad,
        decay_grad,
        skip_grad,
        gate_gain_grad,
    ) = spread(out_grad, step_grad, gate_grad, inner_grad, state_grad, small, heads)
    block_output, input_grad = finish_pass(
        place.reshape(1), x, output_cotangent, own_grad, branch, sums, mean_sum, gain
    )
    return (
        block_output,
        input_grad,
        gain_grad,
        gate_grad,
        inner_grad,
        step_grad,
        state_grad,
        inner_taps,
        inner_bias[0],
        state_taps,
        state_bias[0],
        step_bias_grad[0],
        decay_grad[0],
        skip_grad[0],
        gate_gain_grad[0],
        out_grad,
    )


def solution(mesh):
    return jax.shard_map(
        on_device,
        mesh=mesh,
        in_specs=(
            P(("dp", "ctx"), None),
            P(("dp", "ctx")),
            P(),
            P(("dp", "ctx"), "tp"),
            P(("dp", "ctx"), "tp"),
            P(("dp", "ctx"), "tp"),
            P(("dp", "ctx"), None),
            P(None, "tp"),
            P("tp"),
            P(),
            P(),
            P("tp"),
            P("tp"),
            P("tp"),
            P("tp"),
            P("tp", ("dp", "ctx")),
            P(("dp", "ctx"), None),
        ),
        out_specs=(
            P(("dp", "ctx"), "tp"),
            P(("dp", "ctx"), "tp"),
            P("tp"),
            P(("dp", "ctx"), "tp"),
            P(("dp", "ctx"), "tp"),
            P(("dp", "ctx"), "tp"),
            P(("dp", "ctx"), None),
            P(None, "tp"),
            P("tp"),
            P(),
            P(),
            P("tp"),
            P("tp"),
            P("tp"),
            P("tp"),
            P("tp", ("dp", "ctx")),
        ),
        check_vma=False,
    )
```

```python
import jax
import jax.numpy as jnp
from jax import lax
from jax.experimental import pallas as pl
from jax.experimental.pallas import tpu as pltpu
from jax.sharding import PartitionSpec as P

MODEL_WIDTH = 1024
HEADDIM = 64
STATE = 128
KCONV = 4
SPAN = 256
INNER = 2048


EPSILON = 1e-05
HIGHEST = lax.Precision.HIGHEST


def passed_along(block, distance):
    devices = range(lax.axis_size("ctx"))
    route = [(i - distance, i) for i in devices if i - distance in devices]
    return lax.ppermute(block, "ctx", route)


LANES = 128
VMEM_LIMIT = 60 * 1024 * 1024
BF16 = jnp.bfloat16
F32 = jnp.float32
BLOCKED = -1e30


def dot_nn(a, b):
    return jnp.dot(a, b, preferred_element_type=F32)


def dot_nt(a, b):
    return lax.dot_general(a, b, (((1,), (1,)), ((), ())), preferred_element_type=F32)


def dot_tn(a, b):
    return lax.dot_general(a, b, (((0,), (0,)), ((), ())), preferred_element_type=F32)


def iota(shape, dim):
    return lax.broadcasted_iota(jnp.int32, shape, dim)


def high_low(a):
    high = a.astype(BF16)
    return high, (a - high.astype(F32)).astype(BF16)


def widen(a, heads, width):
    lane = iota(a.shape, 1)
    high = a.astype(BF16).astype(F32)
    low = pltpu.roll(a - high, heads, 1)
    packed = jnp.where(lane < heads, high, jnp.where(lane < 2 * heads, low, 0.0)).astype(BF16)
    row, column = iota((LANES, width), 0), iota((LANES, width), 1)
    place = jnp.where(row < heads, row, row - heads)
    return dot_nn(packed, (column // HEADDIM == place).astype(BF16))


def per_head_sum(a, heads):
    high, low = high_low(a)
    row, column = iota((LANES, a.shape[1]), 0), iota((LANES, a.shape[1]), 1)
    pick = (column // HEADDIM == row).astype(BF16)
    return dot_nt(high, pick) + dot_nt(low, pick)


def row_sum(a):
    folded = a[:, :LANES]
    for i in range(1, a.shape[1] // LANES):
        folded = folded + a[:, i * LANES : (i + 1) * LANES]
    return jnp.sum(folded.T, axis=0, keepdims=True)


def rows_of_heads(column, heads):
    return jnp.concatenate(
        [jnp.broadcast_to(column[h : h + 1, :], (HEADDIM, LANES)) for h in range(heads)], axis=0
    )


def column_of(row):
    return jnp.broadcast_to(row, (LANES, SPAN)).T[:, 0:1]


def sigmoid(v):
    return 0.5 * jnp.tanh(0.5 * v) + 0.5


def normalise(x, gain):
    hidden = x.astype(F32)
    inv = lax.rsqrt(jnp.mean(hidden * hidden, axis=1, keepdims=True) + EPSILON)
    return (hidden * inv * gain).astype(BF16)


def whole(shape):
    return pl.BlockSpec(shape, lambda i: (0,) * len(shape))


def columns_of(array, width, block):
    return pl.BlockSpec((array.shape[0], width), lambda i: (0, block))


def front_kernel(
    heads,
    x_ref,
    marks_ref,
    halo_x_ref,
    flags_ref,
    gain_ref,
    weight_ref,
    taps_ref,
    bias_ref,
    step_bias_ref,
    decay_ref,
    skip_ref,
    normed_ref,
    rows_ref,
    conv_ref,
    mixed_ref,
    cum_ref,
    raw_ref,
    passing_ref,
    out_map_ref,
    states_ref,
    products_ref,
    final_ref,
    halo_rows_ref,
    state,
    product,
    before,
):
    step = pl.program_id(0)
    channels = heads * HEADDIM
    main = channels + 2 * STATE
    gain = gain_ref[...]

    @pl.when(step == 0)
    def _():
        state[...] = jnp.zeros_like(state)
        product[...] = jnp.ones_like(product)
        halo = dot_nn(normalise(halo_x_ref[...], gain), weight_ref[:, :main]).astype(BF16)
        halo_rows_ref[...] = halo
        before[...] = halo.astype(F32)[8:16]

    normed = normalise(x_ref[...], gain)
    normed_ref[...] = normed
    projected = dot_nn(normed, weight_ref[...])
    rows = projected[:, :main].astype(BF16)
    rows_ref[...] = rows
    rows = rows.astype(F32)
    raw = projected[:, main:] + step_bias_ref[...]
    extended = jnp.concatenate([before[...], rows], axis=0)
    before[...] = rows[SPAN - 8 :]
    taps = taps_ref[...]
    conv = bias_ref[...] + taps[0:1] * rows
    lane = iota((SPAN, LANES), 1)
    boundary = jnp.where(step == 0, flags_ref[flags_ref.shape[0] - 1 :, LANES - KCONV :], 0.0)
    reach = 1.0 - boundary
    at_first, at_second = iota((SPAN, 1), 0) == 0, iota((SPAN, 1), 0) == 1
    nearest, second = reach[:, KCONV - 1 :], reach[:, KCONV - 2 : KCONV - 1]
    edges = [
        None,
        None,
        jnp.where(at_first, nearest, 1.0),
        jnp.where(at_first, nearest * second, jnp.where(at_second, nearest, 1.0)),
    ]
    for lag in range(1, KCONV):
        valid = marks_ref[:, lag : lag + 1]
        if edges[lag] is not None:
            valid = valid * edges[lag]
        raw = jnp.where(lane == heads + lag, valid, raw)
        conv = conv + (taps[lag : lag + 1] * extended[8 - lag : 8 - lag + SPAN]) * valid
    raw_ref[...] = raw
    conv_ref[...] = conv
    act = conv * sigmoid(conv)
    values = act[:, :channels]
    map_in = act[:, channels : channels + STATE].astype(BF16)
    map_out = act[:, channels + STATE :].astype(BF16)
    out_map_ref[...] = map_out

    step_size = jnp.maximum(raw, 0.0) + jnp.log1p(jnp.exp(-jnp.abs(raw)))
    log_decay = jnp.where(lane < heads, step_size * (-jnp.exp(decay_ref[...])), 0.0)
    series = jnp.where(lane == heads, marks_ref[:, 0:1], log_decay)
    t, s = iota((SPAN, SPAN), 0), iota((SPAN, SPAN), 1)
    cum = jnp.dot((t >= s).astype(F32), series, precision=HIGHEST, preferred_element_type=F32)
    cum_ref[...] = cum
    cum_rows = cum.T
    segment, segment_row = cum[:, heads : heads + 1], cum_rows[heads : heads + 1, :]
    blocked = jnp.where((segment == segment_row) & (t >= s), 0.0, BLOCKED)
    passing = jnp.where(segment == 0.0, jnp.exp(cum), 0.0)
    product_now = product[...]
    passing_ref[...] = passing * product_now[0:1]
    products_ref[0] = product_now
    product[...] = product_now * passing[SPAN - 1 : SPAN]
    to_end = jnp.where(
        segment == cum[SPAN - 1 : SPAN, heads : heads + 1], jnp.exp(cum[SPAN - 1 : SPAN] - cum), 0.0
    )
    stepped = values * widen(step_size, heads, channels)
    state_now = state[...]
    states_ref[0] = state_now
    scores = dot_nt(map_out, map_in)
    through = widen(passing, heads, channels) * dot_nt(map_out, state_now.astype(BF16))
    half = iota((SPAN, LANES), 1) < HEADDIM
    for pair in range(heads // 2):
        at = slice(pair * LANES, (pair + 1) * LANES)
        both = stepped[:, at]
        total = through[:, at] + skip_ref[:, at] * values[:, at]
        for side in range(2):
            h = 2 * pair + side
            spread = cum[:, h : h + 1] - cum_rows[h : h + 1, :]
            mixing = (jnp.exp(spread + blocked) * scores).astype(BF16)
            own = jnp.where(half if side == 0 else ~half, both, 0.0).astype(BF16)
            total = total + dot_nn(mixing, own)
        mixed_ref[:, at] = total
    ending = (stepped * widen(to_end, heads, channels)).astype(BF16)
    fresh = dot_tn(ending, map_in)
    kept = jnp.where(segment_row[:, SPAN - 1 :] == 0.0, jnp.exp(cum_rows[:, SPAN - 1 :]), 0.0)
    state_next = rows_of_heads(kept, heads) * state_now + fresh
    state[...] = state_next
    final_ref[...] = state_next


def front(x, marks, halo_x, flags, gain, weight, taps, bias, step_bias, decay, skip, heads):
    tokens = x.shape[0]
    channels = heads * HEADDIM
    main = channels + 2 * STATE
    spans = tokens // SPAN

    def chunk(width):
        return pl.BlockSpec((SPAN, width), lambda i: (i, 0))

    def out(shape, dtype):
        return jax.ShapeDtypeStruct(shape, dtype)

    return pl.pallas_call(
        lambda *refs: front_kernel(heads, *refs),
        grid=(spans,),
        in_specs=[
            chunk(MODEL_WIDTH),
            chunk(LANES),
            whole(halo_x.shape),
            whole(flags.shape),
            whole(gain.shape),
            whole(weight.shape),
            whole(taps.shape),
            whole(bias.shape),
            whole(step_bias.shape),
            whole(decay.shape),
            whole(skip.shape),
        ],
        out_specs=[
            chunk(MODEL_WIDTH),
            chunk(main),
            chunk(main),
            chunk(channels),
            chunk(LANES),
            chunk(LANES),
            chunk(LANES),
            chunk(STATE),
            pl.BlockSpec((1, channels, STATE), lambda i: (i, 0, 0)),
            pl.BlockSpec((1, 8, LANES), lambda i: (i, 0, 0)),
            whole((channels, STATE)),
            whole((16, main)),
        ],
        out_shape=[
            out((tokens, MODEL_WIDTH), BF16),
            out((tokens, main), BF16),
            out((tokens, main), F32),
            out((tokens, channels), F32),
            out((tokens, LANES), F32),
            out((tokens, LANES), F32),
            out((tokens, LANES), F32),
            out((tokens, STATE), BF16),
            out((spans, channels, STATE), F32),
            out((spans, 8, LANES), F32),
            out((channels, STATE), F32),
            out((16, main), BF16),
        ],
        scratch_shapes=[
            pltpu.VMEM((channels, STATE), F32),
            pltpu.VMEM((8, LANES), F32),
            pltpu.VMEM((8, main), F32),
        ],
        compiler_params=pltpu.CompilerParams(vmem_limit_bytes=VMEM_LIMIT),
        cost_estimate=pl.CostEstimate(
            flops=2 * tokens * (MODEL_WIDTH * weight.shape[1] + 4 * SPAN * channels),
            bytes_accessed=18 * 2**20,
            transcendentals=tokens * SPAN * heads,
        ),
        name="scan_front",
    )(x, marks, halo_x, flags, gain, weight, taps, bias, step_bias, decay, skip)


def back_kernel(
    heads,
    grad_ref,
    conv_ref,
    rows_ref,
    earlier_ref,
    halo_ref,
    raw_ref,
    cum_ref,
    states_ref,
    products_ref,
    carried_ref,
    next_ref,
    taps_ref,
    decay_ref,
    skip_ref,
    late_ref,
    tail_ref,
    halo_grad_ref,
    sums_ref,
    head_sums_ref,
    flowing,
    after,
):
    step = pl.program_id(0)
    spans = pl.num_programs(0)
    channels = heads * HEADDIM
    main = channels + 2 * STATE

    @pl.when(step == 0)
    def _():
        flowing[...] = next_ref[...]
        after[...] = jnp.zeros_like(after)
        sums_ref[...] = jnp.zeros_like(sums_ref)
        head_sums_ref[...] = jnp.zeros_like(head_sums_ref)

    conv = conv_ref[...]
    sig = sigmoid(conv)
    act = conv * sig
    slope = sig * (1.0 + conv * (1.0 - sig))
    values = act[:, :channels]
    map_in = act[:, channels : channels + STATE].astype(BF16)
    map_out = act[:, channels + STATE :].astype(BF16)
    raw = raw_ref[...]
    step_size = jnp.maximum(raw, 0.0) + jnp.log1p(jnp.exp(-jnp.abs(raw)))
    cum = cum_ref[...]
    cum_rows = cum.T
    segment, segment_row = cum[:, heads : heads + 1], cum_rows[heads : heads + 1, :]
    s, t = iota((SPAN, SPAN), 0), iota((SPAN, SPAN), 1)
    blocked = jnp.where((segment == segment_row) & (t >= s), 0.0, BLOCKED)
    passing = jnp.where(segment == 0.0, jnp.exp(cum), 0.0)
    to_end = jnp.where(
        segment == cum[SPAN - 1 : SPAN, heads : heads + 1], jnp.exp(cum[SPAN - 1 : SPAN] - cum), 0.0
    )
    kept = jnp.where(segment_row[:, SPAN - 1 :] == 0.0, jnp.exp(cum_rows[:, SPAN - 1 :]), 0.0)
    product_column = jnp.broadcast_to(products_ref[0][0:1], (LANES, LANES)).T
    state = states_ref[0] + rows_of_heads(product_column[:, 0:1], heads) * carried_ref[...]
    state_bf = state.astype(BF16)
    flow = flowing[...]
    flow_bf = flow.astype(BF16)
    grad = grad_ref[...]
    step_wide = widen(step_size, heads, channels)
    end_wide = widen(to_end, heads, channels)
    stepped = values * step_wide
    stepped_bf = stepped.astype(BF16)
    grad_bf = grad.astype(BF16)
    reaching = grad * widen(passing, heads, channels)
    reaching_bf = reaching.astype(BF16)
    ending = stepped * end_wide
    ending_bf = ending.astype(BF16)
    from_state = dot_nt(map_out, state_bf)
    from_flow = dot_nt(map_in, flow_bf)
    scores = dot_nt(map_in, map_out)
    half = iota((SPAN, LANES), 1) < HEADDIM
    zero = jnp.zeros((SPAN, LANES), BF16)
    lane = iota((SPAN, LANES), 1)
    grad_scores = jnp.zeros((SPAN, SPAN), F32)
    out_sums = jnp.zeros((SPAN, LANES), F32)
    in_sums = []
    grad_stepped = []
    for pair in range(heads // 2):
        at = slice(pair * LANES, (pair + 1) * LANES)
        total = end_wide[:, at] * from_flow[:, at]
        for side in range(2):
            h = 2 * pair + side
            own = half if side == 0 else ~half
            decay = jnp.exp((cum_rows[h : h + 1, :] - cum[:, h : h + 1]) + blocked)
            own_grad = jnp.where(own, grad_bf[:, at], zero)
            total = total + dot_nn((decay * scores).astype(BF16), own_grad)
            flowed = decay * dot_nt(stepped_bf[:, at], own_grad)
            grad_scores = grad_scores + flowed
            weighed = flowed * scores
            in_sums.append(jnp.sum(weighed, axis=0, keepdims=True))
            out_sums = jnp.where(lane == h, jnp.sum(weighed, axis=1, keepdims=True), out_sums)
        grad_stepped.append(total)
    grad_stepped = jnp.concatenate(grad_stepped, axis=1)
    grad_scores = grad_scores.astype(BF16)
    grad_out_map = dot_tn(grad_scores, map_in) + dot_nn(reaching_bf, state_bf)
    grad_in_map = dot_nn(grad_scores, map_out) + dot_nn(ending_bf, flow_bf)
    ended = per_head_sum(ending * from_flow, heads)
    row, column = iota((LANES, channels), 0), iota((LANES, channels), 1)
    pick = (column // HEADDIM == row).astype(BF16)
    high, low = high_low(flow * state)
    at_last = kept * jnp.sum(dot_nn(pick, high) + dot_nn(pick, low), axis=1, keepdims=True)
    in_rows = jnp.concatenate(
        in_sums + [jnp.zeros((LANES - heads, SPAN), F32)], axis=0
    ) + jnp.where(iota((LANES, SPAN), 1) == SPAN - 1, at_last, 0.0)
    last = iota((SPAN, LANES), 0) == SPAN - 1
    grad_cum = (
        in_rows.T
        - out_sums
        + per_head_sum(reaching * from_state, heads)
        - ended
        + jnp.where(last, jnp.sum(ended, axis=0, keepdims=True), 0.0)
    )
    grad_log = jnp.dot((t >= s).astype(F32), grad_cum, precision=HIGHEST, preferred_element_type=F32)
    rate = -jnp.exp(decay_ref[...])
    grad_step = per_head_sum(grad_stepped * values, heads) + grad_log * rate
    grad_raw = jnp.where(lane < heads, grad_step * sigmoid(raw), 0.0)
    late_ref[:, main:] = grad_raw.astype(BF16)
    head_sums_ref[0:1] += jnp.sum(grad_raw, axis=0, keepdims=True)
    head_sums_ref[1:2] += jnp.sum(grad_log * step_size, axis=0, keepdims=True) * rate
    flowing[...] = rows_of_heads(kept, heads) * flow + dot_tn(reaching_bf, map_out)
    grad_values = grad_stepped * step_wide + skip_ref[...] * grad
    grad_act = jnp.concatenate([grad_values, grad_in_map, grad_out_map], axis=1)
    grad_conv = grad_act * slope
    sums_ref[5:6, :channels] += jnp.sum(grad * values, axis=0, keepdims=True)
    sums_ref[4:5] += jnp.sum(grad_conv, axis=0, keepdims=True)
    rows = rows_ref[...].astype(F32)
    first = step == spans - 1
    previous = jnp.where(first, halo_ref[...].astype(F32), earlier_ref[...].astype(F32))[8:16]
    extended = jnp.concatenate([previous, rows], axis=0)
    sums_ref[0:1] += jnp.sum(grad_conv * rows, axis=0, keepdims=True)
    taps = taps_ref[...]
    grad_rows = taps[0:1] * grad_conv
    halo_grad = jnp.zeros((8, main), F32)
    for lag in range(1, KCONV):
        valid = grad_conv * raw[:, heads + lag : heads + lag + 1]
        sums_ref[lag : lag + 1] += jnp.sum(
            valid * extended[8 - lag : 8 - lag + SPAN], axis=0, keepdims=True
        )
        tapped = taps[lag : lag + 1] * valid
        joined = jnp.concatenate([tapped, after[lag - 1]], axis=0)
        grad_rows = grad_rows + joined[lag : lag + SPAN]
        head = tapped[0:8]
        after[lag - 1] = head
        halo_grad = halo_grad + jnp.concatenate([jnp.zeros((8, main), F32), head], axis=0)[lag : lag + 8]
    late_ref[:, :main] = grad_rows.astype(BF16)
    halo_grad_ref[...] = halo_grad

    @pl.when(step == 0)
    def _():
        tail_ref[...] = grad_rows[SPAN - 16 :]


def back_pass(
    grad, conv, rows, halo, raw, cum, states, products, carried, following, taps, decay, skip, heads
):
    tokens = grad.shape[0]
    channels = heads * HEADDIM
    main = channels + 2 * STATE
    spans = tokens // SPAN

    def chunk(width):
        return pl.BlockSpec((SPAN, width), lambda i: (spans - 1 - i, 0))

    return pl.pallas_call(
        lambda *refs: back_kernel(heads, *refs),
        grid=(spans,),
        in_specs=[
            chunk(channels),
            chunk(main),
            chunk(main),
            pl.BlockSpec((16, main), lambda i: (jnp.maximum((spans - 1 - i) * (SPAN // 16) - 1, 0), 0)),
            whole(halo.shape),
            chunk(LANES),
            chunk(LANES),
            pl.BlockSpec((1, channels, STATE), lambda i: (spans - 1 - i, 0, 0)),
            pl.BlockSpec((1, 8, LANES), lambda i: (spans - 1 - i, 0, 0)),
            whole(carried.shape),
            whole(following.shape),
            whole(taps.shape),
            whole(decay.shape),
            whole(skip.shape),
        ],
        out_specs=[
            chunk(main + LANES),
            whole((16, main)),
            whole((8, main)),
            whole((8, main)),
            whole((8, LANES)),
        ],
        out_shape=[
            jax.ShapeDtypeStruct((tokens, main + LANES), BF16),
            jax.ShapeDtypeStruct((16, main), F32),
            jax.ShapeDtypeStruct((8, main), F32),
            jax.ShapeDtypeStruct((8, main), F32),
            jax.ShapeDtypeStruct((8, LANES), F32),
        ],
        scratch_shapes=[
            pltpu.VMEM((channels, STATE), F32),
            pltpu.VMEM((KCONV - 1, 8, main), F32),
        ],
        compiler_params=pltpu.CompilerParams(vmem_limit_bytes=VMEM_LIMIT),
        cost_estimate=pl.CostEstimate(
            flops=2 * tokens * 12 * SPAN * channels,
            bytes_accessed=12 * 2**20,
            transcendentals=tokens * SPAN * heads,
        ),
        name="scan_back",
    )(
        grad, conv, rows, rows, halo, raw, cum, states, products, carried, following, taps, decay, skip
    )


def input_kernel(
    x_ref,
    grad_gate_ref,
    late_ref,
    tail_ref,
    returned_ref,
    gate_weight_ref,
    late_weight_ref,
    gain_ref,
    part_ref,
    sums_ref,
    grad_gain_ref,
    whole_late_ref,
):
    step = pl.program_id(0)
    whole_late_ref[...] = late_ref[...]

    @pl.when(step == pl.num_programs(0) - 1)
    def _():
        main = tail_ref.shape[1]
        tail = tail_ref[...] + jnp.concatenate([jnp.zeros((8, main), F32), returned_ref[...]], axis=0)
        whole_late_ref[SPAN - 16 :, :main] = tail.astype(BF16)

    part = dot_nt(grad_gate_ref[...], gate_weight_ref[...])
    part = part + dot_nt(whole_late_ref[...], late_weight_ref[...])
    part_ref[...] = part.astype(BF16)
    hidden = x_ref[...].astype(F32)
    inv = lax.rsqrt(jnp.mean(hidden * hidden, axis=1, keepdims=True) + EPSILON)
    term = part * hidden
    sums_ref[...] = jnp.broadcast_to(row_sum(term * gain_ref[...]), (8, SPAN))
    gain_part = jnp.sum(term * inv, axis=0, keepdims=True)

    @pl.when(step == 0)
    def _():
        grad_gain_ref[...] = jnp.zeros_like(grad_gain_ref)

    grad_gain_ref[0:1] += gain_part


def input_pass(x, grad_gate, late, tail, returned, early_weight, late_weight, gain):
    tokens = x.shape[0]
    channels = grad_gate.shape[1]

    def chunk(width):
        return pl.BlockSpec((SPAN, width), lambda i: (i, 0))

    return pl.pallas_call(
        input_kernel,
        grid=(tokens // SPAN,),
        in_specs=[
            chunk(MODEL_WIDTH),
            chunk(channels),
            chunk(late.shape[1]),
            whole(tail.shape),
            whole(returned.shape),
            columns_of(early_weight, channels, 0),
            whole(late_weight.shape),
            whole(gain.shape),
        ],
        out_specs=[
            chunk(MODEL_WIDTH),
            pl.BlockSpec((8, SPAN), lambda i: (0, i)),
            whole((8, MODEL_WIDTH)),
            chunk(late.shape[1]),
        ],
        out_shape=[
            jax.ShapeDtypeStruct((tokens, MODEL_WIDTH), BF16),
            jax.ShapeDtypeStruct((8, tokens), F32),
            jax.ShapeDtypeStruct((8, MODEL_WIDTH), F32),
            jax.ShapeDtypeStruct(late.shape, BF16),
        ],
        compiler_params=pltpu.CompilerParams(vmem_limit_bytes=VMEM_LIMIT),
        cost_estimate=pl.CostEstimate(
            flops=2 * tokens * MODEL_WIDTH * (channels + late.shape[1]),
            bytes_accessed=12 * 2**20,
            transcendentals=0,
        ),
        name="input_pass",
    )(x, grad_gate, late, tail, returned, early_weight, late_weight, gain)


def spread_kernel(heads, out_ref, step_ref, gate_ref, inner_ref, state_ref, small_ref, *outs):
    channels = heads * HEADDIM
    out_out, step_out, gate_out, inner_out, state_out = outs[:5]
    taps_out, bias_out, state_taps_out, state_bias_out, step_bias_out, decay_out, skip_out, gain_out = outs[5:]
    out_out[...] = out_ref[...].T
    step_out[...] = step_ref[:, :heads]
    gate_out[...] = gate_ref[...]
    inner_out[...] = inner_ref[...]
    state_out[...] = state_ref[...]
    heads_at = 2 * channels
    state_at = heads_at + LANES
    taps_out[...] = small_ref[:KCONV, :channels]
    bias_out[...] = small_ref[KCONV : KCONV + 1, :channels]
    state_taps_out[...] = small_ref[:KCONV, state_at : state_at + 2 * STATE]
    state_bias_out[...] = small_ref[KCONV : KCONV + 1, state_at : state_at + 2 * STATE]
    step_bias_out[...] = small_ref[0:1, heads_at : heads_at + LANES][:, :heads]
    decay_out[...] = small_ref[1:2, heads_at : heads_at + LANES][:, :heads]
    skip_out[...] = per_head_sum(small_ref[:, :channels], heads)[5:6, :heads]
    gain_out[...] = small_ref[0:1, channels:heads_at]


def spread(out_grad, step_grad, gate_grad, inner_grad, state_grad, small, heads):
    depth = out_grad.shape[0]
    channels = heads * HEADDIM
    vmem = pl.BlockSpec(memory_space=pltpu.VMEM)
    shapes = [
        (channels, depth),
        (depth, heads),
        (depth, channels),
        (depth, channels),
        (depth, 2 * STATE),
        (KCONV, channels),
        (1, channels),
        (KCONV, 2 * STATE),
        (1, 2 * STATE),
        (1, heads),
        (1, heads),
        (1, heads),
        (1, channels),
    ]
    return pl.pallas_call(
        lambda *refs: spread_kernel(heads, *refs),
        in_specs=[vmem] * 6,
        out_specs=[vmem] * len(shapes),
        out_shape=[jax.ShapeDtypeStruct(shape, F32) for shape in shapes],
        name="spread",
    )(out_grad, step_grad, gate_grad, inner_grad, state_grad, small)


def finish_kernel(
    place_ref,
    x_ref,
    own_x_ref,
    own_cot_ref,
    part_ref,
    branch_ref,
    sums_ref,
    mean_ref,
    gain_ref,
    output_ref,
    grad_ref,
):
    hidden = x_ref[...].astype(F32)
    inv = lax.rsqrt(jnp.mean(hidden * hidden, axis=1, keepdims=True) + EPSILON)
    own = own_x_ref[...].astype(F32)
    gate_inv = lax.rsqrt(column_of(sums_ref[0:1]) / INNER + EPSILON)
    output_ref[...] = (own + gate_inv * branch_ref[...].astype(F32)).astype(BF16)
    mean = column_of(mean_ref[0:1]) / MODEL_WIDTH
    scaled = part_ref[...].astype(F32) * gain_ref[...]
    grad_ref[...] = own_cot_ref[...].astype(F32) + inv * scaled - own * (inv * inv * inv * mean)


def finish_pass(place, x, cot, part, branch, sums, mean, gain):
    tokens, share = part.shape

    def chunk(width):
        return pl.BlockSpec((SPAN, width), lambda i, place: (i, 0))

    own = pl.BlockSpec((SPAN, share), lambda i, place: (i, place[0]))
    rows = pl.BlockSpec((8, SPAN), lambda i, place: (0, i))
    return pl.pallas_call(
        finish_kernel,
        grid_spec=pltpu.PrefetchScalarGridSpec(
            num_scalar_prefetch=1,
            grid=(tokens // SPAN,),
            in_specs=[
                chunk(MODEL_WIDTH),
                own,
                own,
                chunk(share),
                chunk(share),
                rows,
                rows,
                pl.BlockSpec((1, share), lambda i, place: (0, place[0])),
            ],
            out_specs=[chunk(share), chunk(share)],
        ),
        out_shape=[
            jax.ShapeDtypeStruct((tokens, share), BF16),
            jax.ShapeDtypeStruct((tokens, share), F32),
        ],
        compiler_params=pltpu.CompilerParams(vmem_limit_bytes=VMEM_LIMIT),
        name="finish",
    )(place, x, x, cot, part, branch, sums, mean, gain)


def prep_kernel(
    heads,
    gate_ref,
    out_ref,
    input_ref,
    state_ref,
    step_ref,
    flags_ref,
    inner_taps_ref,
    state_taps_ref,
    inner_bias_ref,
    state_bias_ref,
    params_ref,
    early_ref,
    late_ref,
    flags_out_ref,
    marks_ref,
    taps_ref,
    bias_ref,
    step_bias_ref,
    decay_ref,
    skip_ref,
    shifted,
):
    channels = heads * HEADDIM
    depth = gate_ref.shape[0]
    main = channels + 2 * STATE
    early_ref[:, :channels] = gate_ref[...]
    early_ref[:, channels:] = out_ref[...].astype(F32).T.astype(BF16)
    late_ref[:, :channels] = input_ref[...]
    late_ref[:, channels:main] = state_ref[...]
    steps = jnp.concatenate([step_ref[...].astype(F32), jnp.zeros((LANES - heads, depth), F32)], axis=0)
    late_ref[:, main:] = steps.T.astype(BF16)
    flags = flags_ref[...].astype(F32)
    flags_out_ref[...] = flags
    blocks = flags.shape[0]
    shifted[0:8] = jnp.zeros((8, LANES), F32)
    for i in range(blocks):
        shifted[8 + i * LANES : 8 + (i + 1) * LANES] = jnp.broadcast_to(flags[i : i + 1], (LANES, LANES)).T
    lane = iota((LANES, LANES), 1)
    for i in range(blocks):
        at = 8 + i * LANES
        own = shifted[at : at + LANES]
        lag1 = 1.0 - own
        lag2 = lag1 * (1.0 - shifted[at - 1 : at - 1 + LANES])
        lag3 = lag2 * (1.0 - shifted[at - 2 : at - 2 + LANES])
        marks_ref[i * LANES : (i + 1) * LANES] = jnp.where(
            lane == 0, own, jnp.where(lane == 1, lag1, jnp.where(lane == 2, lag2, lag3))
        )
    taps_ref[:, :channels] = inner_taps_ref[...]
    taps_ref[:, channels:] = state_taps_ref[...]
    for i in range(channels // LANES):
        bias_ref[:, i * LANES : (i + 1) * LANES] = inner_bias_ref[i : i + 1]
    for i in range(2 * STATE // LANES):
        at = channels + i * LANES
        bias_ref[:, at : at + LANES] = state_bias_ref[i : i + 1]
    params = params_ref[...]
    step_bias_ref[...] = params[0:1]
    decay_ref[...] = params[1:2]
    skips = [jnp.broadcast_to(params[2:3, h : h + 1], (1, HEADDIM)) for h in range(heads)]
    skip_ref[...] = jnp.concatenate(skips, axis=1)


def prepare(
    gate_proj, out_proj, input_proj, state_proj, step_proj, first, taps, state_taps, bias, state_bias, params, heads
):
    depth, channels = gate_proj.shape
    main = channels + 2 * STATE
    tokens = first.shape[0]
    vmem = pl.BlockSpec(memory_space=pltpu.VMEM)
    out = jax.ShapeDtypeStruct
    return pl.pallas_call(
        lambda *refs: prep_kernel(heads, *refs),
        in_specs=[vmem] * 11,
        out_specs=[vmem] * 9,
        out_shape=[
            out((depth, 2 * channels), BF16),
            out((depth, main + LANES), BF16),
            out((tokens // LANES, LANES), F32),
            out((tokens, LANES), F32),
            out((KCONV, main), F32),
            out((1, main), F32),
            out((1, LANES), F32),
            out((1, LANES), F32),
            out((1, channels), F32),
        ],
        scratch_shapes=[pltpu.VMEM((tokens + 8, LANES), F32)],
        compiler_params=pltpu.CompilerParams(vmem_limit_bytes=VMEM_LIMIT),
        name="prepare",
    )(
        gate_proj,
        out_proj,
        input_proj,
        state_proj,
        step_proj.T,
        first.reshape(-1, LANES),
        taps,
        state_taps,
        bias.reshape(-1, LANES),
        state_bias.reshape(-1, LANES),
        params,
    )


MESH = pl.DeviceIdType.MESH


def remote(source, target, sends, receives, place):
    return pltpu.make_async_remote_copy(
        src_ref=source,
        dst_ref=target,
        send_sem=sends,
        recv_sem=receives,
        device_id=place,
        device_id_type=MESH,
    )


def greet(places):
    barrier = pltpu.get_barrier_semaphore()
    for place in places:
        pl.semaphore_signal(barrier, inc=1, device_id=place, device_id_type=MESH)
    pl.semaphore_wait(barrier, len(places))


def peers_of(axis):
    size, me = lax.axis_size(axis), lax.axis_index(axis)
    return [lax.rem(me + off, size) for off in range(1, size)]


def gather_kernel(count, *refs):
    shards, (x_ref, flags_ref) = refs[:count], refs[count : count + 2]
    outs, (halo_ref, other_flags_ref) = refs[count + 2 : 2 * count + 2], refs[2 * count + 2 : 2 * count + 4]
    send, receive, pass_send, pass_receive, own_sem, side_send, side_receive = refs[2 * count + 4 :]
    size, me = lax.axis_size("dp"), lax.axis_index("dp")
    core = lax.axis_index("ctx")
    partner = {"ctx": 1 - core}
    peers = peers_of("dp")
    greet([partner] + [{"dp": p} for p in peers])

    def rows(out, owner):
        depth = out.shape[0] // (2 * size)
        return out.at[pl.ds(pl.multiple_of((owner * 2 + core) * depth, depth), depth)]

    last = x_ref.shape[0] - 16
    waits = [
        remote(x_ref.at[pl.ds(last, 16)], halo_ref, side_send.at[0], side_receive.at[0], partner),
        remote(flags_ref, other_flags_ref, side_send.at[1], side_receive.at[1], partner),
    ]
    for copy in waits:
        copy.start()
    arriving, local = [], []
    for k in range(count):
        for off in range(size - 1, 0, -1):
            copy = remote(
                shards[k],
                rows(outs[k], me),
                send.at[k, off - 1],
                receive.at[k, off - 1],
                {"dp": peers[off - 1]},
            )
            copy.start()
            arriving.append((k, off, copy))
        copy = remote(shards[k], rows(outs[k], me), pass_send.at[k, 0], pass_receive.at[k, 0], partner)
        copy.start()
        waits.append(copy)
        copy = pltpu.make_async_copy(shards[k], rows(outs[k], me), own_sem.at[k])
        copy.start()
        local.append(copy)
    for k, off, copy in arriving:
        copy.wait_recv()
        block = rows(outs[k], lax.rem(me + size - off, size))
        onward = remote(block, block, pass_send.at[k, off], pass_receive.at[k, off], partner)
        onward.start()
        waits.append(onward)
    for copy in local + waits:
        copy.wait()
    for _, _, copy in arriving:
        copy.wait_send()


def gather(shards, x, flags, collective_id):
    size, count = lax.axis_size("dp"), len(shards)
    anywhere = pl.BlockSpec(memory_space=pl.ANY)
    dma = pltpu.SemaphoreType.DMA
    return pl.pallas_call(
        lambda *refs: gather_kernel(count, *refs),
        in_specs=[anywhere] * (count + 2),
        out_specs=[anywhere] * (count + 2),
        out_shape=[jax.ShapeDtypeStruct((s.shape[0] * 2 * size, s.shape[1]), s.dtype) for s in shards]
        + [jax.ShapeDtypeStruct((16, x.shape[1]), x.dtype), jax.ShapeDtypeStruct(flags.shape, flags.dtype)],
        scratch_shapes=[
            dma((count, size - 1)),
            dma((count, size - 1)),
            dma((count, size)),
            dma((count, size)),
            dma((count,)),
            dma((2,)),
            dma((2,)),
        ],
        compiler_params=pltpu.CompilerParams(collective_id=collective_id, has_side_effects=True),
        name="gather",
    )(*shards, x, flags)


def add_rows(out, terms, step_rows, first=0, width=None):
    rows = out.shape[0]
    columns = slice(None) if width is None else pl.ds(first, width)

    def add(step, carry):
        at = pl.ds(pl.multiple_of(step * step_rows, step_rows), step_rows)
        total = terms[0][at, columns].astype(F32)
        for term in terms[1:]:
            total = total + term[at, columns].astype(F32)
        out[at, :] = total.astype(out.dtype)
        return carry

    lax.fori_loop(0, rows // step_rows, add, 0)


def mid_kernel(
    heads,
    normed_hbm,
    cot_hbm,
    local_hbm,
    early_hbm,
    passing_ref,
    out_map_ref,
    final_ref,
    gain_ref,
    gated_hbm,
    grad_mixed_hbm,
    grad_gate_hbm,
    branch_hbm,
    carried_ref,
    following_ref,
    sums_ref,
    grad_gain_ref,
    normed,
    cot,
    mixed,
    early,
    gate,
    back,
    branch,
    gated_out,
    grad_gate_out,
    own_sums,
    arriving,
    through,
    in_sem,
    out_sem,
    side_send,
    side_receive,
    send,
    receive,
):
    channels = heads * HEADDIM
    tokens = normed.shape[0]
    spans = tokens // SPAN
    core = lax.axis_index("ctx")
    partner = {"ctx": 1 - core}
    peers = peers_of("tp")
    loads = [
        pltpu.make_async_copy(source, target, in_sem.at[i])
        for i, (source, target) in enumerate(
            ((early_hbm, early), (cot_hbm, cot), (normed_hbm, normed), (local_hbm, mixed))
        )
    ]
    for copy in loads:
        copy.start()
    greet([partner] + [{"tp": p} for p in peers])
    carry = remote(final_ref, carried_ref, side_send.at[0], side_receive.at[0], partner)
    carry.start()
    loads[0].wait()
    loads[1].wait()
    loads[2].wait()

    def rows_at(i):
        return pl.ds(pl.multiple_of(i * SPAN, SPAN), SPAN)

    def project(i, carry_on):
        at = rows_at(i)
        back[at, :] = dot_nn(cot[at, :], early[:, channels:])
        gate[at, :] = dot_nn(normed[at, :], early[:, :channels])
        return carry_on

    lax.fori_loop(0, spans, project, 0)
    loads[3].wait()
    carry.wait_recv()
    carried = carried_ref[...] * jnp.where(core > 0, 1.0, 0.0)
    carried_ref[...] = carried
    carried = carried.astype(BF16)
    gain = gain_ref[...]

    def out(source, target, at, sem):
        return pltpu.make_async_copy(source.at[at], target.at[at], sem)

    def gating(i, carry_on):
        at = rows_at(i)
        whole_mixed = mixed[at, :] + widen(passing_ref[at, :], heads, channels) * dot_nt(
            out_map_ref[at, :], carried
        )
        mixed[at, :] = whole_mixed
        own_gate = gate[at, :]
        gated = whole_mixed * (own_gate * sigmoid(own_gate))
        weighed = gated * gain
        branch[at, :] = dot_nt(weighed.astype(BF16), early[:, channels:]).astype(BF16)
        out(branch, branch_hbm, at, out_sem.at[0, i]).start()
        own_sums[:, at] = jnp.where(
            iota((8, SPAN), 0) < 4, row_sum(gated * gated), row_sum(weighed * back[at, :])
        )
        return carry_on

    lax.fori_loop(0, spans, gating, 0)
    copies = []
    for i, p in enumerate(peers):
        copies.append(remote(own_sums, arriving.at[i], send.at[i], receive.at[i], {"tp": p}))
        copies[-1].start()
    through[...] = jnp.zeros_like(through)
    grad_gain_ref[...] = jnp.zeros_like(grad_gain_ref)
    for copy in copies:
        copy.wait_recv()
    total = own_sums[...]
    for i in range(len(peers)):
        total = total + arriving[i]
    sums_ref[...] = total

    def middle(i, carry_on):
        at = rows_at(i)
        inv = lax.rsqrt(column_of(sums_ref[0:1, at]) / INNER + EPSILON)
        cross = column_of(sums_ref[4:5, at])
        own_gate, own_mixed, own_back = gate[at, :], mixed[at, :], back[at, :]
        sig = sigmoid(own_gate)
        gate_silu = own_gate * sig
        normal = own_mixed * gate_silu * inv
        gated_out[at, :] = (normal * gain).astype(BF16)
        grad_gated = inv * (own_back * gain) - normal * (inv * inv * (cross / INNER))
        grad_mixed = grad_gated * gate_silu
        grad_gate = grad_gated * own_mixed * sig * (1.0 + own_gate * (1.0 - sig))
        grad_gate_out[at, :] = grad_gate.astype(BF16)
        reaching = (grad_mixed * widen(passing_ref[at, :], heads, channels)).astype(BF16)
        through[...] += dot_tn(reaching, out_map_ref[at, :])
        grad_gain_ref[0:1, :] += jnp.sum(own_back * normal, axis=0, keepdims=True)
        back[at, :] = grad_mixed
        out(back, grad_mixed_hbm, at, out_sem.at[1, i]).start()
        out(gated_out, gated_hbm, at, out_sem.at[2, i]).start()
        out(grad_gate_out, grad_gate_hbm, at, out_sem.at[3, i]).start()
        return carry_on

    lax.fori_loop(0, spans, middle, 0)
    follow = remote(through, following_ref, side_send.at[1], side_receive.at[1], partner)
    follow.start()
    follow.wait_recv()
    following_ref[...] = following_ref[...] * jnp.where(core > 0, 0.0, 1.0)

    def finished(i, carry_on):
        at = rows_at(i)
        out(branch, branch_hbm, at, out_sem.at[0, i]).wait()
        out(back, grad_mixed_hbm, at, out_sem.at[1, i]).wait()
        out(gated_out, gated_hbm, at, out_sem.at[2, i]).wait()
        out(grad_gate_out, grad_gate_hbm, at, out_sem.at[3, i]).wait()
        return carry_on

    lax.fori_loop(0, spans, finished, 0)
    for copy in copies + [carry, follow]:
        copy.wait_send()


def mid_pass(normed, cot, local, early, passing, out_map, final_state, gain, heads, collective_id):
    tokens = normed.shape[0]
    channels = heads * HEADDIM
    spans = tokens // SPAN
    others = lax.axis_size("tp") - 1
    anywhere = pl.BlockSpec(memory_space=pl.ANY)
    vmem = pl.BlockSpec(memory_space=pltpu.VMEM)
    dma = pltpu.SemaphoreType.DMA
    out = jax.ShapeDtypeStruct
    return pl.pallas_call(
        lambda *refs: mid_kernel(heads, *refs),
        in_specs=[anywhere] * 4 + [vmem] * 4,
        out_specs=[anywhere] * 4 + [vmem] * 4,
        out_shape=[
            out((tokens, channels), BF16),
            out((tokens, channels), F32),
            out((tokens, channels), BF16),
            out((tokens, MODEL_WIDTH), BF16),
            out((channels, STATE), F32),
            out((channels, STATE), F32),
            out((8, tokens), F32),
            out((8, channels), F32),
        ],
        scratch_shapes=[
            pltpu.VMEM(normed.shape, BF16),
            pltpu.VMEM(cot.shape, BF16),
            pltpu.VMEM(local.shape, F32),
            pltpu.VMEM(early.shape, BF16),
            pltpu.VMEM(local.shape, F32),
            pltpu.VMEM(local.shape, F32),
            pltpu.VMEM((tokens, MODEL_WIDTH), BF16),
            pltpu.VMEM(local.shape, BF16),
            pltpu.VMEM(local.shape, BF16),
            pltpu.VMEM((8, tokens), F32),
            pltpu.VMEM((others, 8, tokens), F32),
            pltpu.VMEM((channels, STATE), F32),
            dma((4,)),
            dma((4, spans)),
            dma((2,)),
            dma((2,)),
            dma((others,)),
            dma((others,)),
        ],
        compiler_params=pltpu.CompilerParams(
            collective_id=collective_id, has_side_effects=True, vmem_limit_bytes=VMEM_LIMIT
        ),
        cost_estimate=pl.CostEstimate(
            flops=6 * tokens * MODEL_WIDTH * channels,
            bytes_accessed=16 * 2**20,
            transcendentals=2 * tokens * channels,
        ),
        name="middle",
    )(normed, cot, local, early, passing, out_map, final_state, gain)


def final_kernel(count, local_inner, shared, *refs):
    mean_ref, small_ref = refs[:2]
    wide_refs = refs[2 : 2 + count]
    mean_out_ref, gate_ref, out_ref, inner_ref, state_ref, step_ref, small_out_ref = refs[2 + count : 9 + count]
    scratch = refs[9 + count :]
    wide = [(wide_refs[k],) + tuple(scratch[3 * k : 3 * k + 3]) for k in range(count)]
    (
        mean_in,
        small_in,
        small_sum,
        small_far,
        shared_own,
        shared_in,
        state_own,
        state_in,
        z_send,
        z_receive,
        near_send,
        near_receive,
        far_send,
        far_receive,
        own_sem,
        small_send,
        small_receive,
    ) = scratch[3 * count :]
    size, me = lax.axis_size("dp"), lax.axis_index("dp")
    line = lax.axis_size("tp")
    core = lax.axis_index("ctx")
    partner = {"ctx": 1 - core}
    dp_peers, tp_peers = peers_of("dp"), peers_of("tp")
    greet([partner] + [{"dp": p} for p in dp_peers] + [{"tp": p} for p in tp_peers])
    near, local = {}, {}
    order = list(range(1, size)) + [0]
    for off in order:
        owner = lax.rem(me + off, size)
        for k, (grads, own, arriving, _) in enumerate(wide):
            depth = grads.shape[0] // (2 * size)

            def block(c, grads=grads, depth=depth, owner=owner):
                return grads.at[pl.ds(pl.multiple_of((owner * 2 + c) * depth, depth), depth)]

            near[off, k] = remote(
                block(1 - core), arriving.at[off], near_send.at[k, off], near_receive.at[k, off], partner
            )
            near[off, k].start()
            local[off, k] = pltpu.make_async_copy(block(core), own.at[off], own_sem.at[k, off])
            local[off, k].start()
    small_near = remote(small_ref, small_in, small_send.at[0], small_receive.at[0], partner)
    small_near.start()
    z_copies = []
    for i in range(line - 1):
        z_copies.append(
            remote(mean_ref, mean_in.at[i], z_send.at[0, i], z_receive.at[0, i], {"tp": tp_peers[i]})
        )
        z_copies[-1].start()
    far = []
    for off in order:
        for k, (_, own, arriving, remote_in) in enumerate(wide):
            local[off, k].wait()
            near[off, k].wait_recv()
            add_rows(own.at[off], [own.at[off], arriving.at[off]], 16)
            if off > 0:
                copy = remote(
                    own.at[off],
                    remote_in.at[off - 1],
                    far_send.at[k, off - 1],
                    far_receive.at[k, off - 1],
                    {"dp": dp_peers[off - 1]},
                )
                copy.start()
                far.append(copy)
    small_near.wait_recv()
    small_sum[...] = small_ref[...] + small_in[...]
    small_copies = []
    for off in range(1, size):
        copy = remote(
            small_sum, small_far.at[off - 1], small_send.at[off], small_receive.at[off], {"dp": dp_peers[off - 1]}
        )
        copy.start()
        small_copies.append(copy)
    for copy in z_copies:
        copy.wait_recv()
    add_rows(mean_out_ref, [mean_ref] + [mean_in.at[i] for i in range(line - 1)], 8)
    for copy in small_copies:
        copy.wait_recv()
    total = small_sum[...]
    for off in range(1, size):
        total = total + small_far[off - 1]
    small_out_ref[...] = total
    shared_own[...] = total[:, -shared:]
    terms = [[own.at[0]] + [remote_in.at[i] for i in range(size - 1)] for _, own, _, remote_in in wide]
    for copy in far:
        copy.wait_recv()
    add_rows(state_own, terms[2], 16, local_inner, 2 * STATE)
    last = []
    for i in range(line - 1):
        place = {"tp": tp_peers[i]}
        last.append(remote(state_own, state_in.at[i], z_send.at[1, i], z_receive.at[1, i], place))
        last.append(remote(shared_own, shared_in.at[i], z_send.at[2, i], z_receive.at[2, i], place))
    for copy in last:
        copy.start()
    add_rows(gate_ref, terms[0], 16)
    add_rows(out_ref, terms[1], 16)
    add_rows(inner_ref, terms[2], 16, 0, local_inner)
    add_rows(step_ref, terms[2], 16, local_inner + 2 * STATE, LANES)
    for copy in last:
        copy.wait_recv()
    add_rows(state_ref, [state_own] + [state_in.at[i] for i in range(line - 1)], 16)
    total = shared_own[...]
    for i in range(line - 1):
        total = total + shared_in[i]
    small_out_ref[:, -shared:] = total
    for copy in z_copies + last + far + small_copies + [small_near] + list(near.values()):
        copy.wait_send()


def final_exchange(mean, small, wide, local_inner, shared, collective_id):
    size, line = lax.axis_size("dp"), lax.axis_size("tp")
    count = len(wide)
    depth = wide[0].shape[0] // (2 * size)
    anywhere = pl.BlockSpec(memory_space=pl.ANY)
    vmem = pl.BlockSpec(memory_space=pltpu.VMEM)
    dma = pltpu.SemaphoreType.DMA

    def out(*shape):
        return jax.ShapeDtypeStruct(shape, F32)

    slots = []
    for like in wide:
        for copies in (size, size, size - 1):
            slots.append(pltpu.VMEM((copies, depth, like.shape[1]), BF16))
    return pl.pallas_call(
        lambda *refs: final_kernel(count, local_inner, shared, *refs),
        in_specs=[vmem, vmem] + [anywhere] * count,
        out_specs=[vmem] * 7,
        out_shape=[
            out(*mean.shape),
            out(depth, local_inner),
            out(depth, local_inner),
            out(depth, local_inner),
            out(depth, 2 * STATE),
            out(depth, LANES),
            out(*small.shape),
        ],
        scratch_shapes=slots
        + [
            pltpu.VMEM((line - 1,) + mean.shape, F32),
            pltpu.VMEM(small.shape, F32),
            pltpu.VMEM(small.shape, F32),
            pltpu.VMEM((size - 1,) + small.shape, F32),
            pltpu.VMEM((8, shared), F32),
            pltpu.VMEM((line - 1, 8, shared), F32),
            pltpu.VMEM((depth, 2 * STATE), BF16),
            pltpu.VMEM((line - 1, depth, 2 * STATE), BF16),
            dma((3, line - 1)),
            dma((3, line - 1)),
            dma((count, size)),
            dma((count, size)),
            dma((count, size - 1)),
            dma((count, size - 1)),
            dma((count, size)),
            dma((size,)),
            dma((size,)),
        ],
        compiler_params=pltpu.CompilerParams(
            collective_id=collective_id, has_side_effects=True, vmem_limit_bytes=VMEM_LIMIT
        ),
        name="final_exchange",
    )(mean, small, *wide)


def on_device(
    block_input_activations,
    sequence_first_token,
    norm_gain,
    gate_proj,
    input_proj,
    step_proj,
    state_proj,
    conv_inner_weight,
    conv_inner_bias,
    conv_state_weight,
    conv_state_bias,
    step_bias,
    decay_log,
    skip_weight,
    gate_gain,
    out_proj,
    output_cotangent,
):
    everyone = ("dp", "ctx")
    x = block_input_activations
    local_inner = gate_proj.shape[1]
    heads = step_bias.shape[0]
    tokens = x.shape[0]
    main = local_inner + 2 * STATE
    params = jnp.pad(jnp.stack([step_bias, decay_log, skip_weight]), ((0, 5), (0, LANES - heads)))
    early_shard, late_shard, flags, marks, taps, bias, step_row, decay_row, skip_row = prepare(
        gate_proj,
        out_proj,
        input_proj,
        state_proj,
        step_proj,
        sequence_first_token,
        conv_inner_weight,
        conv_state_weight,
        conv_inner_bias,
        conv_state_bias,
        params,
        heads,
    )
    early_full = lax.all_gather(early_shard, everyone, axis=0, tiled=True)
    late_full, halo_x, other_flags = gather([late_shard], x, flags, 4)
    gain = norm_gain[None, :]
    gated_gain = gate_gain[None, :]
    (
        normed,
        rows,
        conv,
        mixed_local,
        cum,
        raw,
        passing,
        out_map,
        states,
        products,
        final_state,
        halo_rows,
    ) = front(
        x, marks, halo_x, other_flags, gain, late_full, taps, bias, step_row, decay_row, skip_row, heads
    )
    gated_normed, grad_mixed, grad_gate, branch_part, carried, following, sums, grad_gain_gate = mid_pass(
        normed, output_cotangent, mixed_local, early_full, passing, out_map, final_state, gated_gain, heads, 1
    )
    branch = lax.psum_scatter(branch_part, "tp", scatter_dimension=1, tiled=True)
    grad_out = dot_tn(output_cotangent, gated_normed).astype(BF16)
    grad_gate_weight = dot_tn(normed, grad_gate).astype(BF16)
    late, tail, halo_grad, conv_sums, head_sums = back_pass(
        grad_mixed,
        conv,
        rows,
        halo_rows,
        raw,
        cum,
        states,
        products,
        carried,
        following,
        taps,
        decay_row,
        skip_row,
        heads,
    )
    returned = passed_along(halo_grad, -1)
    tensor_part, mean_sum, gain_sums, late = input_pass(
        x, grad_gate, late, tail, returned, early_full, late_full, gain
    )
    own_grad = lax.psum_scatter(tensor_part, "tp", scatter_dimension=1, tiled=True)
    late_weight = dot_tn(normed, late).astype(BF16)
    shared = 2 * STATE + MODEL_WIDTH
    small = jnp.concatenate(
        [conv_sums[:, :local_inner], grad_gain_gate, head_sums, conv_sums[:, local_inner:], gain_sums], axis=1
    )
    mean_sum, gate_grad, out_grad, inner_grad, state_grad, step_grad, small = final_exchange(
        mean_sum, small, [grad_gate_weight, grad_out, late_weight], local_inner, shared, 2
    )
    place = lax.axis_index("tp")
    share = MODEL_WIDTH // lax.axis_size("tp")
    gain_grad = lax.dynamic_slice_in_dim(small[0], small.shape[1] - MODEL_WIDTH + place * share, share, 0)
    (
        out_grad,
        step_grad,
        gate_grad,
        inner_grad,
        state_grad,
        inner_taps,
        inner_bias,
        state_taps,
        state_bias,
        step_bias_grad,
        decay_grad,
        skip_grad,
        gate_gain_grad,
    ) = spread(out_grad, step_grad, gate_grad, inner_grad, state_grad, small, heads)
    block_output, input_grad = finish_pass(
        place.reshape(1), x, output_cotangent, own_grad, branch, sums, mean_sum, gain
    )
    return (
        block_output,
        input_grad,
        gain_grad,
        gate_grad,
        inner_grad,
        step_grad,
        state_grad,
        inner_taps,
        inner_bias[0],
        state_taps,
        state_bias[0],
        step_bias_grad[0],
        decay_grad[0],
        skip_grad[0],
        gate_gain_grad[0],
        out_grad,
    )


def solution(mesh):
    return jax.shard_map(
        on_device,
        mesh=mesh,
        in_specs=(
            P(("dp", "ctx"), None),
            P(("dp", "ctx")),
            P(),
            P(("dp", "ctx"), "tp"),
            P(("dp", "ctx"), "tp"),
            P(("dp", "ctx"), "tp"),
            P(("dp", "ctx"), None),
            P(None, "tp"),
            P("tp"),
            P(),
            P(),
            P("tp"),
            P("tp"),
            P("tp"),
            P("tp"),
            P("tp", ("dp", "ctx")),
            P(("dp", "ctx"), None),
        ),
        out_specs=(
            P(("dp", "ctx"), "tp"),
            P(("dp", "ctx"), "tp"),
            P("tp"),
            P(("dp", "ctx"), "tp"),
            P(("dp", "ctx"), "tp"),
            P(("dp", "ctx"), "tp"),
            P(("dp", "ctx"), None),
            P(None, "tp"),
            P("tp"),
            P(),
            P(),
            P("tp"),
            P("tp"),
            P("tp"),
            P("tp"),
            P("tp", ("dp", "ctx")),
        ),
        check_vma=False,
    )
```

```python
import jax
import jax.numpy as jnp
from jax import lax
from jax.experimental import pallas as pl
from jax.experimental.pallas import tpu as pltpu
from jax.sharding import PartitionSpec as P

MODEL_WIDTH = 1024
HEADDIM = 64
STATE = 128
KCONV = 4
SPAN = 256
INNER = 2048


EPSILON = 1e-05
HIGHEST = lax.Precision.HIGHEST


def passed_along(block, distance):
    devices = range(lax.axis_size("ctx"))
    route = [(i - distance, i) for i in devices if i - distance in devices]
    return lax.ppermute(block, "ctx", route)


LANES = 128
VMEM_LIMIT = 60 * 1024 * 1024
BF16 = jnp.bfloat16
F32 = jnp.float32
BLOCKED = -1e30


def dot_nn(a, b):
    return jnp.dot(a, b, preferred_element_type=F32)


def dot_nt(a, b):
    return lax.dot_general(a, b, (((1,), (1,)), ((), ())), preferred_element_type=F32)


def dot_tn(a, b):
    return lax.dot_general(a, b, (((0,), (0,)), ((), ())), preferred_element_type=F32)


def iota(shape, dim):
    return lax.broadcasted_iota(jnp.int32, shape, dim)


def high_low(a):
    high = a.astype(BF16)
    return high, (a - high.astype(F32)).astype(BF16)


def widen(a, heads, width):
    lane = iota(a.shape, 1)
    high = a.astype(BF16).astype(F32)
    low = pltpu.roll(a - high, heads, 1)
    packed = jnp.where(lane < heads, high, jnp.where(lane < 2 * heads, low, 0.0)).astype(BF16)
    row, column = iota((LANES, width), 0), iota((LANES, width), 1)
    place = jnp.where(row < heads, row, row - heads)
    return dot_nn(packed, (column // HEADDIM == place).astype(BF16))


def per_head_sum(a, heads):
    high, low = high_low(a)
    row, column = iota((LANES, a.shape[1]), 0), iota((LANES, a.shape[1]), 1)
    pick = (column // HEADDIM == row).astype(BF16)
    return dot_nt(high, pick) + dot_nt(low, pick)


def row_sum(a):
    folded = a[:, :LANES]
    for i in range(1, a.shape[1] // LANES):
        folded = folded + a[:, i * LANES : (i + 1) * LANES]
    return jnp.sum(folded.T, axis=0, keepdims=True)


def rows_of_heads(column, heads):
    return jnp.concatenate(
        [jnp.broadcast_to(column[h : h + 1, :], (HEADDIM, LANES)) for h in range(heads)], axis=0
    )


def column_of(row):
    return jnp.broadcast_to(row, (LANES, SPAN)).T[:, 0:1]


def sigmoid(v):
    return 0.5 * jnp.tanh(0.5 * v) + 0.5


def normalise(x, gain):
    hidden = x.astype(F32)
    inv = lax.rsqrt(jnp.mean(hidden * hidden, axis=1, keepdims=True) + EPSILON)
    return (hidden * inv * gain).astype(BF16)


def whole(shape):
    return pl.BlockSpec(shape, lambda i: (0,) * len(shape))


def columns_of(array, width, block):
    return pl.BlockSpec((array.shape[0], width), lambda i: (0, block))


def front_kernel(
    heads,
    x_ref,
    marks_ref,
    halo_x_ref,
    flags_ref,
    gain_ref,
    weight_ref,
    taps_ref,
    bias_ref,
    step_bias_ref,
    decay_ref,
    skip_ref,
    normed_ref,
    rows_ref,
    conv_ref,
    mixed_ref,
    cum_ref,
    raw_ref,
    passing_ref,
    out_map_ref,
    states_ref,
    products_ref,
    final_ref,
    halo_rows_ref,
    state,
    product,
    before,
):
    step = pl.program_id(0)
    channels = heads * HEADDIM
    main = channels + 2 * STATE
    gain = gain_ref[...]

    @pl.when(step == 0)
    def _():
        state[...] = jnp.zeros_like(state)
        product[...] = jnp.ones_like(product)
        halo = dot_nn(normalise(halo_x_ref[...], gain), weight_ref[:, :main]).astype(BF16)
        halo_rows_ref[...] = halo
        before[...] = halo.astype(F32)[8:16]

    normed = normalise(x_ref[...], gain)
    normed_ref[...] = normed
    projected = dot_nn(normed, weight_ref[...])
    rows = projected[:, :main].astype(BF16)
    rows_ref[...] = rows
    rows = rows.astype(F32)
    raw = projected[:, main:] + step_bias_ref[...]
    extended = jnp.concatenate([before[...], rows], axis=0)
    before[...] = rows[SPAN - 8 :]
    taps = taps_ref[...]
    conv = bias_ref[...] + taps[0:1] * rows
    lane = iota((SPAN, LANES), 1)
    boundary = jnp.where(step == 0, flags_ref[flags_ref.shape[0] - 1 :, LANES - KCONV :], 0.0)
    reach = 1.0 - boundary
    at_first, at_second = iota((SPAN, 1), 0) == 0, iota((SPAN, 1), 0) == 1
    nearest, second = reach[:, KCONV - 1 :], reach[:, KCONV - 2 : KCONV - 1]
    edges = [
        None,
        None,
        jnp.where(at_first, nearest, 1.0),
        jnp.where(at_first, nearest * second, jnp.where(at_second, nearest, 1.0)),
    ]
    for lag in range(1, KCONV):
        valid = marks_ref[:, lag : lag + 1]
        if edges[lag] is not None:
            valid = valid * edges[lag]
        raw = jnp.where(lane == heads + lag, valid, raw)
        conv = conv + (taps[lag : lag + 1] * extended[8 - lag : 8 - lag + SPAN]) * valid
    raw_ref[...] = raw
    conv_ref[...] = conv
    act = conv * sigmoid(conv)
    values = act[:, :channels]
    map_in = act[:, channels : channels + STATE].astype(BF16)
    map_out = act[:, channels + STATE :].astype(BF16)
    out_map_ref[...] = map_out

    step_size = jnp.maximum(raw, 0.0) + jnp.log1p(jnp.exp(-jnp.abs(raw)))
    log_decay = jnp.where(lane < heads, step_size * (-jnp.exp(decay_ref[...])), 0.0)
    series = jnp.where(lane == heads, marks_ref[:, 0:1], log_decay)
    t, s = iota((SPAN, SPAN), 0), iota((SPAN, SPAN), 1)
    cum = jnp.dot((t >= s).astype(F32), series, precision=HIGHEST, preferred_element_type=F32)
    cum_ref[...] = cum
    cum_rows = cum.T
    segment, segment_row = cum[:, heads : heads + 1], cum_rows[heads : heads + 1, :]
    blocked = jnp.where((segment == segment_row) & (t >= s), 0.0, BLOCKED)
    passing = jnp.where(segment == 0.0, jnp.exp(cum), 0.0)
    product_now = product[...]
    passing_ref[...] = passing * product_now[0:1]
    products_ref[0] = product_now
    product[...] = product_now * passing[SPAN - 1 : SPAN]
    to_end = jnp.where(
        segment == cum[SPAN - 1 : SPAN, heads : heads + 1], jnp.exp(cum[SPAN - 1 : SPAN] - cum), 0.0
    )
    stepped = values * widen(step_size, heads, channels)
    state_now = state[...]
    states_ref[0] = state_now
    scores = dot_nt(map_out, map_in)
    through = widen(passing, heads, channels) * dot_nt(map_out, state_now.astype(BF16))
    half = iota((SPAN, LANES), 1) < HEADDIM
    for pair in range(heads // 2):
        at = slice(pair * LANES, (pair + 1) * LANES)
        both = stepped[:, at]
        total = through[:, at] + skip_ref[:, at] * values[:, at]
        for side in range(2):
            h = 2 * pair + side
            spread = cum[:, h : h + 1] - cum_rows[h : h + 1, :]
            mixing = (jnp.exp(spread + blocked) * scores).astype(BF16)
            own = jnp.where(half if side == 0 else ~half, both, 0.0).astype(BF16)
            total = total + dot_nn(mixing, own)
        mixed_ref[:, at] = total
    ending = (stepped * widen(to_end, heads, channels)).astype(BF16)
    fresh = dot_tn(ending, map_in)
    kept = jnp.where(segment_row[:, SPAN - 1 :] == 0.0, jnp.exp(cum_rows[:, SPAN - 1 :]), 0.0)
    state_next = rows_of_heads(kept, heads) * state_now + fresh
    state[...] = state_next
    final_ref[...] = state_next


def front(x, marks, halo_x, flags, gain, weight, taps, bias, step_bias, decay, skip, heads):
    tokens = x.shape[0]
    channels = heads * HEADDIM
    main = channels + 2 * STATE
    spans = tokens // SPAN

    def chunk(width):
        return pl.BlockSpec((SPAN, width), lambda i: (i, 0))

    def out(shape, dtype):
        return jax.ShapeDtypeStruct(shape, dtype)

    return pl.pallas_call(
        lambda *refs: front_kernel(heads, *refs),
        grid=(spans,),
        in_specs=[
            chunk(MODEL_WIDTH),
            chunk(LANES),
            whole(halo_x.shape),
            whole(flags.shape),
            whole(gain.shape),
            whole(weight.shape),
            whole(taps.shape),
            whole(bias.shape),
            whole(step_bias.shape),
            whole(decay.shape),
            whole(skip.shape),
        ],
        out_specs=[
            chunk(MODEL_WIDTH),
            chunk(main),
            chunk(main),
            chunk(channels),
            chunk(LANES),
            chunk(LANES),
            chunk(LANES),
            chunk(STATE),
            pl.BlockSpec((1, channels, STATE), lambda i: (i, 0, 0)),
            pl.BlockSpec((1, 8, LANES), lambda i: (i, 0, 0)),
            whole((channels, STATE)),
            whole((16, main)),
        ],
        out_shape=[
            out((tokens, MODEL_WIDTH), BF16),
            out((tokens, main), BF16),
            out((tokens, main), F32),
            out((tokens, channels), F32),
            out((tokens, LANES), F32),
            out((tokens, LANES), F32),
            out((tokens, LANES), F32),
            out((tokens, STATE), BF16),
            out((spans, channels, STATE), F32),
            out((spans, 8, LANES), F32),
            out((channels, STATE), F32),
            out((16, main), BF16),
        ],
        scratch_shapes=[
            pltpu.VMEM((channels, STATE), F32),
            pltpu.VMEM((8, LANES), F32),
            pltpu.VMEM((8, main), F32),
        ],
        compiler_params=pltpu.CompilerParams(vmem_limit_bytes=VMEM_LIMIT),
        cost_estimate=pl.CostEstimate(
            flops=2 * tokens * (MODEL_WIDTH * weight.shape[1] + 4 * SPAN * channels),
            bytes_accessed=18 * 2**20,
            transcendentals=tokens * SPAN * heads,
        ),
        name="scan_front",
    )(x, marks, halo_x, flags, gain, weight, taps, bias, step_bias, decay, skip)


def back_kernel(
    heads,
    grad_ref,
    conv_ref,
    rows_ref,
    earlier_ref,
    halo_ref,
    raw_ref,
    cum_ref,
    states_ref,
    products_ref,
    carried_ref,
    next_ref,
    taps_ref,
    decay_ref,
    skip_ref,
    late_ref,
    tail_ref,
    halo_grad_ref,
    sums_ref,
    head_sums_ref,
    flowing,
    after,
):
    step = pl.program_id(0)
    spans = pl.num_programs(0)
    channels = heads * HEADDIM
    main = channels + 2 * STATE

    @pl.when(step == 0)
    def _():
        flowing[...] = next_ref[...]
        after[...] = jnp.zeros_like(after)
        sums_ref[...] = jnp.zeros_like(sums_ref)
        head_sums_ref[...] = jnp.zeros_like(head_sums_ref)

    conv = conv_ref[...]
    sig = sigmoid(conv)
    act = conv * sig
    slope = sig * (1.0 + conv * (1.0 - sig))
    values = act[:, :channels]
    map_in = act[:, channels : channels + STATE].astype(BF16)
    map_out = act[:, channels + STATE :].astype(BF16)
    raw = raw_ref[...]
    step_size = jnp.maximum(raw, 0.0) + jnp.log1p(jnp.exp(-jnp.abs(raw)))
    cum = cum_ref[...]
    cum_rows = cum.T
    segment, segment_row = cum[:, heads : heads + 1], cum_rows[heads : heads + 1, :]
    s, t = iota((SPAN, SPAN), 0), iota((SPAN, SPAN), 1)
    blocked = jnp.where((segment == segment_row) & (t >= s), 0.0, BLOCKED)
    passing = jnp.where(segment == 0.0, jnp.exp(cum), 0.0)
    to_end = jnp.where(
        segment == cum[SPAN - 1 : SPAN, heads : heads + 1], jnp.exp(cum[SPAN - 1 : SPAN] - cum), 0.0
    )
    kept = jnp.where(segment_row[:, SPAN - 1 :] == 0.0, jnp.exp(cum_rows[:, SPAN - 1 :]), 0.0)
    product_column = jnp.broadcast_to(products_ref[0][0:1], (LANES, LANES)).T
    state = states_ref[0] + rows_of_heads(product_column[:, 0:1], heads) * carried_ref[...]
    state_bf = state.astype(BF16)
    flow = flowing[...]
    flow_bf = flow.astype(BF16)
    grad = grad_ref[...]
    step_wide = widen(step_size, heads, channels)
    end_wide = widen(to_end, heads, channels)
    stepped = values * step_wide
    stepped_bf = stepped.astype(BF16)
    grad_bf = grad.astype(BF16)
    reaching = grad * widen(passing, heads, channels)
    reaching_bf = reaching.astype(BF16)
    ending = stepped * end_wide
    ending_bf = ending.astype(BF16)
    from_state = dot_nt(map_out, state_bf)
    from_flow = dot_nt(map_in, flow_bf)
    scores = dot_nt(map_in, map_out)
    half = iota((SPAN, LANES), 1) < HEADDIM
    zero = jnp.zeros((SPAN, LANES), BF16)
    lane = iota((SPAN, LANES), 1)
    grad_scores = jnp.zeros((SPAN, SPAN), F32)
    out_sums = jnp.zeros((SPAN, LANES), F32)
    in_sums = []
    grad_stepped = []
    for pair in range(heads // 2):
        at = slice(pair * LANES, (pair + 1) * LANES)
        total = end_wide[:, at] * from_flow[:, at]
        for side in range(2):
            h = 2 * pair + side
            own = half if side == 0 else ~half
            decay = jnp.exp((cum_rows[h : h + 1, :] - cum[:, h : h + 1]) + blocked)
            own_grad = jnp.where(own, grad_bf[:, at], zero)
            total = total + dot_nn((decay * scores).astype(BF16), own_grad)
            flowed = decay * dot_nt(stepped_bf[:, at], own_grad)
            grad_scores = grad_scores + flowed
            weighed = flowed * scores
            in_sums.append(jnp.sum(weighed, axis=0, keepdims=True))
            out_sums = jnp.where(lane == h, jnp.sum(weighed, axis=1, keepdims=True), out_sums)
        grad_stepped.append(total)
    grad_stepped = jnp.concatenate(grad_stepped, axis=1)
    grad_scores = grad_scores.astype(BF16)
    grad_out_map = dot_tn(grad_scores, map_in) + dot_nn(reaching_bf, state_bf)
    grad_in_map = dot_nn(grad_scores, map_out) + dot_nn(ending_bf, flow_bf)
    ended = per_head_sum(ending * from_flow, heads)
    row, column = iota((LANES, channels), 0), iota((LANES, channels), 1)
    pick = (column // HEADDIM == row).astype(BF16)
    high, low = high_low(flow * state)
    at_last = kept * jnp.sum(dot_nn(pick, high) + dot_nn(pick, low), axis=1, keepdims=True)
    in_rows = jnp.concatenate(
        in_sums + [jnp.zeros((LANES - heads, SPAN), F32)], axis=0
    ) + jnp.where(iota((LANES, SPAN), 1) == SPAN - 1, at_last, 0.0)
    last = iota((SPAN, LANES), 0) == SPAN - 1
    grad_cum = (
        in_rows.T
        - out_sums
        + per_head_sum(reaching * from_state, heads)
        - ended
        + jnp.where(last, jnp.sum(ended, axis=0, keepdims=True), 0.0)
    )
    grad_log = jnp.dot((t >= s).astype(F32), grad_cum, precision=HIGHEST, preferred_element_type=F32)
    rate = -jnp.exp(decay_ref[...])
    grad_step = per_head_sum(grad_stepped * values, heads) + grad_log * rate
    grad_raw = jnp.where(lane < heads, grad_step * sigmoid(raw), 0.0)
    late_ref[:, main:] = grad_raw.astype(BF16)
    head_sums_ref[0:1] += jnp.sum(grad_raw, axis=0, keepdims=True)
    head_sums_ref[1:2] += jnp.sum(grad_log * step_size, axis=0, keepdims=True) * rate
    flowing[...] = rows_of_heads(kept, heads) * flow + dot_tn(reaching_bf, map_out)
    grad_values = grad_stepped * step_wide + skip_ref[...] * grad
    grad_act = jnp.concatenate([grad_values, grad_in_map, grad_out_map], axis=1)
    grad_conv = grad_act * slope
    sums_ref[5:6, :channels] += jnp.sum(grad * values, axis=0, keepdims=True)
    sums_ref[4:5] += jnp.sum(grad_conv, axis=0, keepdims=True)
    rows = rows_ref[...].astype(F32)
    first = step == spans - 1
    previous = jnp.where(first, halo_ref[...].astype(F32), earlier_ref[...].astype(F32))[8:16]
    extended = jnp.concatenate([previous, rows], axis=0)
    sums_ref[0:1] += jnp.sum(grad_conv * rows, axis=0, keepdims=True)
    taps = taps_ref[...]
    grad_rows = taps[0:1] * grad_conv
    halo_grad = jnp.zeros((8, main), F32)
    for lag in range(1, KCONV):
        valid = grad_conv * raw[:, heads + lag : heads + lag + 1]
        sums_ref[lag : lag + 1] += jnp.sum(
            valid * extended[8 - lag : 8 - lag + SPAN], axis=0, keepdims=True
        )
        tapped = taps[lag : lag + 1] * valid
        joined = jnp.concatenate([tapped, after[lag - 1]], axis=0)
        grad_rows = grad_rows + joined[lag : lag + SPAN]
        head = tapped[0:8]
        after[lag - 1] = head
        halo_grad = halo_grad + jnp.concatenate([jnp.zeros((8, main), F32), head], axis=0)[lag : lag + 8]
    late_ref[:, :main] = grad_rows.astype(BF16)
    halo_grad_ref[...] = halo_grad

    @pl.when(step == 0)
    def _():
        tail_ref[...] = grad_rows[SPAN - 16 :]


def back_pass(
    grad, conv, rows, halo, raw, cum, states, products, carried, following, taps, decay, skip, heads
):
    tokens = grad.shape[0]
    channels = heads * HEADDIM
    main = channels + 2 * STATE
    spans = tokens // SPAN

    def chunk(width):
        return pl.BlockSpec((SPAN, width), lambda i: (spans - 1 - i, 0))

    return pl.pallas_call(
        lambda *refs: back_kernel(heads, *refs),
        grid=(spans,),
        in_specs=[
            chunk(channels),
            chunk(main),
            chunk(main),
            pl.BlockSpec((16, main), lambda i: (jnp.maximum((spans - 1 - i) * (SPAN // 16) - 1, 0), 0)),
            whole(halo.shape),
            chunk(LANES),
            chunk(LANES),
            pl.BlockSpec((1, channels, STATE), lambda i: (spans - 1 - i, 0, 0)),
            pl.BlockSpec((1, 8, LANES), lambda i: (spans - 1 - i, 0, 0)),
            whole(carried.shape),
            whole(following.shape),
            whole(taps.shape),
            whole(decay.shape),
            whole(skip.shape),
        ],
        out_specs=[
            chunk(main + LANES),
            whole((16, main)),
            whole((8, main)),
            whole((8, main)),
            whole((8, LANES)),
        ],
        out_shape=[
            jax.ShapeDtypeStruct((tokens, main + LANES), BF16),
            jax.ShapeDtypeStruct((16, main), F32),
            jax.ShapeDtypeStruct((8, main), F32),
            jax.ShapeDtypeStruct((8, main), F32),
            jax.ShapeDtypeStruct((8, LANES), F32),
        ],
        scratch_shapes=[
            pltpu.VMEM((channels, STATE), F32),
            pltpu.VMEM((KCONV - 1, 8, main), F32),
        ],
        compiler_params=pltpu.CompilerParams(vmem_limit_bytes=VMEM_LIMIT),
        cost_estimate=pl.CostEstimate(
            flops=2 * tokens * 12 * SPAN * channels,
            bytes_accessed=12 * 2**20,
            transcendentals=tokens * SPAN * heads,
        ),
        name="scan_back",
    )(
        grad, conv, rows, rows, halo, raw, cum, states, products, carried, following, taps, decay, skip
    )


def input_kernel(
    x_ref,
    grad_gate_ref,
    late_ref,
    tail_ref,
    returned_ref,
    gate_weight_ref,
    late_weight_ref,
    gain_ref,
    part_ref,
    sums_ref,
    grad_gain_ref,
    whole_late_ref,
):
    step = pl.program_id(0)
    whole_late_ref[...] = late_ref[...]

    @pl.when(step == pl.num_programs(0) - 1)
    def _():
        main = tail_ref.shape[1]
        tail = tail_ref[...] + jnp.concatenate([jnp.zeros((8, main), F32), returned_ref[...]], axis=0)
        whole_late_ref[SPAN - 16 :, :main] = tail.astype(BF16)

    part = dot_nt(grad_gate_ref[...], gate_weight_ref[...])
    part = part + dot_nt(whole_late_ref[...], late_weight_ref[...])
    part_ref[...] = part.astype(BF16)
    hidden = x_ref[...].astype(F32)
    square = hidden * hidden
    inv = lax.rsqrt(jnp.mean(square, axis=1, keepdims=True) + EPSILON)
    term = part * hidden
    sums_ref[...] = jnp.where(iota((8, SPAN), 0) < 4, row_sum(term * gain_ref[...]), row_sum(square))
    gain_part = jnp.sum(term * inv, axis=0, keepdims=True)

    @pl.when(step == 0)
    def _():
        grad_gain_ref[...] = jnp.zeros_like(grad_gain_ref)

    grad_gain_ref[0:1] += gain_part


def input_pass(x, grad_gate, late, tail, returned, early_weight, late_weight, gain):
    tokens = x.shape[0]
    channels = grad_gate.shape[1]

    def chunk(width):
        return pl.BlockSpec((SPAN, width), lambda i: (i, 0))

    return pl.pallas_call(
        input_kernel,
        grid=(tokens // SPAN,),
        in_specs=[
            chunk(MODEL_WIDTH),
            chunk(channels),
            chunk(late.shape[1]),
            whole(tail.shape),
            whole(returned.shape),
            columns_of(early_weight, channels, 0),
            whole(late_weight.shape),
            whole(gain.shape),
        ],
        out_specs=[
            chunk(MODEL_WIDTH),
            pl.BlockSpec((8, SPAN), lambda i: (0, i)),
            whole((8, MODEL_WIDTH)),
            chunk(late.shape[1]),
        ],
        out_shape=[
            jax.ShapeDtypeStruct((tokens, MODEL_WIDTH), BF16),
            jax.ShapeDtypeStruct((8, tokens), F32),
            jax.ShapeDtypeStruct((8, MODEL_WIDTH), F32),
            jax.ShapeDtypeStruct(late.shape, BF16),
        ],
        compiler_params=pltpu.CompilerParams(vmem_limit_bytes=VMEM_LIMIT),
        cost_estimate=pl.CostEstimate(
            flops=2 * tokens * MODEL_WIDTH * (channels + late.shape[1]),
            bytes_accessed=12 * 2**20,
            transcendentals=0,
        ),
        name="input_pass",
    )(x, grad_gate, late, tail, returned, early_weight, late_weight, gain)


def spread_kernel(heads, out_ref, step_ref, gate_ref, inner_ref, state_ref, small_ref, *outs):
    channels = heads * HEADDIM
    out_out, step_out, gate_out, inner_out, state_out = outs[:5]
    taps_out, bias_out, state_taps_out, state_bias_out, step_bias_out, decay_out, skip_out, gain_out = outs[5:]
    out_out[...] = out_ref[...].T
    step_out[...] = step_ref[:, :heads]
    gate_out[...] = gate_ref[...]
    inner_out[...] = inner_ref[...]
    state_out[...] = state_ref[...]
    heads_at = 2 * channels
    state_at = heads_at + LANES
    taps_out[...] = small_ref[:KCONV, :channels]
    bias_out[...] = small_ref[KCONV : KCONV + 1, :channels]
    state_taps_out[...] = small_ref[:KCONV, state_at : state_at + 2 * STATE]
    state_bias_out[...] = small_ref[KCONV : KCONV + 1, state_at : state_at + 2 * STATE]
    step_bias_out[...] = small_ref[0:1, heads_at : heads_at + LANES][:, :heads]
    decay_out[...] = small_ref[1:2, heads_at : heads_at + LANES][:, :heads]
    skip_out[...] = per_head_sum(small_ref[:, :channels], heads)[5:6, :heads]
    gain_out[...] = small_ref[0:1, channels:heads_at]


def spread(out_grad, step_grad, gate_grad, inner_grad, state_grad, small, heads):
    depth = out_grad.shape[0]
    channels = heads * HEADDIM
    vmem = pl.BlockSpec(memory_space=pltpu.VMEM)
    shapes = [
        (channels, depth),
        (depth, heads),
        (depth, channels),
        (depth, channels),
        (depth, 2 * STATE),
        (KCONV, channels),
        (1, channels),
        (KCONV, 2 * STATE),
        (1, 2 * STATE),
        (1, heads),
        (1, heads),
        (1, heads),
        (1, channels),
    ]
    return pl.pallas_call(
        lambda *refs: spread_kernel(heads, *refs),
        in_specs=[vmem] * 6,
        out_specs=[vmem] * len(shapes),
        out_shape=[jax.ShapeDtypeStruct(shape, F32) for shape in shapes],
        name="spread",
    )(out_grad, step_grad, gate_grad, inner_grad, state_grad, small)


def output_kernel(place_ref, own_x_ref, branch_ref, sums_ref, output_ref):
    gate_inv = lax.rsqrt(column_of(sums_ref[0:1]) / INNER + EPSILON)
    output_ref[...] = (own_x_ref[...].astype(F32) + gate_inv * branch_ref[...].astype(F32)).astype(BF16)


def grad_kernel(line, place_ref, own_x_ref, own_cot_ref, part_ref, mean_ref, gain_ref, grad_ref):
    inv = lax.rsqrt(column_of(mean_ref[4:5]) / (line * MODEL_WIDTH) + EPSILON)
    mean = column_of(mean_ref[0:1]) / MODEL_WIDTH
    scaled = part_ref[...].astype(F32) * gain_ref[...]
    own = own_x_ref[...].astype(F32)
    grad_ref[...] = own_cot_ref[...].astype(F32) + inv * scaled - own * (inv * inv * inv * mean)


def finish_specs(share):
    chunk = pl.BlockSpec((SPAN, share), lambda i, place: (i, 0))
    own = pl.BlockSpec((SPAN, share), lambda i, place: (i, place[0]))
    rows = pl.BlockSpec((8, SPAN), lambda i, place: (0, i))
    return chunk, own, rows, pl.BlockSpec((1, share), lambda i, place: (0, place[0]))


def output_pass(place, x, branch, sums):
    tokens, share = branch.shape
    chunk, own, rows, _ = finish_specs(share)
    return pl.pallas_call(
        output_kernel,
        grid_spec=pltpu.PrefetchScalarGridSpec(
            num_scalar_prefetch=1,
            grid=(tokens // SPAN,),
            in_specs=[own, chunk, rows],
            out_specs=chunk,
        ),
        out_shape=jax.ShapeDtypeStruct((tokens, share), BF16),
        compiler_params=pltpu.CompilerParams(vmem_limit_bytes=VMEM_LIMIT),
        name="output_pass",
    )(place, x, branch, sums)


def grad_pass(place, x, cot, part, mean, gain, line):
    tokens, share = part.shape
    chunk, own, rows, gains = finish_specs(share)
    return pl.pallas_call(
        lambda *refs: grad_kernel(line, *refs),
        grid_spec=pltpu.PrefetchScalarGridSpec(
            num_scalar_prefetch=1,
            grid=(tokens // SPAN,),
            in_specs=[own, own, chunk, rows, gains],
            out_specs=chunk,
        ),
        out_shape=jax.ShapeDtypeStruct((tokens, share), F32),
        compiler_params=pltpu.CompilerParams(vmem_limit_bytes=VMEM_LIMIT),
        name="grad_pass",
    )(place, x, cot, part, mean, gain)


def prep_kernel(
    heads,
    gate_ref,
    out_ref,
    input_ref,
    state_ref,
    step_ref,
    flags_ref,
    inner_taps_ref,
    state_taps_ref,
    inner_bias_ref,
    state_bias_ref,
    params_ref,
    early_ref,
    late_ref,
    flags_out_ref,
    marks_ref,
    taps_ref,
    bias_ref,
    step_bias_ref,
    decay_ref,
    skip_ref,
    shifted,
):
    channels = heads * HEADDIM
    depth = gate_ref.shape[0]
    main = channels + 2 * STATE
    early_ref[:, :channels] = gate_ref[...]
    early_ref[:, channels:] = out_ref[...].astype(F32).T.astype(BF16)
    late_ref[:, :channels] = input_ref[...]
    late_ref[:, channels:main] = state_ref[...]
    steps = jnp.concatenate([step_ref[...].astype(F32), jnp.zeros((LANES - heads, depth), F32)], axis=0)
    late_ref[:, main:] = steps.T.astype(BF16)
    flags = flags_ref[...].astype(F32)
    flags_out_ref[...] = flags
    blocks = flags.shape[0]
    shifted[0:8] = jnp.zeros((8, LANES), F32)
    for i in range(blocks):
        shifted[8 + i * LANES : 8 + (i + 1) * LANES] = jnp.broadcast_to(flags[i : i + 1], (LANES, LANES)).T
    lane = iota((LANES, LANES), 1)
    for i in range(blocks):
        at = 8 + i * LANES
        own = shifted[at : at + LANES]
        lag1 = 1.0 - own
        lag2 = lag1 * (1.0 - shifted[at - 1 : at - 1 + LANES])
        lag3 = lag2 * (1.0 - shifted[at - 2 : at - 2 + LANES])
        marks_ref[i * LANES : (i + 1) * LANES] = jnp.where(
            lane == 0, own, jnp.where(lane == 1, lag1, jnp.where(lane == 2, lag2, lag3))
        )
    taps_ref[:, :channels] = inner_taps_ref[...]
    taps_ref[:, channels:] = state_taps_ref[...]
    for i in range(channels // LANES):
        bias_ref[:, i * LANES : (i + 1) * LANES] = inner_bias_ref[i : i + 1]
    for i in range(2 * STATE // LANES):
        at = channels + i * LANES
        bias_ref[:, at : at + LANES] = state_bias_ref[i : i + 1]
    params = params_ref[...]
    step_bias_ref[...] = params[0:1]
    decay_ref[...] = params[1:2]
    skips = [jnp.broadcast_to(params[2:3, h : h + 1], (1, HEADDIM)) for h in range(heads)]
    skip_ref[...] = jnp.concatenate(skips, axis=1)


def prepare(
    gate_proj, out_proj, input_proj, state_proj, step_proj, first, taps, state_taps, bias, state_bias, params, heads
):
    depth, channels = gate_proj.shape
    main = channels + 2 * STATE
    tokens = first.shape[0]
    vmem = pl.BlockSpec(memory_space=pltpu.VMEM)
    out = jax.ShapeDtypeStruct
    return pl.pallas_call(
        lambda *refs: prep_kernel(heads, *refs),
        in_specs=[vmem] * 11,
        out_specs=[vmem] * 9,
        out_shape=[
            out((depth, 2 * channels), BF16),
            out((depth, main + LANES), BF16),
            out((tokens // LANES, LANES), F32),
            out((tokens, LANES), F32),
            out((KCONV, main), F32),
            out((1, main), F32),
            out((1, LANES), F32),
            out((1, LANES), F32),
            out((1, channels), F32),
        ],
        scratch_shapes=[pltpu.VMEM((tokens + 8, LANES), F32)],
        compiler_params=pltpu.CompilerParams(vmem_limit_bytes=VMEM_LIMIT),
        name="prepare",
    )(
        gate_proj,
        out_proj,
        input_proj,
        state_proj,
        step_proj.T,
        first.reshape(-1, LANES),
        taps,
        state_taps,
        bias.reshape(-1, LANES),
        state_bias.reshape(-1, LANES),
        params,
    )


MESH = pl.DeviceIdType.MESH


def remote(source, target, sends, receives, place):
    return pltpu.make_async_remote_copy(
        src_ref=source,
        dst_ref=target,
        send_sem=sends,
        recv_sem=receives,
        device_id=place,
        device_id_type=MESH,
    )


def greet(places):
    barrier = pltpu.get_barrier_semaphore()
    for place in places:
        pl.semaphore_signal(barrier, inc=1, device_id=place, device_id_type=MESH)
    pl.semaphore_wait(barrier, len(places))


def peers_of(axis):
    size, me = lax.axis_size(axis), lax.axis_index(axis)
    return [lax.rem(me + off, size) for off in range(1, size)]


def gather_kernel(count, *refs):
    shards, (x_ref, flags_ref) = refs[:count], refs[count : count + 2]
    outs, (halo_ref, other_flags_ref) = refs[count + 2 : 2 * count + 2], refs[2 * count + 2 : 2 * count + 4]
    send, receive, pass_send, pass_receive, own_sem, side_send, side_receive = refs[2 * count + 4 :]
    size, me = lax.axis_size("dp"), lax.axis_index("dp")
    core = lax.axis_index("ctx")
    partner = {"ctx": 1 - core}
    peers = peers_of("dp")
    greet([partner] + [{"dp": p} for p in peers])

    def rows(out, owner):
        depth = out.shape[0] // (2 * size)
        return out.at[pl.ds(pl.multiple_of((owner * 2 + core) * depth, depth), depth)]

    last = x_ref.shape[0] - 16
    waits = [
        remote(x_ref.at[pl.ds(last, 16)], halo_ref, side_send.at[0], side_receive.at[0], partner),
        remote(flags_ref, other_flags_ref, side_send.at[1], side_receive.at[1], partner),
    ]
    for copy in waits:
        copy.start()
    arriving, local = [], []
    for k in range(count):
        for off in range(size - 1, 0, -1):
            copy = remote(
                shards[k],
                rows(outs[k], me),
                send.at[k, off - 1],
                receive.at[k, off - 1],
                {"dp": peers[off - 1]},
            )
            copy.start()
            arriving.append((k, off, copy))
        copy = remote(shards[k], rows(outs[k], me), pass_send.at[k, 0], pass_receive.at[k, 0], partner)
        copy.start()
        waits.append(copy)
        copy = pltpu.make_async_copy(shards[k], rows(outs[k], me), own_sem.at[k])
        copy.start()
        local.append(copy)
    for k, off, copy in arriving:
        copy.wait_recv()
        block = rows(outs[k], lax.rem(me + size - off, size))
        onward = remote(block, block, pass_send.at[k, off], pass_receive.at[k, off], partner)
        onward.start()
        waits.append(onward)
    for copy in local + waits:
        copy.wait()
    for _, _, copy in arriving:
        copy.wait_send()


def gather(shards, x, flags, collective_id):
    size, count = lax.axis_size("dp"), len(shards)
    anywhere = pl.BlockSpec(memory_space=pl.ANY)
    dma = pltpu.SemaphoreType.DMA
    return pl.pallas_call(
        lambda *refs: gather_kernel(count, *refs),
        in_specs=[anywhere] * (count + 2),
        out_specs=[anywhere] * (count + 2),
        out_shape=[jax.ShapeDtypeStruct((s.shape[0] * 2 * size, s.shape[1]), s.dtype) for s in shards]
        + [jax.ShapeDtypeStruct((16, x.shape[1]), x.dtype), jax.ShapeDtypeStruct(flags.shape, flags.dtype)],
        scratch_shapes=[
            dma((count, size - 1)),
            dma((count, size - 1)),
            dma((count, size)),
            dma((count, size)),
            dma((count,)),
            dma((2,)),
            dma((2,)),
        ],
        compiler_params=pltpu.CompilerParams(collective_id=collective_id, has_side_effects=True),
        name="gather",
    )(*shards, x, flags)


def add_rows(out, terms, step_rows, first=0, width=None):
    rows = out.shape[0]
    columns = slice(None) if width is None else pl.ds(first, width)

    def add(step, carry):
        at = pl.ds(pl.multiple_of(step * step_rows, step_rows), step_rows)
        total = terms[0][at, columns].astype(F32)
        for term in terms[1:]:
            total = total + term[at, columns].astype(F32)
        out[at, :] = total.astype(out.dtype)
        return carry

    lax.fori_loop(0, rows // step_rows, add, 0)


def chunk_rows(i):
    return pl.ds(pl.multiple_of(i * SPAN, SPAN), SPAN)


def moves(pairs, sems, outward):
    def move(k, i):
        hbm, vmem = pairs[k]
        source, target = (vmem, hbm) if outward else (hbm, vmem)
        return pltpu.make_async_copy(source.at[chunk_rows(i)], target.at[chunk_rows(i)], sems.at[k, i])

    return move


def each_span(spans, action):
    def body(i, carry_on):
        action(i)
        return carry_on

    lax.fori_loop(0, spans, body, 0)


def branch_kernel(
    heads,
    normed_hbm,
    local_hbm,
    early_hbm,
    cot_hbm,
    passing_ref,
    out_map_ref,
    final_ref,
    gain_ref,
    branch_hbm,
    gate_hbm,
    mixed_hbm,
    back_hbm,
    carried_ref,
    sums_ref,
    normed,
    mixed,
    early,
    cot,
    gate,
    back,
    weighed,
    branch,
    own_sums,
    arriving,
    in_sem,
    early_sem,
    out_sem,
    side_send,
    side_receive,
    send,
    receive,
):
    channels = heads * HEADDIM
    spans = normed.shape[0] // SPAN
    core = lax.axis_index("ctx")
    partner = {"ctx": 1 - core}
    peers = peers_of("tp")
    load = moves(((normed_hbm, normed), (cot_hbm, cot), (local_hbm, mixed)), in_sem, False)
    store = moves(
        ((branch_hbm, branch), (gate_hbm, gate), (mixed_hbm, mixed), (back_hbm, back)), out_sem, True
    )
    early_load = pltpu.make_async_copy(early_hbm, early, early_sem)
    early_load.start()
    for k in range(3):
        each_span(spans, lambda i, k=k: load(k, i).start())
    greet([partner] + [{"tp": p} for p in peers])
    carry = remote(final_ref, carried_ref, side_send, side_receive, partner)
    carry.start()
    early_load.wait()

    def project(i):
        load(0, i).wait()
        gate[chunk_rows(i), :] = dot_nn(normed[chunk_rows(i), :], early[:, :channels])
        store(1, i).start()
        load(1, i).wait()
        back[chunk_rows(i), :] = dot_nn(cot[chunk_rows(i), :], early[:, channels:])
        store(3, i).start()

    each_span(spans, project)
    carry.wait_recv()
    carried = carried_ref[...] * jnp.where(core > 0, 1.0, 0.0)
    carried_ref[...] = carried
    carried = carried.astype(BF16)
    gain = gain_ref[...]

    def gating(i):
        at = chunk_rows(i)
        load(2, i).wait()
        whole_mixed = mixed[at, :] + widen(passing_ref[at, :], heads, channels) * dot_nt(
            out_map_ref[at, :], carried
        )
        mixed[at, :] = whole_mixed
        store(2, i).start()
        own_gate = gate[at, :]
        gated = whole_mixed * (own_gate * sigmoid(own_gate))
        scaled = gated * gain
        weighed[at, :] = scaled.astype(BF16)
        own_sums[:, at] = jnp.where(
            iota((8, SPAN), 0) < 4, row_sum(gated * gated), row_sum(scaled * back[at, :])
        )

    each_span(spans, gating)
    copies = []
    for i, p in enumerate(peers):
        copies.append(remote(own_sums, arriving.at[i], send.at[i], receive.at[i], {"tp": p}))
        copies[-1].start()

    def branching(i):
        at = chunk_rows(i)
        branch[at, :] = dot_nt(weighed[at, :], early[:, channels:]).astype(BF16)
        store(0, i).start()

    each_span(spans, branching)
    for copy in copies:
        copy.wait_recv()
    total = own_sums[...]
    for i in range(len(peers)):
        total = total + arriving[i]
    sums_ref[...] = total
    for k in range(4):
        each_span(spans, lambda i, k=k: store(k, i).wait())
    for copy in copies + [carry]:
        copy.wait_send()


def branch_pass(normed, local, early, cot, passing, out_map, final_state, gain, heads, collective_id):
    tokens = normed.shape[0]
    channels = heads * HEADDIM
    spans = tokens // SPAN
    others = lax.axis_size("tp") - 1
    anywhere = pl.BlockSpec(memory_space=pl.ANY)
    vmem = pl.BlockSpec(memory_space=pltpu.VMEM)
    dma = pltpu.SemaphoreType.DMA
    out = jax.ShapeDtypeStruct
    return pl.pallas_call(
        lambda *refs: branch_kernel(heads, *refs),
        in_specs=[anywhere] * 4 + [vmem] * 4,
        out_specs=[anywhere] * 4 + [vmem] * 2,
        out_shape=[
            out((tokens, MODEL_WIDTH), BF16),
            out((tokens, channels), F32),
            out((tokens, channels), F32),
            out((tokens, channels), F32),
            out((channels, STATE), F32),
            out((8, tokens), F32),
        ],
        scratch_shapes=[
            pltpu.VMEM(normed.shape, BF16),
            pltpu.VMEM(local.shape, F32),
            pltpu.VMEM(early.shape, BF16),
            pltpu.VMEM(cot.shape, BF16),
            pltpu.VMEM(local.shape, F32),
            pltpu.VMEM(local.shape, F32),
            pltpu.VMEM(local.shape, BF16),
            pltpu.VMEM((tokens, MODEL_WIDTH), BF16),
            pltpu.VMEM((8, tokens), F32),
            pltpu.VMEM((others, 8, tokens), F32),
            dma((3, spans)),
            dma,
            dma((4, spans)),
            dma,
            dma,
            dma((others,)),
            dma((others,)),
        ],
        compiler_params=pltpu.CompilerParams(
            collective_id=collective_id, has_side_effects=True, vmem_limit_bytes=VMEM_LIMIT
        ),
        cost_estimate=pl.CostEstimate(
            flops=6 * tokens * MODEL_WIDTH * channels,
            bytes_accessed=14 * 2**20,
            transcendentals=tokens * channels,
        ),
        name="branch_pass",
    )(normed, local, early, cot, passing, out_map, final_state, gain)


def mid_kernel(
    heads,
    gate_hbm,
    mixed_hbm,
    back_hbm,
    sums_ref,
    passing_ref,
    out_map_ref,
    gain_ref,
    gated_hbm,
    grad_mixed_hbm,
    grad_gate_hbm,
    following_ref,
    grad_gain_ref,
    gate,
    mixed,
    back,
    gated_out,
    grad_gate_out,
    through,
    in_sem,
    out_sem,
    side_send,
    side_receive,
):
    channels = heads * HEADDIM
    spans = gate.shape[0] // SPAN
    core = lax.axis_index("ctx")
    partner = {"ctx": 1 - core}
    load = moves(((gate_hbm, gate), (mixed_hbm, mixed), (back_hbm, back)), in_sem, False)
    store = moves(
        ((grad_mixed_hbm, back), (gated_hbm, gated_out), (grad_gate_hbm, grad_gate_out)), out_sem, True
    )
    for i in range(spans):
        for k in range(3):
            load(k, i).start()
    greet([partner])
    gain = gain_ref[...]
    through[...] = jnp.zeros_like(through)
    grad_gain_ref[...] = jnp.zeros_like(grad_gain_ref)

    def middle(i):
        at = chunk_rows(i)
        for k in range(3):
            load(k, i).wait()
        inv = lax.rsqrt(column_of(sums_ref[0:1, at]) / INNER + EPSILON)
        cross = column_of(sums_ref[4:5, at])
        own_gate, own_mixed, own_back = gate[at, :], mixed[at, :], back[at, :]
        sig = sigmoid(own_gate)
        gate_silu = own_gate * sig
        normal = own_mixed * gate_silu * inv
        gated_out[at, :] = (normal * gain).astype(BF16)
        store(1, i).start()
        grad_gated = inv * (own_back * gain) - normal * (inv * inv * (cross / INNER))
        grad_mixed = grad_gated * gate_silu
        grad_gate = grad_gated * own_mixed * sig * (1.0 + own_gate * (1.0 - sig))
        grad_gate_out[at, :] = grad_gate.astype(BF16)
        store(2, i).start()
        reaching = (grad_mixed * widen(passing_ref[at, :], heads, channels)).astype(BF16)
        through[...] += dot_tn(reaching, out_map_ref[at, :])
        grad_gain_ref[0:1, :] += jnp.sum(own_back * normal, axis=0, keepdims=True)
        back[at, :] = grad_mixed
        store(0, i).start()

    each_span(spans, middle)
    follow = remote(through, following_ref, side_send, side_receive, partner)
    follow.start()
    follow.wait_recv()
    following_ref[...] = following_ref[...] * jnp.where(core > 0, 0.0, 1.0)
    for k in range(3):
        each_span(spans, lambda i, k=k: store(k, i).wait())
    follow.wait_send()


def mid_pass(gate, mixed, back, sums, passing, out_map, gain, heads, collective_id):
    tokens = gate.shape[0]
    channels = heads * HEADDIM
    spans = tokens // SPAN
    anywhere = pl.BlockSpec(memory_space=pl.ANY)
    vmem = pl.BlockSpec(memory_space=pltpu.VMEM)
    dma = pltpu.SemaphoreType.DMA
    out = jax.ShapeDtypeStruct
    return pl.pallas_call(
        lambda *refs: mid_kernel(heads, *refs),
        in_specs=[anywhere] * 3 + [vmem] * 4,
        out_specs=[anywhere] * 3 + [vmem] * 2,
        out_shape=[
            out((tokens, channels), BF16),
            out((tokens, channels), F32),
            out((tokens, channels), BF16),
            out((channels, STATE), F32),
            out((8, channels), F32),
        ],
        scratch_shapes=[
            pltpu.VMEM(gate.shape, F32),
            pltpu.VMEM(gate.shape, F32),
            pltpu.VMEM(gate.shape, F32),
            pltpu.VMEM(gate.shape, BF16),
            pltpu.VMEM(gate.shape, BF16),
            pltpu.VMEM((channels, STATE), F32),
            dma((3, spans)),
            dma((3, spans)),
            dma,
            dma,
        ],
        compiler_params=pltpu.CompilerParams(
            collective_id=collective_id, has_side_effects=True, vmem_limit_bytes=VMEM_LIMIT
        ),
        cost_estimate=pl.CostEstimate(
            flops=2 * tokens * STATE * channels,
            bytes_accessed=14 * 2**20,
            transcendentals=2 * tokens * channels,
        ),
        name="middle",
    )(gate, mixed, back, sums, passing, out_map, gain)


def final_kernel(count, local_inner, shared, *refs):
    mean_ref, small_ref = refs[:2]
    wide_refs = refs[2 : 2 + count]
    mean_out_ref, gate_ref, out_ref, inner_ref, state_ref, step_ref, small_out_ref = refs[2 + count : 9 + count]
    scratch = refs[9 + count :]
    wide = [(wide_refs[k],) + tuple(scratch[3 * k : 3 * k + 3]) for k in range(count)]
    (
        mean_in,
        small_in,
        small_sum,
        small_far,
        shared_own,
        shared_in,
        state_own,
        state_in,
        z_send,
        z_receive,
        near_send,
        near_receive,
        far_send,
        far_receive,
        own_sem,
        small_send,
        small_receive,
    ) = scratch[3 * count :]
    size, me = lax.axis_size("dp"), lax.axis_index("dp")
    line = lax.axis_size("tp")
    core = lax.axis_index("ctx")
    partner = {"ctx": 1 - core}
    dp_peers, tp_peers = peers_of("dp"), peers_of("tp")
    greet([partner] + [{"dp": p} for p in dp_peers] + [{"tp": p} for p in tp_peers])
    near, local = {}, {}
    order = list(range(1, size)) + [0]
    small_near = remote(small_ref, small_in, small_send.at[0], small_receive.at[0], partner)
    small_near.start()
    steps = [(off, 0) for off in order] + [(off, k) for off in order for k in range(1, count)]
    for off, k in steps:
        owner = lax.rem(me + off, size)
        for grads, own, arriving, _ in wide[k : k + 1]:
            depth = grads.shape[0] // (2 * size)

            def block(c, grads=grads, depth=depth, owner=owner):
                return grads.at[pl.ds(pl.multiple_of((owner * 2 + c) * depth, depth), depth)]

            near[off, k] = remote(
                block(1 - core), arriving.at[off], near_send.at[k, off], near_receive.at[k, off], partner
            )
            near[off, k].start()
            local[off, k] = pltpu.make_async_copy(block(core), own.at[off], own_sem.at[k, off])
            local[off, k].start()
    z_copies = []
    for i in range(line - 1):
        z_copies.append(
            remote(mean_ref, mean_in.at[i], z_send.at[0, i], z_receive.at[0, i], {"tp": tp_peers[i]})
        )
        z_copies[-1].start()
    far, first_far, small_copies = [], [], []
    for number, (off, k) in enumerate(steps):
        _, own, arriving, remote_in = wide[k]
        local[off, k].wait()
        near[off, k].wait_recv()
        add_rows(own.at[off], [own.at[off], arriving.at[off]], 16)
        if off > 0:
            copy = remote(
                own.at[off],
                remote_in.at[off - 1],
                far_send.at[k, off - 1],
                far_receive.at[k, off - 1],
                {"dp": dp_peers[off - 1]},
            )
            copy.start()
            (first_far if k == 0 else far).append(copy)
        if number == size - 1:
            small_near.wait_recv()
            small_sum[...] = small_ref[...] + small_in[...]
            for other in range(1, size):
                copy = remote(
                    small_sum,
                    small_far.at[other - 1],
                    small_send.at[other],
                    small_receive.at[other],
                    {"dp": dp_peers[other - 1]},
                )
                copy.start()
                small_copies.append(copy)
    for copy in z_copies:
        copy.wait_recv()
    add_rows(mean_out_ref, [mean_ref] + [mean_in.at[i] for i in range(line - 1)], 8)
    for copy in small_copies:
        copy.wait_recv()
    total = small_sum[...]
    for off in range(1, size):
        total = total + small_far[off - 1]
    small_out_ref[...] = total
    shared_own[...] = total[:, -shared:]
    terms = [[own.at[0]] + [remote_in.at[i] for i in range(size - 1)] for _, own, _, remote_in in wide]
    for copy in first_far:
        copy.wait_recv()
    add_rows(state_own, terms[0], 16, 0, 2 * STATE)
    last = []
    for i in range(line - 1):
        place = {"tp": tp_peers[i]}
        last.append(remote(state_own, state_in.at[i], z_send.at[1, i], z_receive.at[1, i], place))
        last.append(remote(shared_own, shared_in.at[i], z_send.at[2, i], z_receive.at[2, i], place))
    for copy in last:
        copy.start()
    add_rows(step_ref, terms[0], 16, 2 * STATE, LANES)
    for copy in far:
        copy.wait_recv()
    add_rows(gate_ref, terms[1], 16)
    add_rows(out_ref, terms[2], 16)
    add_rows(inner_ref, terms[3], 16)
    for copy in last:
        copy.wait_recv()
    add_rows(state_ref, [state_own] + [state_in.at[i] for i in range(line - 1)], 16)
    total = shared_own[...]
    for i in range(line - 1):
        total = total + shared_in[i]
    small_out_ref[:, -shared:] = total
    for copy in z_copies + last + first_far + far + small_copies + [small_near] + list(near.values()):
        copy.wait_send()


def final_exchange(mean, small, wide, local_inner, shared, collective_id):
    size, line = lax.axis_size("dp"), lax.axis_size("tp")
    count = len(wide)
    depth = wide[0].shape[0] // (2 * size)
    anywhere = pl.BlockSpec(memory_space=pl.ANY)
    vmem = pl.BlockSpec(memory_space=pltpu.VMEM)
    dma = pltpu.SemaphoreType.DMA

    def out(*shape):
        return jax.ShapeDtypeStruct(shape, F32)

    slots = []
    for like in wide:
        for copies in (size, size, size - 1):
            slots.append(pltpu.VMEM((copies, depth, like.shape[1]), BF16))
    return pl.pallas_call(
        lambda *refs: final_kernel(count, local_inner, shared, *refs),
        in_specs=[vmem, vmem] + [anywhere] * count,
        out_specs=[vmem] * 7,
        out_shape=[
            out(*mean.shape),
            out(depth, local_inner),
            out(depth, local_inner),
            out(depth, local_inner),
            out(depth, 2 * STATE),
            out(depth, LANES),
            out(*small.shape),
        ],
        scratch_shapes=slots
        + [
            pltpu.VMEM((line - 1,) + mean.shape, F32),
            pltpu.VMEM(small.shape, F32),
            pltpu.VMEM(small.shape, F32),
            pltpu.VMEM((size - 1,) + small.shape, F32),
            pltpu.VMEM((8, shared), F32),
            pltpu.VMEM((line - 1, 8, shared), F32),
            pltpu.VMEM((depth, 2 * STATE), BF16),
            pltpu.VMEM((line - 1, depth, 2 * STATE), BF16),
            dma((3, line - 1)),
            dma((3, line - 1)),
            dma((count, size)),
            dma((count, size)),
            dma((count, size - 1)),
            dma((count, size - 1)),
            dma((count, size)),
            dma((size,)),
            dma((size,)),
        ],
        compiler_params=pltpu.CompilerParams(
            collective_id=collective_id, has_side_effects=True, vmem_limit_bytes=VMEM_LIMIT
        ),
        name="final_exchange",
    )(mean, small, *wide)


def on_device(
    block_input_activations,
    sequence_first_token,
    norm_gain,
    gate_proj,
    input_proj,
    step_proj,
    state_proj,
    conv_inner_weight,
    conv_inner_bias,
    conv_state_weight,
    conv_state_bias,
    step_bias,
    decay_log,
    skip_weight,
    gate_gain,
    out_proj,
    output_cotangent,
):
    everyone = ("dp", "ctx")
    x = block_input_activations
    local_inner = gate_proj.shape[1]
    heads = step_bias.shape[0]
    tokens = x.shape[0]
    main = local_inner + 2 * STATE
    params = jnp.pad(jnp.stack([step_bias, decay_log, skip_weight]), ((0, 5), (0, LANES - heads)))
    early_shard, late_shard, flags, marks, taps, bias, step_row, decay_row, skip_row = prepare(
        gate_proj,
        out_proj,
        input_proj,
        state_proj,
        step_proj,
        sequence_first_token,
        conv_inner_weight,
        conv_state_weight,
        conv_inner_bias,
        conv_state_bias,
        params,
        heads,
    )
    early_full = lax.all_gather(early_shard, everyone, axis=0, tiled=True)
    late_full, halo_x, other_flags = gather([late_shard], x, flags, 4)
    gain = norm_gain[None, :]
    gated_gain = gate_gain[None, :]
    (
        normed,
        rows,
        conv,
        mixed_local,
        cum,
        raw,
        passing,
        out_map,
        states,
        products,
        final_state,
        halo_rows,
    ) = front(
        x, marks, halo_x, other_flags, gain, late_full, taps, bias, step_row, decay_row, skip_row, heads
    )
    branch_part, gate, mixed, back, carried, sums = branch_pass(
        normed, mixed_local, early_full, output_cotangent, passing, out_map, final_state, gated_gain, heads, 1
    )
    branch = lax.psum_scatter(branch_part, "tp", scatter_dimension=1, tiled=True)
    gated_normed, grad_mixed, grad_gate, following, grad_gain_gate = mid_pass(
        gate, mixed, back, sums, passing, out_map, gated_gain, heads, 3
    )
    grad_out = dot_tn(output_cotangent, gated_normed).astype(BF16)
    grad_gate_weight = dot_tn(normed, grad_gate).astype(BF16)
    late, tail, halo_grad, conv_sums, head_sums = back_pass(
        grad_mixed,
        conv,
        rows,
        halo_rows,
        raw,
        cum,
        states,
        products,
        carried,
        following,
        taps,
        decay_row,
        skip_row,
        heads,
    )
    returned = passed_along(halo_grad, -1)
    tensor_part, mean_sum, gain_sums, late = input_pass(
        x, grad_gate, late, tail, returned, early_full, late_full, gain
    )
    own_grad = lax.psum_scatter(tensor_part, "tp", scatter_dimension=1, tiled=True)
    state_weight = dot_tn(normed, late[:, local_inner:]).astype(BF16)
    inner_weight = dot_tn(normed, late[:, :local_inner]).astype(BF16)
    shared = 2 * STATE + MODEL_WIDTH
    small = jnp.concatenate(
        [conv_sums[:, :local_inner], grad_gain_gate, head_sums, conv_sums[:, local_inner:], gain_sums], axis=1
    )
    mean_sum, gate_grad, out_grad, inner_grad, state_grad, step_grad, small = final_exchange(
        mean_sum, small, [state_weight, grad_gate_weight, grad_out, inner_weight], local_inner, shared, 2
    )
    place = lax.axis_index("tp")
    share = MODEL_WIDTH // lax.axis_size("tp")
    gain_grad = lax.dynamic_slice_in_dim(small[0], small.shape[1] - MODEL_WIDTH + place * share, share, 0)
    (
        out_grad,
        step_grad,
        gate_grad,
        inner_grad,
        state_grad,
        inner_taps,
        inner_bias,
        state_taps,
        state_bias,
        step_bias_grad,
        decay_grad,
        skip_grad,
        gate_gain_grad,
    ) = spread(out_grad, step_grad, gate_grad, inner_grad, state_grad, small, heads)
    block_output = output_pass(place.reshape(1), x, branch, sums)
    input_grad = grad_pass(
        place.reshape(1), x, output_cotangent, own_grad, mean_sum, gain, lax.axis_size("tp")
    )
    return (
        block_output,
        input_grad,
        gain_grad,
        gate_grad,
        inner_grad,
        step_grad,
        state_grad,
        inner_taps,
        inner_bias[0],
        state_taps,
        state_bias[0],
        step_bias_grad[0],
        decay_grad[0],
        skip_grad[0],
        gate_gain_grad[0],
        out_grad,
    )


def solution(mesh):
    return jax.shard_map(
        on_device,
        mesh=mesh,
        in_specs=(
            P(("dp", "ctx"), None),
            P(("dp", "ctx")),
            P(),
            P(("dp", "ctx"), "tp"),
            P(("dp", "ctx"), "tp"),
            P(("dp", "ctx"), "tp"),
            P(("dp", "ctx"), None),
            P(None, "tp"),
            P("tp"),
            P(),
            P(),
            P("tp"),
            P("tp"),
            P("tp"),
            P("tp"),
            P("tp", ("dp", "ctx")),
            P(("dp", "ctx"), None),
        ),
        out_specs=(
            P(("dp", "ctx"), "tp"),
            P(("dp", "ctx"), "tp"),
            P("tp"),
            P(("dp", "ctx"), "tp"),
            P(("dp", "ctx"), "tp"),
            P(("dp", "ctx"), "tp"),
            P(("dp", "ctx"), None),
            P(None, "tp"),
            P("tp"),
            P(),
            P(),
            P("tp"),
            P("tp"),
            P("tp"),
            P("tp"),
            P("tp", ("dp", "ctx")),
        ),
        check_vma=False,
    )
```

```python
import jax
import jax.numpy as jnp
from jax import lax
from jax.experimental import pallas as pl
from jax.experimental.pallas import tpu as pltpu
from jax.sharding import PartitionSpec as P

MODEL_WIDTH = 1024
HEADDIM = 64
STATE = 128
KCONV = 4
SPAN = 256
INNER = 2048


EPSILON = 1e-05
HIGHEST = lax.Precision.HIGHEST


def passed_along(block, distance):
    devices = range(lax.axis_size("ctx"))
    route = [(i - distance, i) for i in devices if i - distance in devices]
    return lax.ppermute(block, "ctx", route)


LANES = 128
BLOCK = 512
VMEM_LIMIT = 60 * 1024 * 1024
BF16 = jnp.bfloat16
F32 = jnp.float32
BLOCKED = -1e30


def dot_nn(a, b):
    return jnp.dot(a, b, preferred_element_type=F32)


def dot_nt(a, b):
    return lax.dot_general(a, b, (((1,), (1,)), ((), ())), preferred_element_type=F32)


def dot_tn(a, b):
    return lax.dot_general(a, b, (((0,), (0,)), ((), ())), preferred_element_type=F32)


def iota(shape, dim):
    return lax.broadcasted_iota(jnp.int32, shape, dim)


def high_low(a):
    high = a.astype(BF16)
    return high, (a - high.astype(F32)).astype(BF16)


def widen(a, heads, width):
    lane = iota(a.shape, 1)
    high = a.astype(BF16).astype(F32)
    low = pltpu.roll(a - high, heads, 1)
    packed = jnp.where(lane < heads, high, jnp.where(lane < 2 * heads, low, 0.0)).astype(BF16)
    row, column = iota((LANES, width), 0), iota((LANES, width), 1)
    place = jnp.where(row < heads, row, row - heads)
    return dot_nn(packed, (column // HEADDIM == place).astype(BF16))


def per_head_sum(a, heads):
    high, low = high_low(a)
    row, column = iota((LANES, a.shape[1]), 0), iota((LANES, a.shape[1]), 1)
    pick = (column // HEADDIM == row).astype(BF16)
    return dot_nt(high, pick) + dot_nt(low, pick)


def triangle_sum(triangle, series):
    lane = iota(series.shape, 1)
    series = jnp.where(lane < 16, series, 0.0)
    high = series.astype(BF16).astype(F32)
    middle = (series - high).astype(BF16).astype(F32)
    low = series - high - middle
    packed = high + pltpu.roll(middle, 16, 1) + pltpu.roll(low, 32, 1)
    sums = dot_nn(triangle.astype(BF16), packed.astype(BF16))
    total = sums + pltpu.roll(sums, LANES - 16, 1) + pltpu.roll(sums, LANES - 32, 1)
    return jnp.where(lane < 16, total, 0.0)


def row_sum(a):
    folded = a[:, :LANES]
    for i in range(1, a.shape[1] // LANES):
        folded = folded + a[:, i * LANES : (i + 1) * LANES]
    return jnp.sum(folded.T, axis=0, keepdims=True)


def rows_of_heads(column, heads):
    return jnp.concatenate(
        [jnp.broadcast_to(column[h : h + 1, :], (HEADDIM, LANES)) for h in range(heads)], axis=0
    )


def column_of(row):
    return jnp.broadcast_to(row, (LANES, row.shape[1])).T[:, 0:1]


def sigmoid(v):
    return 0.5 * jnp.tanh(0.5 * v) + 0.5


def normalise(x, gain):
    hidden = x.astype(F32)
    inv = lax.rsqrt(jnp.mean(hidden * hidden, axis=1, keepdims=True) + EPSILON)
    return (hidden * inv * gain).astype(BF16)


def whole(shape):
    return pl.BlockSpec(shape, lambda i: (0,) * len(shape))


def columns_of(array, width, block):
    return pl.BlockSpec((array.shape[0], width), lambda i: (0, block))


def front_kernel(
    heads,
    x_ref,
    marks_ref,
    halo_x_ref,
    flags_ref,
    gain_ref,
    weight_ref,
    taps_ref,
    bias_ref,
    step_bias_ref,
    decay_ref,
    skip_ref,
    normed_ref,
    rows_ref,
    conv_ref,
    mixed_ref,
    cum_ref,
    raw_ref,
    passing_ref,
    out_map_ref,
    states_ref,
    products_ref,
    final_ref,
    halo_rows_ref,
    state,
    product,
    before,
):
    step = pl.program_id(0)
    channels = heads * HEADDIM
    main = channels + 2 * STATE
    gain = gain_ref[...]

    @pl.when(step == 0)
    def _():
        state[...] = jnp.zeros_like(state)
        product[...] = jnp.ones_like(product)
        halo = dot_nn(normalise(halo_x_ref[...], gain), weight_ref[:, :main]).astype(BF16)
        halo_rows_ref[...] = halo
        before[...] = halo.astype(F32)[8:16]

    normed = normalise(x_ref[...], gain)
    normed_ref[...] = normed
    projected = dot_nn(normed, weight_ref[...])
    rows = projected[:, :main].astype(BF16)
    rows_ref[...] = rows
    rows = rows.astype(F32)
    raw = projected[:, main:] + step_bias_ref[...]
    extended = jnp.concatenate([before[...], rows], axis=0)
    before[...] = rows[SPAN - 8 :]
    taps = taps_ref[...]
    conv = bias_ref[...] + taps[0:1] * rows
    lane = iota((SPAN, LANES), 1)
    boundary = jnp.where(step == 0, flags_ref[flags_ref.shape[0] - 1 :, LANES - KCONV :], 0.0)
    reach = 1.0 - boundary
    at_first, at_second = iota((SPAN, 1), 0) == 0, iota((SPAN, 1), 0) == 1
    nearest, second = reach[:, KCONV - 1 :], reach[:, KCONV - 2 : KCONV - 1]
    edges = [
        None,
        None,
        jnp.where(at_first, nearest, 1.0),
        jnp.where(at_first, nearest * second, jnp.where(at_second, nearest, 1.0)),
    ]
    for lag in range(1, KCONV):
        valid = marks_ref[:, lag : lag + 1]
        if edges[lag] is not None:
            valid = valid * edges[lag]
        raw = jnp.where(lane == heads + lag, valid, raw)
        conv = conv + (taps[lag : lag + 1] * extended[8 - lag : 8 - lag + SPAN]) * valid
    raw_ref[...] = raw
    conv_ref[...] = conv
    act = conv * sigmoid(conv)
    values = act[:, :channels]
    map_in = act[:, channels : channels + STATE].astype(BF16)
    map_out = act[:, channels + STATE :].astype(BF16)
    out_map_ref[...] = map_out

    step_size = jnp.maximum(raw, 0.0) + jnp.log1p(jnp.exp(-jnp.abs(raw)))
    log_decay = jnp.where(lane < heads, step_size * (-jnp.exp(decay_ref[...])), 0.0)
    series = jnp.where(lane == heads, marks_ref[:, 0:1], log_decay)
    t, s = iota((SPAN, SPAN), 0), iota((SPAN, SPAN), 1)
    cum = triangle_sum((t >= s).astype(F32), series)
    cum_ref[...] = cum
    cum_rows = cum.T
    segment, segment_row = cum[:, heads : heads + 1], cum_rows[heads : heads + 1, :]
    blocked = jnp.where((segment == segment_row) & (t >= s), 0.0, BLOCKED)
    passing = jnp.where(segment == 0.0, jnp.exp(cum), 0.0)
    product_now = product[...]
    passing_ref[...] = passing * product_now[0:1]
    products_ref[0] = product_now
    product[...] = product_now * passing[SPAN - 1 : SPAN]
    to_end = jnp.where(
        segment == cum[SPAN - 1 : SPAN, heads : heads + 1], jnp.exp(cum[SPAN - 1 : SPAN] - cum), 0.0
    )
    stepped = values * widen(step_size, heads, channels)
    state_now = state[...]
    states_ref[0] = state_now
    scores = dot_nt(map_out, map_in)
    through = widen(passing, heads, channels) * dot_nt(map_out, state_now.astype(BF16))
    half = iota((SPAN, LANES), 1) < HEADDIM
    for pair in range(heads // 2):
        at = slice(pair * LANES, (pair + 1) * LANES)
        both = stepped[:, at]
        total = through[:, at] + skip_ref[:, at] * values[:, at]
        for side in range(2):
            h = 2 * pair + side
            spread = cum[:, h : h + 1] - cum_rows[h : h + 1, :]
            mixing = (jnp.exp(spread + blocked) * scores).astype(BF16)
            own = jnp.where(half if side == 0 else ~half, both, 0.0).astype(BF16)
            total = total + dot_nn(mixing, own)
        mixed_ref[:, at] = total
    ending = (stepped * widen(to_end, heads, channels)).astype(BF16)
    fresh = dot_tn(ending, map_in)
    kept = jnp.where(segment_row[:, SPAN - 1 :] == 0.0, jnp.exp(cum_rows[:, SPAN - 1 :]), 0.0)
    state_next = rows_of_heads(kept, heads) * state_now + fresh
    state[...] = state_next
    final_ref[...] = state_next


def front(x, marks, halo_x, flags, gain, weight, taps, bias, step_bias, decay, skip, heads):
    tokens = x.shape[0]
    channels = heads * HEADDIM
    main = channels + 2 * STATE
    spans = tokens // SPAN

    def chunk(width):
        return pl.BlockSpec((SPAN, width), lambda i: (i, 0))

    def out(shape, dtype):
        return jax.ShapeDtypeStruct(shape, dtype)

    return pl.pallas_call(
        lambda *refs: front_kernel(heads, *refs),
        grid=(spans,),
        in_specs=[
            chunk(MODEL_WIDTH),
            chunk(LANES),
            whole(halo_x.shape),
            whole(flags.shape),
            whole(gain.shape),
            whole(weight.shape),
            whole(taps.shape),
            whole(bias.shape),
            whole(step_bias.shape),
            whole(decay.shape),
            whole(skip.shape),
        ],
        out_specs=[
            chunk(MODEL_WIDTH),
            chunk(main),
            chunk(main),
            chunk(channels),
            chunk(LANES),
            chunk(LANES),
            chunk(LANES),
            chunk(STATE),
            pl.BlockSpec((1, channels, STATE), lambda i: (i, 0, 0)),
            pl.BlockSpec((1, 8, LANES), lambda i: (i, 0, 0)),
            whole((channels, STATE)),
            whole((16, main)),
        ],
        out_shape=[
            out((tokens, MODEL_WIDTH), BF16),
            out((tokens, main), BF16),
            out((tokens, main), F32),
            out((tokens, channels), F32),
            out((tokens, LANES), F32),
            out((tokens, LANES), F32),
            out((tokens, LANES), F32),
            out((tokens, STATE), BF16),
            out((spans, channels, STATE), F32),
            out((spans, 8, LANES), F32),
            out((channels, STATE), F32),
            out((16, main), BF16),
        ],
        scratch_shapes=[
            pltpu.VMEM((channels, STATE), F32),
            pltpu.VMEM((8, LANES), F32),
            pltpu.VMEM((8, main), F32),
        ],
        compiler_params=pltpu.CompilerParams(vmem_limit_bytes=VMEM_LIMIT),
        cost_estimate=pl.CostEstimate(
            flops=2 * tokens * (MODEL_WIDTH * weight.shape[1] + 4 * SPAN * channels),
            bytes_accessed=18 * 2**20,
            transcendentals=tokens * SPAN * heads,
        ),
        name="scan_front",
    )(x, marks, halo_x, flags, gain, weight, taps, bias, step_bias, decay, skip)


def back_kernel(
    heads,
    grad_ref,
    conv_ref,
    rows_ref,
    earlier_ref,
    halo_ref,
    raw_ref,
    cum_ref,
    states_ref,
    products_ref,
    carried_ref,
    next_ref,
    taps_ref,
    decay_ref,
    skip_ref,
    late_ref,
    tail_ref,
    halo_grad_ref,
    sums_ref,
    head_sums_ref,
    flowing,
    after,
):
    step = pl.program_id(0)
    spans = pl.num_programs(0)
    channels = heads * HEADDIM
    main = channels + 2 * STATE

    @pl.when(step == 0)
    def _():
        flowing[...] = next_ref[...]
        after[...] = jnp.zeros_like(after)
        sums_ref[...] = jnp.zeros_like(sums_ref)
        head_sums_ref[...] = jnp.zeros_like(head_sums_ref)

    conv = conv_ref[...]
    sig = sigmoid(conv)
    act = conv * sig
    slope = sig * (1.0 + conv * (1.0 - sig))
    values = act[:, :channels]
    map_in = act[:, channels : channels + STATE].astype(BF16)
    map_out = act[:, channels + STATE :].astype(BF16)
    raw = raw_ref[...]
    step_size = jnp.maximum(raw, 0.0) + jnp.log1p(jnp.exp(-jnp.abs(raw)))
    cum = cum_ref[...]
    cum_rows = cum.T
    segment, segment_row = cum[:, heads : heads + 1], cum_rows[heads : heads + 1, :]
    s, t = iota((SPAN, SPAN), 0), iota((SPAN, SPAN), 1)
    blocked = jnp.where((segment == segment_row) & (t >= s), 0.0, BLOCKED)
    passing = jnp.where(segment == 0.0, jnp.exp(cum), 0.0)
    to_end = jnp.where(
        segment == cum[SPAN - 1 : SPAN, heads : heads + 1], jnp.exp(cum[SPAN - 1 : SPAN] - cum), 0.0
    )
    kept = jnp.where(segment_row[:, SPAN - 1 :] == 0.0, jnp.exp(cum_rows[:, SPAN - 1 :]), 0.0)
    product_column = jnp.broadcast_to(products_ref[0][0:1], (LANES, LANES)).T
    state = states_ref[0] + rows_of_heads(product_column[:, 0:1], heads) * carried_ref[...]
    state_bf = state.astype(BF16)
    flow = flowing[...]
    flow_bf = flow.astype(BF16)
    grad = grad_ref[...]
    step_wide = widen(step_size, heads, channels)
    end_wide = widen(to_end, heads, channels)
    stepped = values * step_wide
    stepped_bf = stepped.astype(BF16)
    grad_bf = grad.astype(BF16)
    reaching = grad * widen(passing, heads, channels)
    reaching_bf = reaching.astype(BF16)
    ending = stepped * end_wide
    ending_bf = ending.astype(BF16)
    from_state = dot_nt(map_out, state_bf)
    from_flow = dot_nt(map_in, flow_bf)
    scores = dot_nt(map_in, map_out)
    half = iota((SPAN, LANES), 1) < HEADDIM
    zero = jnp.zeros((SPAN, LANES), BF16)
    lane = iota((SPAN, LANES), 1)
    grad_scores = jnp.zeros((SPAN, SPAN), F32)
    out_sums = jnp.zeros((SPAN, LANES), F32)
    in_sums = []
    grad_stepped = []
    for pair in range(heads // 2):
        at = slice(pair * LANES, (pair + 1) * LANES)
        total = end_wide[:, at] * from_flow[:, at]
        for side in range(2):
            h = 2 * pair + side
            own = half if side == 0 else ~half
            decay = jnp.exp((cum_rows[h : h + 1, :] - cum[:, h : h + 1]) + blocked)
            own_grad = jnp.where(own, grad_bf[:, at], zero)
            total = total + dot_nn((decay * scores).astype(BF16), own_grad)
            flowed = decay * dot_nt(stepped_bf[:, at], own_grad)
            grad_scores = grad_scores + flowed
            weighed = flowed * scores
            in_sums.append(jnp.sum(weighed, axis=0, keepdims=True))
            out_sums = jnp.where(lane == h, jnp.sum(weighed, axis=1, keepdims=True), out_sums)
        grad_stepped.append(total)
    grad_stepped = jnp.concatenate(grad_stepped, axis=1)
    grad_scores = grad_scores.astype(BF16)
    grad_out_map = dot_tn(grad_scores, map_in) + dot_nn(reaching_bf, state_bf)
    grad_in_map = dot_nn(grad_scores, map_out) + dot_nn(ending_bf, flow_bf)
    ended = per_head_sum(ending * from_flow, heads)
    row, column = iota((LANES, channels), 0), iota((LANES, channels), 1)
    pick = (column // HEADDIM == row).astype(BF16)
    high, low = high_low(flow * state)
    at_last = kept * jnp.sum(dot_nn(pick, high) + dot_nn(pick, low), axis=1, keepdims=True)
    in_rows = jnp.concatenate(
        in_sums + [jnp.zeros((LANES - heads, SPAN), F32)], axis=0
    ) + jnp.where(iota((LANES, SPAN), 1) == SPAN - 1, at_last, 0.0)
    last = iota((SPAN, LANES), 0) == SPAN - 1
    grad_cum = (
        in_rows.T
        - out_sums
        + per_head_sum(reaching * from_state, heads)
        - ended
        + jnp.where(last, jnp.sum(ended, axis=0, keepdims=True), 0.0)
    )
    grad_log = triangle_sum((t >= s).astype(F32), grad_cum)
    rate = -jnp.exp(decay_ref[...])
    grad_step = per_head_sum(grad_stepped * values, heads) + grad_log * rate
    grad_raw = jnp.where(lane < heads, grad_step * sigmoid(raw), 0.0)
    late_ref[:, main:] = grad_raw.astype(BF16)
    head_sums_ref[0:1] += jnp.sum(grad_raw, axis=0, keepdims=True)
    head_sums_ref[1:2] += jnp.sum(grad_log * step_size, axis=0, keepdims=True) * rate
    flowing[...] = rows_of_heads(kept, heads) * flow + dot_tn(reaching_bf, map_out)
    grad_values = grad_stepped * step_wide + skip_ref[...] * grad
    grad_act = jnp.concatenate([grad_values, grad_in_map, grad_out_map], axis=1)
    grad_conv = grad_act * slope
    sums_ref[5:6, :channels] += jnp.sum(grad * values, axis=0, keepdims=True)
    sums_ref[4:5] += jnp.sum(grad_conv, axis=0, keepdims=True)
    rows = rows_ref[...].astype(F32)
    first = step == spans - 1
    previous = jnp.where(first, halo_ref[...].astype(F32), earlier_ref[...].astype(F32))[8:16]
    extended = jnp.concatenate([previous, rows], axis=0)
    sums_ref[0:1] += jnp.sum(grad_conv * rows, axis=0, keepdims=True)
    taps = taps_ref[...]
    grad_rows = taps[0:1] * grad_conv
    halo_grad = jnp.zeros((8, main), F32)
    for lag in range(1, KCONV):
        valid = grad_conv * raw[:, heads + lag : heads + lag + 1]
        sums_ref[lag : lag + 1] += jnp.sum(
            valid * extended[8 - lag : 8 - lag + SPAN], axis=0, keepdims=True
        )
        tapped = taps[lag : lag + 1] * valid
        joined = jnp.concatenate([tapped, after[lag - 1]], axis=0)
        grad_rows = grad_rows + joined[lag : lag + SPAN]
        head = tapped[0:8]
        after[lag - 1] = head
        halo_grad = halo_grad + jnp.concatenate([jnp.zeros((8, main), F32), head], axis=0)[lag : lag + 8]
    late_ref[:, :main] = grad_rows.astype(BF16)
    halo_grad_ref[...] = halo_grad

    @pl.when(step == 0)
    def _():
        tail_ref[...] = grad_rows[SPAN - 16 :]


def back_pass(
    grad, conv, rows, halo, raw, cum, states, products, carried, following, taps, decay, skip, heads
):
    tokens = grad.shape[0]
    channels = heads * HEADDIM
    main = channels + 2 * STATE
    spans = tokens // SPAN

    def chunk(width):
        return pl.BlockSpec((SPAN, width), lambda i: (spans - 1 - i, 0))

    return pl.pallas_call(
        lambda *refs: back_kernel(heads, *refs),
        grid=(spans,),
        in_specs=[
            chunk(channels),
            chunk(main),
            chunk(main),
            pl.BlockSpec((16, main), lambda i: (jnp.maximum((spans - 1 - i) * (SPAN // 16) - 1, 0), 0)),
            whole(halo.shape),
            chunk(LANES),
            chunk(LANES),
            pl.BlockSpec((1, channels, STATE), lambda i: (spans - 1 - i, 0, 0)),
            pl.BlockSpec((1, 8, LANES), lambda i: (spans - 1 - i, 0, 0)),
            whole(carried.shape),
            whole(following.shape),
            whole(taps.shape),
            whole(decay.shape),
            whole(skip.shape),
        ],
        out_specs=[
            chunk(main + LANES),
            whole((16, main)),
            whole((8, main)),
            whole((8, main)),
            whole((8, LANES)),
        ],
        out_shape=[
            jax.ShapeDtypeStruct((tokens, main + LANES), BF16),
            jax.ShapeDtypeStruct((16, main), F32),
            jax.ShapeDtypeStruct((8, main), F32),
            jax.ShapeDtypeStruct((8, main), F32),
            jax.ShapeDtypeStruct((8, LANES), F32),
        ],
        scratch_shapes=[
            pltpu.VMEM((channels, STATE), F32),
            pltpu.VMEM((KCONV - 1, 8, main), F32),
        ],
        compiler_params=pltpu.CompilerParams(vmem_limit_bytes=VMEM_LIMIT),
        cost_estimate=pl.CostEstimate(
            flops=2 * tokens * 12 * SPAN * channels,
            bytes_accessed=12 * 2**20,
            transcendentals=tokens * SPAN * heads,
        ),
        name="scan_back",
    )(
        grad, conv, rows, rows, halo, raw, cum, states, products, carried, following, taps, decay, skip
    )


def input_kernel(
    x_ref,
    grad_gate_ref,
    late_ref,
    tail_ref,
    returned_ref,
    gate_weight_ref,
    late_weight_ref,
    gain_ref,
    part_ref,
    sums_ref,
    grad_gain_ref,
    whole_late_ref,
):
    step = pl.program_id(0)
    whole_late_ref[...] = late_ref[...]

    @pl.when(step == pl.num_programs(0) - 1)
    def _():
        main = tail_ref.shape[1]
        tail = tail_ref[...] + jnp.concatenate([jnp.zeros((8, main), F32), returned_ref[...]], axis=0)
        whole_late_ref[BLOCK - 16 :, :main] = tail.astype(BF16)

    part = dot_nt(grad_gate_ref[...], gate_weight_ref[...])
    part = part + dot_nt(whole_late_ref[...], late_weight_ref[...])
    part_ref[...] = part.astype(BF16)
    hidden = x_ref[...].astype(F32)
    square = hidden * hidden
    inv = lax.rsqrt(jnp.mean(square, axis=1, keepdims=True) + EPSILON)
    term = part * hidden
    sums_ref[...] = jnp.where(iota((8, BLOCK), 0) < 4, row_sum(term * gain_ref[...]), row_sum(square))
    gain_part = jnp.sum(term * inv, axis=0, keepdims=True)

    @pl.when(step == 0)
    def _():
        grad_gain_ref[...] = jnp.zeros_like(grad_gain_ref)

    grad_gain_ref[0:1] += gain_part


def input_pass(x, grad_gate, late, tail, returned, early_weight, late_weight, gain):
    tokens = x.shape[0]
    channels = grad_gate.shape[1]

    def chunk(width):
        return pl.BlockSpec((BLOCK, width), lambda i: (i, 0))

    return pl.pallas_call(
        input_kernel,
        grid=(tokens // BLOCK,),
        in_specs=[
            chunk(MODEL_WIDTH),
            chunk(channels),
            chunk(late.shape[1]),
            whole(tail.shape),
            whole(returned.shape),
            columns_of(early_weight, channels, 0),
            whole(late_weight.shape),
            whole(gain.shape),
        ],
        out_specs=[
            chunk(MODEL_WIDTH),
            pl.BlockSpec((8, BLOCK), lambda i: (0, i)),
            whole((8, MODEL_WIDTH)),
            chunk(late.shape[1]),
        ],
        out_shape=[
            jax.ShapeDtypeStruct((tokens, MODEL_WIDTH), BF16),
            jax.ShapeDtypeStruct((8, tokens), F32),
            jax.ShapeDtypeStruct((8, MODEL_WIDTH), F32),
            jax.ShapeDtypeStruct(late.shape, BF16),
        ],
        compiler_params=pltpu.CompilerParams(vmem_limit_bytes=VMEM_LIMIT),
        cost_estimate=pl.CostEstimate(
            flops=2 * tokens * MODEL_WIDTH * (channels + late.shape[1]),
            bytes_accessed=12 * 2**20,
            transcendentals=0,
        ),
        name="input_pass",
    )(x, grad_gate, late, tail, returned, early_weight, late_weight, gain)


def spread_kernel(heads, out_ref, step_ref, gate_ref, inner_ref, state_ref, small_ref, *outs):
    channels = heads * HEADDIM
    out_out, step_out, gate_out, inner_out, state_out = outs[:5]
    taps_out, bias_out, state_taps_out, state_bias_out, step_bias_out, decay_out, skip_out, gain_out = outs[5:]
    out_out[...] = out_ref[...].T
    step_out[...] = step_ref[:, :heads]
    gate_out[...] = gate_ref[...]
    inner_out[...] = inner_ref[...]
    state_out[...] = state_ref[...]
    heads_at = 2 * channels
    state_at = heads_at + LANES
    taps_out[...] = small_ref[:KCONV, :channels]
    bias_out[...] = small_ref[KCONV : KCONV + 1, :channels]
    state_taps_out[...] = small_ref[:KCONV, state_at : state_at + 2 * STATE]
    state_bias_out[...] = small_ref[KCONV : KCONV + 1, state_at : state_at + 2 * STATE]
    step_bias_out[...] = small_ref[0:1, heads_at : heads_at + LANES][:, :heads]
    decay_out[...] = small_ref[1:2, heads_at : heads_at + LANES][:, :heads]
    skip_out[...] = per_head_sum(small_ref[:, :channels], heads)[5:6, :heads]
    gain_out[...] = small_ref[0:1, channels:heads_at]


def spread(out_grad, step_grad, gate_grad, inner_grad, state_grad, small, heads):
    depth = out_grad.shape[0]
    channels = heads * HEADDIM
    vmem = pl.BlockSpec(memory_space=pltpu.VMEM)
    shapes = [
        (channels, depth),
        (depth, heads),
        (depth, channels),
        (depth, channels),
        (depth, 2 * STATE),
        (KCONV, channels),
        (1, channels),
        (KCONV, 2 * STATE),
        (1, 2 * STATE),
        (1, heads),
        (1, heads),
        (1, heads),
        (1, channels),
    ]
    return pl.pallas_call(
        lambda *refs: spread_kernel(heads, *refs),
        in_specs=[vmem] * 6,
        out_specs=[vmem] * len(shapes),
        out_shape=[jax.ShapeDtypeStruct(shape, F32) for shape in shapes],
        name="spread",
    )(out_grad, step_grad, gate_grad, inner_grad, state_grad, small)


def output_kernel(place_ref, own_x_ref, branch_ref, sums_ref, output_ref):
    gate_inv = lax.rsqrt(column_of(sums_ref[0:1]) / INNER + EPSILON)
    output_ref[...] = (own_x_ref[...].astype(F32) + gate_inv * branch_ref[...].astype(F32)).astype(BF16)


def grad_kernel(line, place_ref, own_x_ref, own_cot_ref, part_ref, mean_ref, gain_ref, grad_ref):
    inv = lax.rsqrt(column_of(mean_ref[4:5]) / (line * MODEL_WIDTH) + EPSILON)
    mean = column_of(mean_ref[0:1]) / MODEL_WIDTH
    scaled = part_ref[...].astype(F32) * gain_ref[...]
    own = own_x_ref[...].astype(F32)
    grad_ref[...] = own_cot_ref[...].astype(F32) + inv * scaled - own * (inv * inv * inv * mean)


def finish_specs(share):
    chunk = pl.BlockSpec((BLOCK, share), lambda i, place: (i, 0))
    own = pl.BlockSpec((BLOCK, share), lambda i, place: (i, place[0]))
    rows = pl.BlockSpec((8, BLOCK), lambda i, place: (0, i))
    return chunk, own, rows, pl.BlockSpec((1, share), lambda i, place: (0, place[0]))


def output_pass(place, x, branch, sums):
    tokens, share = branch.shape
    chunk, own, rows, _ = finish_specs(share)
    return pl.pallas_call(
        output_kernel,
        grid_spec=pltpu.PrefetchScalarGridSpec(
            num_scalar_prefetch=1,
            grid=(tokens // BLOCK,),
            in_specs=[own, chunk, rows],
            out_specs=chunk,
        ),
        out_shape=jax.ShapeDtypeStruct((tokens, share), BF16),
        compiler_params=pltpu.CompilerParams(vmem_limit_bytes=VMEM_LIMIT),
        name="output_pass",
    )(place, x, branch, sums)


def grad_pass(place, x, cot, part, mean, gain, line):
    tokens, share = part.shape
    chunk, own, rows, gains = finish_specs(share)
    return pl.pallas_call(
        lambda *refs: grad_kernel(line, *refs),
        grid_spec=pltpu.PrefetchScalarGridSpec(
            num_scalar_prefetch=1,
            grid=(tokens // BLOCK,),
            in_specs=[own, own, chunk, rows, gains],
            out_specs=chunk,
        ),
        out_shape=jax.ShapeDtypeStruct((tokens, share), F32),
        compiler_params=pltpu.CompilerParams(vmem_limit_bytes=VMEM_LIMIT),
        name="grad_pass",
    )(place, x, cot, part, mean, gain)


def prep_kernel(
    heads,
    gate_ref,
    out_ref,
    input_ref,
    state_ref,
    step_ref,
    flags_ref,
    inner_taps_ref,
    state_taps_ref,
    inner_bias_ref,
    state_bias_ref,
    params_ref,
    early_ref,
    late_ref,
    flags_out_ref,
    marks_ref,
    taps_ref,
    bias_ref,
    step_bias_ref,
    decay_ref,
    skip_ref,
    shifted,
):
    channels = heads * HEADDIM
    depth = gate_ref.shape[0]
    main = channels + 2 * STATE
    early_ref[:, :channels] = gate_ref[...]
    early_ref[:, channels:] = out_ref[...].astype(F32).T.astype(BF16)
    late_ref[:, :channels] = input_ref[...]
    late_ref[:, channels:main] = state_ref[...]
    steps = jnp.concatenate([step_ref[...].astype(F32), jnp.zeros((LANES - heads, depth), F32)], axis=0)
    late_ref[:, main:] = steps.T.astype(BF16)
    flags = flags_ref[...].astype(F32)
    flags_out_ref[...] = flags
    blocks = flags.shape[0]
    shifted[0:8] = jnp.zeros((8, LANES), F32)
    for i in range(blocks):
        shifted[8 + i * LANES : 8 + (i + 1) * LANES] = jnp.broadcast_to(flags[i : i + 1], (LANES, LANES)).T
    lane = iota((LANES, LANES), 1)
    for i in range(blocks):
        at = 8 + i * LANES
        own = shifted[at : at + LANES]
        lag1 = 1.0 - own
        lag2 = lag1 * (1.0 - shifted[at - 1 : at - 1 + LANES])
        lag3 = lag2 * (1.0 - shifted[at - 2 : at - 2 + LANES])
        marks_ref[i * LANES : (i + 1) * LANES] = jnp.where(
            lane == 0, own, jnp.where(lane == 1, lag1, jnp.where(lane == 2, lag2, lag3))
        )
    taps_ref[:, :channels] = inner_taps_ref[...]
    taps_ref[:, channels:] = state_taps_ref[...]
    for i in range(channels // LANES):
        bias_ref[:, i * LANES : (i + 1) * LANES] = inner_bias_ref[i : i + 1]
    for i in range(2 * STATE // LANES):
        at = channels + i * LANES
        bias_ref[:, at : at + LANES] = state_bias_ref[i : i + 1]
    params = params_ref[...]
    step_bias_ref[...] = params[0:1]
    decay_ref[...] = params[1:2]
    skips = [jnp.broadcast_to(params[2:3, h : h + 1], (1, HEADDIM)) for h in range(heads)]
    skip_ref[...] = jnp.concatenate(skips, axis=1)


def prepare(
    gate_proj, out_proj, input_proj, state_proj, step_proj, first, taps, state_taps, bias, state_bias, params, heads
):
    depth, channels = gate_proj.shape
    main = channels + 2 * STATE
    tokens = first.shape[0]
    vmem = pl.BlockSpec(memory_space=pltpu.VMEM)
    out = jax.ShapeDtypeStruct
    return pl.pallas_call(
        lambda *refs: prep_kernel(heads, *refs),
        in_specs=[vmem] * 11,
        out_specs=[vmem] * 9,
        out_shape=[
            out((depth, 2 * channels), BF16),
            out((depth, main + LANES), BF16),
            out((tokens // LANES, LANES), F32),
            out((tokens, LANES), F32),
            out((KCONV, main), F32),
            out((1, main), F32),
            out((1, LANES), F32),
            out((1, LANES), F32),
            out((1, channels), F32),
        ],
        scratch_shapes=[pltpu.VMEM((tokens + 8, LANES), F32)],
        compiler_params=pltpu.CompilerParams(vmem_limit_bytes=VMEM_LIMIT),
        name="prepare",
    )(
        gate_proj,
        out_proj,
        input_proj,
        state_proj,
        step_proj.T,
        first.reshape(-1, LANES),
        taps,
        state_taps,
        bias.reshape(-1, LANES),
        state_bias.reshape(-1, LANES),
        params,
    )


MESH = pl.DeviceIdType.MESH


def remote(source, target, sends, receives, place):
    return pltpu.make_async_remote_copy(
        src_ref=source,
        dst_ref=target,
        send_sem=sends,
        recv_sem=receives,
        device_id=place,
        device_id_type=MESH,
    )


def greet(places):
    barrier = pltpu.get_barrier_semaphore()
    for place in places:
        pl.semaphore_signal(barrier, inc=1, device_id=place, device_id_type=MESH)
    pl.semaphore_wait(barrier, len(places))


def peers_of(axis):
    size, me = lax.axis_size(axis), lax.axis_index(axis)
    return [lax.rem(me + off, size) for off in range(1, size)]


def gather_kernel(count, *refs):
    shards, (x_ref, flags_ref) = refs[:count], refs[count : count + 2]
    outs, (halo_ref, other_flags_ref) = refs[count + 2 : 2 * count + 2], refs[2 * count + 2 : 2 * count + 4]
    send, receive, pass_send, pass_receive, own_sem, side_send, side_receive = refs[2 * count + 4 :]
    size, me = lax.axis_size("dp"), lax.axis_index("dp")
    core = lax.axis_index("ctx")
    partner = {"ctx": 1 - core}
    peers = peers_of("dp")
    greet([partner] + [{"dp": p} for p in peers])

    def rows(out, owner):
        depth = out.shape[0] // (2 * size)
        return out.at[pl.ds(pl.multiple_of((owner * 2 + core) * depth, depth), depth)]

    last = x_ref.shape[0] - 16
    waits = [
        remote(x_ref.at[pl.ds(last, 16)], halo_ref, side_send.at[0], side_receive.at[0], partner),
        remote(flags_ref, other_flags_ref, side_send.at[1], side_receive.at[1], partner),
    ]
    for copy in waits:
        copy.start()
    arriving, local = [], []
    for k in range(count):
        for off in range(size - 1, 0, -1):
            copy = remote(
                shards[k],
                rows(outs[k], me),
                send.at[k, off - 1],
                receive.at[k, off - 1],
                {"dp": peers[off - 1]},
            )
            copy.start()
            arriving.append((k, off, copy))
        copy = remote(shards[k], rows(outs[k], me), pass_send.at[k, 0], pass_receive.at[k, 0], partner)
        copy.start()
        waits.append(copy)
        copy = pltpu.make_async_copy(shards[k], rows(outs[k], me), own_sem.at[k])
        copy.start()
        local.append(copy)
    for k, off, copy in arriving:
        copy.wait_recv()
        block = rows(outs[k], lax.rem(me + size - off, size))
        onward = remote(block, block, pass_send.at[k, off], pass_receive.at[k, off], partner)
        onward.start()
        waits.append(onward)
    for copy in local + waits:
        copy.wait()
    for _, _, copy in arriving:
        copy.wait_send()


def gather(shards, x, flags, collective_id):
    size, count = lax.axis_size("dp"), len(shards)
    anywhere = pl.BlockSpec(memory_space=pl.ANY)
    dma = pltpu.SemaphoreType.DMA
    return pl.pallas_call(
        lambda *refs: gather_kernel(count, *refs),
        in_specs=[anywhere] * (count + 2),
        out_specs=[anywhere] * (count + 2),
        out_shape=[jax.ShapeDtypeStruct((s.shape[0] * 2 * size, s.shape[1]), s.dtype) for s in shards]
        + [jax.ShapeDtypeStruct((16, x.shape[1]), x.dtype), jax.ShapeDtypeStruct(flags.shape, flags.dtype)],
        scratch_shapes=[
            dma((count, size - 1)),
            dma((count, size - 1)),
            dma((count, size)),
            dma((count, size)),
            dma((count,)),
            dma((2,)),
            dma((2,)),
        ],
        compiler_params=pltpu.CompilerParams(collective_id=collective_id, has_side_effects=True),
        name="gather",
    )(*shards, x, flags)


def add_rows(out, terms, step_rows, first=0, width=None):
    rows = out.shape[0]
    columns = slice(None) if width is None else pl.ds(first, width)

    def add(step, carry):
        at = pl.ds(pl.multiple_of(step * step_rows, step_rows), step_rows)
        total = terms[0][at, columns].astype(F32)
        for term in terms[1:]:
            total = total + term[at, columns].astype(F32)
        out[at, :] = total.astype(out.dtype)
        return carry

    lax.fori_loop(0, rows // step_rows, add, 0)


def chunk_rows(i):
    return pl.ds(pl.multiple_of(i * BLOCK, BLOCK), BLOCK)


def moves(pairs, sems, outward):
    def move(k, i):
        hbm, vmem = pairs[k]
        source, target = (vmem, hbm) if outward else (hbm, vmem)
        return pltpu.make_async_copy(source.at[chunk_rows(i)], target.at[chunk_rows(i)], sems.at[k, i])

    return move


def each_span(spans, action):
    def body(i, carry_on):
        action(i)
        return carry_on

    lax.fori_loop(0, spans, body, 0)


def branch_kernel(
    heads,
    normed_hbm,
    local_hbm,
    early_hbm,
    cot_hbm,
    passing_ref,
    out_map_ref,
    final_ref,
    gain_ref,
    branch_hbm,
    gate_hbm,
    mixed_hbm,
    back_hbm,
    carried_ref,
    sums_ref,
    normed,
    mixed,
    early,
    cot,
    gate,
    back,
    weighed,
    branch,
    own_sums,
    arriving,
    in_sem,
    early_sem,
    out_sem,
    side_send,
    side_receive,
    send,
    receive,
):
    channels = heads * HEADDIM
    spans = normed.shape[0] // BLOCK
    core = lax.axis_index("ctx")
    partner = {"ctx": 1 - core}
    peers = peers_of("tp")
    load = moves(((normed_hbm, normed), (cot_hbm, cot), (local_hbm, mixed)), in_sem, False)
    store = moves(
        ((branch_hbm, branch), (gate_hbm, gate), (mixed_hbm, mixed), (back_hbm, back)), out_sem, True
    )
    early_load = pltpu.make_async_copy(early_hbm, early, early_sem)
    early_load.start()
    for k in range(3):
        each_span(spans, lambda i, k=k: load(k, i).start())
    greet([partner] + [{"tp": p} for p in peers])
    carry = remote(final_ref, carried_ref, side_send, side_receive, partner)
    carry.start()
    early_load.wait()

    def project(i):
        load(0, i).wait()
        gate[chunk_rows(i), :] = dot_nn(normed[chunk_rows(i), :], early[:, :channels])
        store(1, i).start()
        load(1, i).wait()
        back[chunk_rows(i), :] = dot_nn(cot[chunk_rows(i), :], early[:, channels:])
        store(3, i).start()

    each_span(spans, project)
    carry.wait_recv()
    carried = carried_ref[...] * jnp.where(core > 0, 1.0, 0.0)
    carried_ref[...] = carried
    carried = carried.astype(BF16)
    gain = gain_ref[...]

    def gating(i):
        at = chunk_rows(i)
        load(2, i).wait()
        whole_mixed = mixed[at, :] + widen(passing_ref[at, :], heads, channels) * dot_nt(
            out_map_ref[at, :], carried
        )
        mixed[at, :] = whole_mixed
        store(2, i).start()
        own_gate = gate[at, :]
        gated = whole_mixed * (own_gate * sigmoid(own_gate))
        scaled = gated * gain
        weighed[at, :] = scaled.astype(BF16)
        own_sums[:, at] = jnp.where(
            iota((8, BLOCK), 0) < 4, row_sum(gated * gated), row_sum(scaled * back[at, :])
        )

    each_span(spans, gating)
    copies = []
    for i, p in enumerate(peers):
        copies.append(remote(own_sums, arriving.at[i], send.at[i], receive.at[i], {"tp": p}))
        copies[-1].start()

    def branching(i):
        at = chunk_rows(i)
        branch[at, :] = dot_nt(weighed[at, :], early[:, channels:]).astype(BF16)
        store(0, i).start()

    each_span(spans, branching)
    for copy in copies:
        copy.wait_recv()
    total = own_sums[...]
    for i in range(len(peers)):
        total = total + arriving[i]
    sums_ref[...] = total
    for k in range(4):
        each_span(spans, lambda i, k=k: store(k, i).wait())
    for copy in copies + [carry]:
        copy.wait_send()


def branch_pass(normed, local, early, cot, passing, out_map, final_state, gain, heads, collective_id):
    tokens = normed.shape[0]
    channels = heads * HEADDIM
    spans = tokens // BLOCK
    others = lax.axis_size("tp") - 1
    anywhere = pl.BlockSpec(memory_space=pl.ANY)
    vmem = pl.BlockSpec(memory_space=pltpu.VMEM)
    dma = pltpu.SemaphoreType.DMA
    out = jax.ShapeDtypeStruct
    return pl.pallas_call(
        lambda *refs: branch_kernel(heads, *refs),
        in_specs=[anywhere] * 4 + [vmem] * 4,
        out_specs=[anywhere] * 4 + [vmem] * 2,
        out_shape=[
            out((tokens, MODEL_WIDTH), BF16),
            out((tokens, channels), F32),
            out((tokens, channels), F32),
            out((tokens, channels), F32),
            out((channels, STATE), F32),
            out((8, tokens), F32),
        ],
        scratch_shapes=[
            pltpu.VMEM(normed.shape, BF16),
            pltpu.VMEM(local.shape, F32),
            pltpu.VMEM(early.shape, BF16),
            pltpu.VMEM(cot.shape, BF16),
            pltpu.VMEM(local.shape, F32),
            pltpu.VMEM(local.shape, F32),
            pltpu.VMEM(local.shape, BF16),
            pltpu.VMEM((tokens, MODEL_WIDTH), BF16),
            pltpu.VMEM((8, tokens), F32),
            pltpu.VMEM((others, 8, tokens), F32),
            dma((3, spans)),
            dma,
            dma((4, spans)),
            dma,
            dma,
            dma((others,)),
            dma((others,)),
        ],
        compiler_params=pltpu.CompilerParams(
            collective_id=collective_id, has_side_effects=True, vmem_limit_bytes=VMEM_LIMIT
        ),
        cost_estimate=pl.CostEstimate(
            flops=6 * tokens * MODEL_WIDTH * channels,
            bytes_accessed=14 * 2**20,
            transcendentals=tokens * channels,
        ),
        name="branch_pass",
    )(normed, local, early, cot, passing, out_map, final_state, gain)


def mid_kernel(
    heads,
    gate_hbm,
    mixed_hbm,
    back_hbm,
    sums_ref,
    passing_ref,
    out_map_ref,
    gain_ref,
    gated_hbm,
    grad_mixed_hbm,
    grad_gate_hbm,
    following_ref,
    grad_gain_ref,
    gate,
    mixed,
    back,
    gated_out,
    grad_gate_out,
    through,
    in_sem,
    out_sem,
    side_send,
    side_receive,
):
    channels = heads * HEADDIM
    spans = gate.shape[0] // BLOCK
    core = lax.axis_index("ctx")
    partner = {"ctx": 1 - core}
    load = moves(((gate_hbm, gate), (mixed_hbm, mixed), (back_hbm, back)), in_sem, False)
    store = moves(
        ((grad_mixed_hbm, back), (gated_hbm, gated_out), (grad_gate_hbm, grad_gate_out)), out_sem, True
    )
    for i in range(spans):
        for k in range(3):
            load(k, i).start()
    greet([partner])
    gain = gain_ref[...]
    through[...] = jnp.zeros_like(through)
    grad_gain_ref[...] = jnp.zeros_like(grad_gain_ref)

    def middle(i):
        at = chunk_rows(i)
        for k in range(3):
            load(k, i).wait()
        inv = lax.rsqrt(column_of(sums_ref[0:1, at]) / INNER + EPSILON)
        cross = column_of(sums_ref[4:5, at])
        own_gate, own_mixed, own_back = gate[at, :], mixed[at, :], back[at, :]
        sig = sigmoid(own_gate)
        gate_silu = own_gate * sig
        normal = own_mixed * gate_silu * inv
        gated_out[at, :] = (normal * gain).astype(BF16)
        store(1, i).start()
        grad_gated = inv * (own_back * gain) - normal * (inv * inv * (cross / INNER))
        grad_mixed = grad_gated * gate_silu
        grad_gate = grad_gated * own_mixed * sig * (1.0 + own_gate * (1.0 - sig))
        grad_gate_out[at, :] = grad_gate.astype(BF16)
        store(2, i).start()
        reaching = (grad_mixed * widen(passing_ref[at, :], heads, channels)).astype(BF16)
        through[...] += dot_tn(reaching, out_map_ref[at, :])
        grad_gain_ref[0:1, :] += jnp.sum(own_back * normal, axis=0, keepdims=True)
        back[at, :] = grad_mixed
        store(0, i).start()

    each_span(spans, middle)
    follow = remote(through, following_ref, side_send, side_receive, partner)
    follow.start()
    follow.wait_recv()
    following_ref[...] = following_ref[...] * jnp.where(core > 0, 0.0, 1.0)
    for k in range(3):
        each_span(spans, lambda i, k=k: store(k, i).wait())
    follow.wait_send()


def mid_pass(gate, mixed, back, sums, passing, out_map, gain, heads, collective_id):
    tokens = gate.shape[0]
    channels = heads * HEADDIM
    spans = tokens // BLOCK
    anywhere = pl.BlockSpec(memory_space=pl.ANY)
    vmem = pl.BlockSpec(memory_space=pltpu.VMEM)
    dma = pltpu.SemaphoreType.DMA
    out = jax.ShapeDtypeStruct
    return pl.pallas_call(
        lambda *refs: mid_kernel(heads, *refs),
        in_specs=[anywhere] * 3 + [vmem] * 4,
        out_specs=[anywhere] * 3 + [vmem] * 2,
        out_shape=[
            out((tokens, channels), BF16),
            out((tokens, channels), F32),
            out((tokens, channels), BF16),
            out((channels, STATE), F32),
            out((8, channels), F32),
        ],
        scratch_shapes=[
            pltpu.VMEM(gate.shape, F32),
            pltpu.VMEM(gate.shape, F32),
            pltpu.VMEM(gate.shape, F32),
            pltpu.VMEM(gate.shape, BF16),
            pltpu.VMEM(gate.shape, BF16),
            pltpu.VMEM((channels, STATE), F32),
            dma((3, spans)),
            dma((3, spans)),
            dma,
            dma,
        ],
        compiler_params=pltpu.CompilerParams(
            collective_id=collective_id, has_side_effects=True, vmem_limit_bytes=VMEM_LIMIT
        ),
        cost_estimate=pl.CostEstimate(
            flops=2 * tokens * STATE * channels,
            bytes_accessed=14 * 2**20,
            transcendentals=2 * tokens * channels,
        ),
        name="middle",
    )(gate, mixed, back, sums, passing, out_map, gain)


def final_kernel(count, local_inner, shared, *refs):
    mean_ref, small_ref = refs[:2]
    wide_refs = refs[2 : 2 + count]
    mean_out_ref, gate_ref, out_ref, inner_ref, state_ref, step_ref, small_out_ref = refs[2 + count : 9 + count]
    scratch = refs[9 + count :]
    wide = [(wide_refs[k],) + tuple(scratch[3 * k : 3 * k + 3]) for k in range(count)]
    (
        mean_in,
        small_in,
        small_sum,
        small_far,
        shared_own,
        shared_in,
        state_own,
        state_in,
        z_send,
        z_receive,
        near_send,
        near_receive,
        far_send,
        far_receive,
        own_sem,
        small_send,
        small_receive,
    ) = scratch[3 * count :]
    size, me = lax.axis_size("dp"), lax.axis_index("dp")
    line = lax.axis_size("tp")
    core = lax.axis_index("ctx")
    partner = {"ctx": 1 - core}
    dp_peers, tp_peers = peers_of("dp"), peers_of("tp")
    greet([partner] + [{"dp": p} for p in dp_peers] + [{"tp": p} for p in tp_peers])
    near, local = {}, {}
    order = list(range(1, size)) + [0]
    small_near = remote(small_ref, small_in, small_send.at[0], small_receive.at[0], partner)
    small_near.start()
    steps = [(off, 0) for off in order] + [(off, k) for off in order for k in range(1, count)]
    for off, k in steps:
        owner = lax.rem(me + off, size)
        for grads, own, arriving, _ in wide[k : k + 1]:
            depth = grads.shape[0] // (2 * size)

            def block(c, grads=grads, depth=depth, owner=owner):
                return grads.at[pl.ds(pl.multiple_of((owner * 2 + c) * depth, depth), depth)]

            near[off, k] = remote(
                block(1 - core), arriving.at[off], near_send.at[k, off], near_receive.at[k, off], partner
            )
            near[off, k].start()
            local[off, k] = pltpu.make_async_copy(block(core), own.at[off], own_sem.at[k, off])
            local[off, k].start()
    z_copies = []
    for i in range(line - 1):
        z_copies.append(
            remote(mean_ref, mean_in.at[i], z_send.at[0, i], z_receive.at[0, i], {"tp": tp_peers[i]})
        )
        z_copies[-1].start()
    far, first_far, small_copies = [], [], []
    for number, (off, k) in enumerate(steps):
        _, own, arriving, remote_in = wide[k]
        local[off, k].wait()
        near[off, k].wait_recv()
        add_rows(own.at[off], [own.at[off], arriving.at[off]], 16)
        if off > 0:
            copy = remote(
                own.at[off],
                remote_in.at[off - 1],
                far_send.at[k, off - 1],
                far_receive.at[k, off - 1],
                {"dp": dp_peers[off - 1]},
            )
            copy.start()
            (first_far if k == 0 else far).append(copy)
        if number == size - 1:
            small_near.wait_recv()
            small_sum[...] = small_ref[...] + small_in[...]
            for other in range(1, size):
                copy = remote(
                    small_sum,
                    small_far.at[other - 1],
                    small_send.at[other],
                    small_receive.at[other],
                    {"dp": dp_peers[other - 1]},
                )
                copy.start()
                small_copies.append(copy)
    for copy in z_copies:
        copy.wait_recv()
    add_rows(mean_out_ref, [mean_ref] + [mean_in.at[i] for i in range(line - 1)], 8)
    for copy in small_copies:
        copy.wait_recv()
    total = small_sum[...]
    for off in range(1, size):
        total = total + small_far[off - 1]
    small_out_ref[...] = total
    shared_own[...] = total[:, -shared:]
    terms = [[own.at[0]] + [remote_in.at[i] for i in range(size - 1)] for _, own, _, remote_in in wide]
    for copy in first_far:
        copy.wait_recv()
    add_rows(state_own, terms[0], 16, 0, 2 * STATE)
    last = []
    for i in range(line - 1):
        place = {"tp": tp_peers[i]}
        last.append(remote(state_own, state_in.at[i], z_send.at[1, i], z_receive.at[1, i], place))
        last.append(remote(shared_own, shared_in.at[i], z_send.at[2, i], z_receive.at[2, i], place))
    for copy in last:
        copy.start()
    add_rows(step_ref, terms[0], 16, 2 * STATE, LANES)
    for copy in far:
        copy.wait_recv()
    add_rows(gate_ref, terms[1], 16)
    add_rows(out_ref, terms[2], 16)
    add_rows(inner_ref, terms[3], 16)
    for copy in last:
        copy.wait_recv()
    add_rows(state_ref, [state_own] + [state_in.at[i] for i in range(line - 1)], 16)
    total = shared_own[...]
    for i in range(line - 1):
        total = total + shared_in[i]
    small_out_ref[:, -shared:] = total
    for copy in z_copies + last + first_far + far + small_copies + [small_near] + list(near.values()):
        copy.wait_send()


def final_exchange(mean, small, wide, local_inner, shared, collective_id):
    size, line = lax.axis_size("dp"), lax.axis_size("tp")
    count = len(wide)
    depth = wide[0].shape[0] // (2 * size)
    anywhere = pl.BlockSpec(memory_space=pl.ANY)
    vmem = pl.BlockSpec(memory_space=pltpu.VMEM)
    dma = pltpu.SemaphoreType.DMA

    def out(*shape):
        return jax.ShapeDtypeStruct(shape, F32)

    slots = []
    for like in wide:
        for copies in (size, size, size - 1):
            slots.append(pltpu.VMEM((copies, depth, like.shape[1]), BF16))
    return pl.pallas_call(
        lambda *refs: final_kernel(count, local_inner, shared, *refs),
        in_specs=[vmem, vmem] + [anywhere] * count,
        out_specs=[vmem] * 7,
        out_shape=[
            out(*mean.shape),
            out(depth, local_inner),
            out(depth, local_inner),
            out(depth, local_inner),
            out(depth, 2 * STATE),
            out(depth, LANES),
            out(*small.shape),
        ],
        scratch_shapes=slots
        + [
            pltpu.VMEM((line - 1,) + mean.shape, F32),
            pltpu.VMEM(small.shape, F32),
            pltpu.VMEM(small.shape, F32),
            pltpu.VMEM((size - 1,) + small.shape, F32),
            pltpu.VMEM((8, shared), F32),
            pltpu.VMEM((line - 1, 8, shared), F32),
            pltpu.VMEM((depth, 2 * STATE), BF16),
            pltpu.VMEM((line - 1, depth, 2 * STATE), BF16),
            dma((3, line - 1)),
            dma((3, line - 1)),
            dma((count, size)),
            dma((count, size)),
            dma((count, size - 1)),
            dma((count, size - 1)),
            dma((count, size)),
            dma((size,)),
            dma((size,)),
        ],
        compiler_params=pltpu.CompilerParams(
            collective_id=collective_id, has_side_effects=True, vmem_limit_bytes=VMEM_LIMIT
        ),
        name="final_exchange",
    )(mean, small, *wide)


def on_device(
    block_input_activations,
    sequence_first_token,
    norm_gain,
    gate_proj,
    input_proj,
    step_proj,
    state_proj,
    conv_inner_weight,
    conv_inner_bias,
    conv_state_weight,
    conv_state_bias,
    step_bias,
    decay_log,
    skip_weight,
    gate_gain,
    out_proj,
    output_cotangent,
):
    everyone = ("dp", "ctx")
    x = block_input_activations
    local_inner = gate_proj.shape[1]
    heads = step_bias.shape[0]
    tokens = x.shape[0]
    main = local_inner + 2 * STATE
    params = jnp.pad(jnp.stack([step_bias, decay_log, skip_weight]), ((0, 5), (0, LANES - heads)))
    early_shard, late_shard, flags, marks, taps, bias, step_row, decay_row, skip_row = prepare(
        gate_proj,
        out_proj,
        input_proj,
        state_proj,
        step_proj,
        sequence_first_token,
        conv_inner_weight,
        conv_state_weight,
        conv_inner_bias,
        conv_state_bias,
        params,
        heads,
    )
    early_full = lax.all_gather(early_shard, everyone, axis=0, tiled=True)
    late_full, halo_x, other_flags = gather([late_shard], x, flags, 4)
    gain = norm_gain[None, :]
    gated_gain = gate_gain[None, :]
    (
        normed,
        rows,
        conv,
        mixed_local,
        cum,
        raw,
        passing,
        out_map,
        states,
        products,
        final_state,
        halo_rows,
    ) = front(
        x, marks, halo_x, other_flags, gain, late_full, taps, bias, step_row, decay_row, skip_row, heads
    )
    branch_part, gate, mixed, back, carried, sums = branch_pass(
        normed, mixed_local, early_full, output_cotangent, passing, out_map, final_state, gated_gain, heads, 1
    )
    branch = lax.psum_scatter(branch_part, "tp", scatter_dimension=1, tiled=True)
    gated_normed, grad_mixed, grad_gate, following, grad_gain_gate = mid_pass(
        gate, mixed, back, sums, passing, out_map, gated_gain, heads, 3
    )
    grad_out = dot_tn(output_cotangent, gated_normed).astype(BF16)
    grad_gate_weight = dot_tn(normed, grad_gate).astype(BF16)
    late, tail, halo_grad, conv_sums, head_sums = back_pass(
        grad_mixed,
        conv,
        rows,
        halo_rows,
        raw,
        cum,
        states,
        products,
        carried,
        following,
        taps,
        decay_row,
        skip_row,
        heads,
    )
    returned = passed_along(halo_grad, -1)
    tensor_part, mean_sum, gain_sums, late = input_pass(
        x, grad_gate, late, tail, returned, early_full, late_full, gain
    )
    own_grad = lax.psum_scatter(tensor_part, "tp", scatter_dimension=1, tiled=True)
    state_weight = dot_tn(normed, late[:, local_inner:]).astype(BF16)
    inner_weight = dot_tn(normed, late[:, :local_inner]).astype(BF16)
    shared = 2 * STATE + MODEL_WIDTH
    small = jnp.concatenate(
        [conv_sums[:, :local_inner], grad_gain_gate, head_sums, conv_sums[:, local_inner:], gain_sums], axis=1
    )
    mean_sum, gate_grad, out_grad, inner_grad, state_grad, step_grad, small = final_exchange(
        mean_sum, small, [state_weight, grad_gate_weight, grad_out, inner_weight], local_inner, shared, 2
    )
    place = lax.axis_index("tp")
    share = MODEL_WIDTH // lax.axis_size("tp")
    gain_grad = lax.dynamic_slice_in_dim(small[0], small.shape[1] - MODEL_WIDTH + place * share, share, 0)
    (
        out_grad,
        step_grad,
        gate_grad,
        inner_grad,
        state_grad,
        inner_taps,
        inner_bias,
        state_taps,
        state_bias,
        step_bias_grad,
        decay_grad,
        skip_grad,
        gate_gain_grad,
    ) = spread(out_grad, step_grad, gate_grad, inner_grad, state_grad, small, heads)
    block_output = output_pass(place.reshape(1), x, branch, sums)
    input_grad = grad_pass(
        place.reshape(1), x, output_cotangent, own_grad, mean_sum, gain, lax.axis_size("tp")
    )
    return (
        block_output,
        input_grad,
        gain_grad,
        gate_grad,
        inner_grad,
        step_grad,
        state_grad,
        inner_taps,
        inner_bias[0],
        state_taps,
        state_bias[0],
        step_bias_grad[0],
        decay_grad[0],
        skip_grad[0],
        gate_gain_grad[0],
        out_grad,
    )


def solution(mesh):
    return jax.shard_map(
        on_device,
        mesh=mesh,
        in_specs=(
            P(("dp", "ctx"), None),
            P(("dp", "ctx")),
            P(),
            P(("dp", "ctx"), "tp"),
            P(("dp", "ctx"), "tp"),
            P(("dp", "ctx"), "tp"),
            P(("dp", "ctx"), None),
            P(None, "tp"),
            P("tp"),
            P(),
            P(),
            P("tp"),
            P("tp"),
            P("tp"),
            P("tp"),
            P("tp", ("dp", "ctx")),
            P(("dp", "ctx"), None),
        ),
        out_specs=(
            P(("dp", "ctx"), "tp"),
            P(("dp", "ctx"), "tp"),
            P("tp"),
            P(("dp", "ctx"), "tp"),
            P(("dp", "ctx"), "tp"),
            P(("dp", "ctx"), "tp"),
            P(("dp", "ctx"), None),
            P(None, "tp"),
            P("tp"),
            P(),
            P(),
            P("tp"),
            P("tp"),
            P("tp"),
            P("tp"),
            P("tp", ("dp", "ctx")),
        ),
        check_vma=False,
    )
```
